32 devices in a mesh: dp: 16 (over z, y, core), tensor: 2 (over x).
Axes of the slice: x: 2, y: 2, z: 4, core: 2. Of those that a mesh axis runs over, the one named last changes fastest.
Arguments:
- block_input: bfloat16 [16384, 768], P('dp'), may hold values from -6 to 6
- first_gain: float32 [768], replicated, may hold values from 0.5 to 1.5
- first_shift: float32 [768], replicated, may hold values from -1.2 to 1.2
- qkv_weight: bfloat16 [3, 768, 768], P(None, None, 'tensor'), may hold values from -0.21875 to 0.21875
- qv_bias: float32 [2, 768], P(None, 'tensor'), may hold values from -0.6 to 0.6
- proj_weight: bfloat16 [768, 768], P('tensor'), may hold values from -12 to 12
- proj_bias: float32 [768], replicated, may hold values from -6 to 6
- second_gain: float32 [768], replicated, may hold values from 0.5 to 1.5
- second_shift: float32 [768], replicated, may hold values from -1.2 to 1.2
- fc_weight: bfloat16 [768, 3072], P(None, 'tensor'), may hold values from -0.21875 to 0.21875
- fc_bias: float32 [3072], P('tensor'), may hold values from -3 to 3
- out_weight: bfloat16 [3072, 768], P('tensor'), may hold values from -0.75 to 0.75
- out_bias: float32 [768], replicated, may hold values from -6 to 6
- cotangent: bfloat16 [16384, 768], P('dp'), may hold values from -6 to 6
- lengths: int32 [16], P('dp'), may hold values from 256 to 1024, as said below
Outputs:
- block_output: bfloat16 [16384, 768], P('dp')
- grad_input: float32 [16384, 768], P('dp')
- grad_first_gain: float32 [768], replicated
- grad_first_shift: float32 [768], replicated
- grad_qkv_weight: float32 [3, 768, 768], P(None, 'dp', 'tensor')
- grad_qv_bias: float32 [2, 768], P(None, 'tensor')
- grad_proj_weight: float32 [768, 768], P('tensor', 'dp')
- grad_proj_bias: float32 [768], replicated
- grad_second_gain: float32 [768], replicated
- grad_second_shift: float32 [768], replicated
- grad_fc_weight: float32 [768, 3072], P('dp', 'tensor')
- grad_fc_bias: float32 [3072], P('tensor')
- grad_out_weight: float32 [3072, 768], P('tensor', 'dp')
- grad_out_bias: float32 [768], replicated
The draws below stay inside these ranges and needn't reach their ends.
Inputs may be any that keep to these rules, and one draw needn't show every extreme that they name: Sequence s has its valid tokens in its first lengths[s] slots of 1024, padding after them; some sequence is full.
All inputs are finite; a program needn't handle non-finite values.
Results may differ from the reference program's by a relative error of at most 0.015.
Values may be sent and summed in bfloat16 or wider, within the bound.
No kernel may reach another device: no remote copies, remote signals or barrier semaphores. Data moves between devices by JAX's collectives and lax.ppermute only.
A program may use at most 192 MiB of HBM per device.

```python
import jax
import jax.numpy as jnp
from jax import lax

D = 768
HEADS = 12
HEAD_DIM = 64
FF = 3072
SEQS = 1
LEN = 1024
MIN_LEN = 256
SEQUENCES = 16
TOKENS = 16384
N_DP = 16
N_TENSOR = 2


def draw_lengths(key, part):
    first_key, second_key = jax.random.split(jax.random.fold_in(key, 17))
    drawn = jax.random.randint(first_key, (SEQUENCES,), MIN_LEN, LEN + 1)
    full_spot = jax.random.randint(second_key, (), 0, SEQUENCES)
    return jnp.where(jnp.arange(SEQUENCES) == full_spot, LEN, drawn).astype(jnp.int32)


def strengthened(array, stream_key, source, target, blocks, factor):
    def block_of(position):
        return (jnp.arange(array.shape[position]) // (array.shape[position] // blocks)).reshape((-1,) + (1,) * (array.ndim - 1 - position))

    first = jax.random.permutation(stream_key, blocks)[block_of(target)]
    other_side = (block_of(target) + blocks // 2) % blocks
    return jnp.where((block_of(source) == first) | (block_of(source) == other_side), factor * array, array)


def level_of(key, extent, cuts, smallest, largest):
    def one(position, blocks):
        draws = jax.random.uniform(jax.random.fold_in(jax.random.fold_in(key, 6), position), (blocks,), jnp.float32, smallest / len(cuts), largest / len(cuts))
        return jnp.repeat(jnp.exp(draws), extent[position] // blocks).reshape((-1,) + (1,) * (len(extent) - position - 1))

    gain = one(*cuts[0])
    for cut in cuts[1:]:
        gain = gain * one(*cut)
    return gain


def noise(stream_key, dims, deviation, most, pieces=(), kind=jnp.bfloat16):
    result = deviation * jax.random.normal(stream_key, dims, jnp.float32)
    if pieces:
        result = result * level_of(stream_key, dims, pieces, -0.22, 0.18)
    return jnp.clip(result, -most, most).astype(kind)


def noise_with(stream_key, shape, scale, reach, cuts, heavy, held_as=jnp.bfloat16):
    values = scale * jax.random.normal(stream_key, shape, jnp.float32)
    if cuts:
        values = values * level_of(stream_key, shape, cuts, -0.22, 0.18)
    return jnp.clip(strengthened(values, jax.random.fold_in(stream_key, 3), *heavy), -reach, reach).astype(held_as)


def setup_inputs(seed: int = 0) -> dict:
    key_list = jax.random.split(jax.random.key(seed), 16)
    block_input = noise(key_list[0], (TOKENS, D), 1.0, 6.0, ((0, 16),))
    first_gain = jnp.clip(1.0 + 0.1 * jax.random.normal(key_list[1], (D,), jnp.float32), 0.5, 1.5)
    first_shift = noise(key_list[2], (D,), 0.2, 1.2, (), jnp.float32)
    qkv_weight = noise(key_list[3], (3, D, D), D ** -0.5, 0.21875, ((2, 2),))
    qv_bias = noise(key_list[4], (2, D), 0.1, 0.6, ((1, 2),), jnp.float32)
    proj_weight = noise(key_list[5], (D, D), 2.0, 12.0, ((0, 2),))
    proj_bias = noise(key_list[6], (D,), 1.0, 6.0, (), jnp.float32)
    second_gain = jnp.clip(1.0 + 0.1 * jax.random.normal(key_list[7], (D,), jnp.float32), 0.5, 1.5)
    second_shift = noise(key_list[8], (D,), 0.2, 1.2, (), jnp.float32)
    fc_weight = noise(key_list[9], (D, FF), D ** -0.5, 0.21875, ((1, 2),))
    fc_bias = noise(key_list[10], (FF,), 0.5, 3.0, ((0, 2),), jnp.float32)
    out_weight = noise(key_list[11], (FF, D), (FF // 48) ** -0.5, 0.75, ((0, 2),))
    out_bias = noise(key_list[12], (D,), 1.0, 6.0, (), jnp.float32)
    cotangent = noise_with(key_list[13], (TOKENS, D), 1.0, 6.0, ((0, 16),), (0, 1, 16, 2.0))
    lengths = draw_lengths(jax.random.fold_in(key_list[15], 71), 0)
    return {"block_input": block_input, "first_gain": first_gain, "first_shift": first_shift, "qkv_weight": qkv_weight, "qv_bias": qv_bias, "proj_weight": proj_weight, "proj_bias": proj_bias, "second_gain": second_gain, "second_shift": second_shift, "fc_weight": fc_weight, "fc_bias": fc_bias, "out_weight": out_weight, "out_bias": out_bias, "cotangent": cotangent, "lengths": lengths}


@jax.custom_vjp
def low(v):
    return lax.optimization_barrier(v.astype(jnp.bfloat16)).astype(jnp.float32)

@jax.custom_vjp
def low_back(v):
    return v

def low_keep(v):
    return (low(v), None)

def low_pass(kept, grad):
    return (grad,)

def back_keep(v):
    return (v, None)

def back_low(kept, grad):
    return (low(grad),)
low.defvjp(low_keep, low_pass)
low_back.defvjp(back_keep, back_low)
epsilon = 1e-05
branch_scale = 48 ** (-0.5)
gelu_coef = 0.7978845608028654
cubic_coef = 0.044715
masked_fill = -1000000000.0

def matmul_high(left, right):
    return jnp.dot(left, right, precision=lax.Precision.HIGHEST)

def layer_norm(values, gain_vec, shift_vec):
    row_mean = lax.optimization_barrier(jnp.mean(values, -1, keepdims=True))
    centered = values - row_mean
    variance = lax.optimization_barrier(jnp.mean(centered * centered, -1, keepdims=True))
    return centered * lax.rsqrt(variance + epsilon) * gain_vec + shift_vec

def gelu_tanh(values):
    return 0.5 * values * (1.0 + jnp.tanh(gelu_coef * (values + cubic_coef * values * values * values)))

def forward(resid, first_gain, first_shift, qkv_weight, qv_bias, proj_weight, proj_bias, second_gain, second_shift, fc_weight, fc_bias, out_weight, out_bias, seq_lengths):
    row_count = resid.shape[0]
    normed_low = low(layer_norm(resid, first_gain, first_shift))
    queries = low(low_back(matmul_high(normed_low, qkv_weight[0]) + qv_bias[0]))
    keys_low = low(low_back(matmul_high(normed_low, qkv_weight[1])))
    values_low = low(low_back(matmul_high(normed_low, qkv_weight[2]) + qv_bias[1]))
    head_shape = (SEQS, LEN, HEADS, HEAD_DIM)
    queries = queries.reshape(head_shape)
    keys_low = keys_low.reshape(head_shape)
    values_low = values_low.reshape(head_shape)
    positions = jnp.arange(LEN)
    allowed = (positions[:, None] >= positions[None, :])[None] & (positions[None, None, :] < seq_lengths[:, None, None])
    raw = jnp.einsum('sqhd,skhd->shqk', queries, keys_low, precision=lax.Precision.HIGHEST) * HEAD_DIM ** (-0.5)
    scores = low_back(jnp.where(allowed[:, None], raw, masked_fill))
    attn_prob = jax.nn.softmax(scores, axis=-1)
    context = jnp.einsum('shqk,skhd->sqhd', low(attn_prob), values_low, precision=lax.Precision.HIGHEST).reshape(row_count, D)
    context = low(low_back(context))
    head_width = D // N_TENSOR
    attn_sum = jnp.zeros((row_count, D), jnp.float32)
    for group in range(N_TENSOR):
        lower_edge = group * head_width
        attn_sum = attn_sum + low(matmul_high(context[:, lower_edge:lower_edge + head_width], proj_weight[lower_edge:lower_edge + head_width]))
    attn_sum = low_back(attn_sum)
    middle = resid + branch_scale * (attn_sum + proj_bias)
    second_low = low(layer_norm(middle, second_gain, second_shift))
    hidden = low_back(matmul_high(second_low, fc_weight) + fc_bias)
    activation = low(gelu_tanh(hidden))
    unit_width = FF // N_TENSOR
    mlp_sum = jnp.zeros((row_count, D), jnp.float32)
    for group in range(N_TENSOR):
        lower_edge = group * unit_width
        mlp_sum = mlp_sum + low(matmul_high(activation[:, lower_edge:lower_edge + unit_width], out_weight[lower_edge:lower_edge + unit_width]))
    mlp_sum = low_back(mlp_sum)
    return middle + branch_scale * (mlp_sum + out_bias)

def reference(block_input, first_gain, first_shift, qkv_weight, qv_bias, proj_weight, proj_bias, second_gain, second_shift, fc_weight, fc_bias, out_weight, out_bias, cotangent, lengths):
    weights_all = tuple((argument.astype(jnp.float32) for argument in (first_gain, first_shift, qkv_weight, qv_bias, proj_weight, proj_bias, second_gain, second_shift, fc_weight, fc_bias, out_weight, out_bias)))
    tokens_all = block_input.astype(jnp.float32).reshape(N_DP, SEQS * LEN, D)
    cot_all = cotangent.astype(jnp.float32).reshape(N_DP, SEQS * LEN, D)
    length_all = lengths.reshape(N_DP, SEQS)
    positions = jnp.arange(LEN)

    def scan_step(totals, member):
        tokens, cot_block, seq_lengths = member
        valid_rows = (positions[None, :] < seq_lengths[:, None]).astype(jnp.float32).reshape(SEQS * LEN, 1)

        def apply_block(resid, *weights):
            return forward(resid, *weights, seq_lengths)
        outputs, pullback = jax.vjp(apply_block, tokens, *weights_all)
        gradients = pullback(cot_block * valid_rows)
        totals = tuple((running + fresh for running, fresh in zip(totals, gradients[1:])))
        return (totals, (outputs.astype(jnp.bfloat16), gradients[0]))
    zeros_init = tuple((jnp.zeros_like(argument) for argument in weights_all))
    totals, (outputs_all, input_grads) = lax.scan(scan_step, zeros_init, (tokens_all, cot_all, length_all))
    return (outputs_all.reshape(TOKENS, D), input_grads.reshape(TOKENS, D), totals[0], totals[1], totals[2], totals[3], totals[4], totals[5], totals[6], totals[7], totals[8], totals[9], totals[10], totals[11])
```

```python
import functools

import jax
import jax.numpy as jnp
from jax import lax
from jax.experimental import pallas as pl
from jax.experimental.pallas import tpu as pltpu
from jax.sharding import PartitionSpec as P

HEADS = 12
EPSILON = 1e-05
BRANCH = 48 ** (-0.5)
GELU = 0.7978845608028654
CUBIC = 0.044715
FILL = -1e30
BF = jnp.bfloat16
F32 = jnp.float32
VMEM_LIMIT = 60 * 1024 * 1024
TILE = 256
ROWS = 512
HIDDEN = 512


def dot(left, right):
    return lax.dot_general(left, right, (((1,), (0,)), ((), ())), preferred_element_type=F32)


def dot_nt(left, right):
    return lax.dot_general(left, right, (((1,), (1,)), ((), ())), preferred_element_type=F32)


def norm_parts(values):
    row_mean = jnp.mean(values, -1, keepdims=True)
    centered = values - row_mean
    inverse = lax.rsqrt(jnp.mean(centered * centered, -1, keepdims=True) + EPSILON)
    return centered * inverse, inverse


def norm_back(grad_out, normed, inverse, gain):
    scaled = grad_out * gain
    inner = (
        scaled
        - jnp.mean(scaled, -1, keepdims=True)
        - normed * jnp.mean(scaled * normed, -1, keepdims=True)
    )
    return inverse * inner


def vmem():
    return pl.BlockSpec(memory_space=pltpu.VMEM)


def smem():
    return pl.BlockSpec(memory_space=pltpu.SMEM)


def anywhere():
    return pl.BlockSpec(memory_space=pl.ANY)


def call(body, name, outs, specs, scratch, flops, args):
    moved = sum(a.size * a.dtype.itemsize for a in args)
    moved += sum(o.size * o.dtype.itemsize for o in outs)
    return pl.pallas_call(
        body,
        name=name,
        out_shape=outs,
        in_specs=specs,
        out_specs=tuple(vmem() for _ in outs),
        scratch_shapes=scratch,
        compiler_params=pltpu.CompilerParams(vmem_limit_bytes=VMEM_LIMIT),
        cost_estimate=pl.CostEstimate(flops=flops, bytes_accessed=moved, transcendentals=0),
    )(*args)


def out(shape, dtype):
    return jax.ShapeDtypeStruct(shape, dtype)


def fetch_rows(pieces, target, turn, sems):
    count = len(pieces)
    copies = []
    for index, piece in enumerate(pieces):
        rows = piece.shape[-2]
        place = xor_index(index, turn) if count > 1 else 0
        start = pl.multiple_of(place * rows, 32) if count > 1 else 0
        where = pl.ds(start, rows)
        view = target.at[:, where, :] if len(target.shape) == 3 else target.at[where, :]
        copies.append(pltpu.make_async_copy(piece, view, sems.at[index]))
    return copies


def xor_index(index, turn):
    return jnp.bitwise_xor(jnp.int32(index), turn)


def forward_kernel(own, count, turn_ref, length_ref, source_ref, gain_ref, shift_ref, bias_ref, *rest):
    pieces, rest = rest[:count], rest[count:]
    if own:
        a_ref, at_ref, rest = rest[0], rest[1], rest[2:]
    else:
        a_ref = source_ref
    q_ref, k_ref, v_ref, ctx_ref, ctxt_ref, lse_ref, w_ref, vt_ref, aug_ref, sems = rest
    copies = fetch_rows(pieces, w_ref, turn_ref[0], sems)
    for copy in copies:
        copy.start()
    slots, width = q_ref.shape
    length = length_ref[0]
    if own:
        for start in range(0, slots, ROWS):
            rows = slice(start, start + ROWS)
            normed, _ = norm_parts(source_ref[rows, :].astype(F32))
            low = (normed * gain_ref[...] + shift_ref[...]).astype(BF)
            a_ref[rows, :] = low
            at_ref[:, rows] = low.T
    for copy in copies:
        copy.wait()
    for start in range(0, slots, ROWS):
        rows = slice(start, start + ROWS)
        low = a_ref[rows, :]
        q_ref[rows, :] = ((dot(low, w_ref[0]) + bias_ref[0:1, :]).astype(BF) * 0.125).astype(BF)
        k_ref[rows, :] = dot(low, w_ref[1]).astype(BF)
        values = (dot(low, w_ref[2]) + bias_ref[1:2, :]).astype(BF)
        v_ref[rows, :] = values
        vt_ref[:, rows] = values.T

    @pl.loop(0, width // 128)
    def _(pair):
        lanes = pl.ds(pl.multiple_of(pair * 128, 128), 128)
        lane_k = lax.broadcasted_iota(jnp.int32, (slots, 128), 1)
        pos_k = lax.broadcasted_iota(jnp.int32, (slots, 128), 0)
        bias = jnp.where(pos_k < length, 0.0, FILL)
        k_pair = k_ref[:, lanes].astype(F32)
        for half in (0, 1):
            bias_lane = 64 * (1 - half)
            aug_ref[half] = jnp.where(lane_k == bias_lane, bias, k_pair).astype(BF)
        lane_q = lax.broadcasted_iota(jnp.int32, (TILE, 128), 1)
        key_pos = lax.broadcasted_iota(jnp.int32, (TILE, TILE), 0)
        query_pos = lax.broadcasted_iota(jnp.int32, (TILE, TILE), 1)
        causal = jnp.where(key_pos <= query_pos, 0.0, FILL)
        for block in range(slots // TILE):
            extent = (block + 1) * TILE
            columns = slice(block * TILE, extent)
            q_pair = q_ref[columns, lanes].astype(F32)
            for half in (0, 1):
                bias_lane = 64 * (1 - half)
                q_aug = jnp.where(
                    lane_q // 64 == half, q_pair, jnp.where(lane_q == bias_lane, 1.0, 0.0)
                ).astype(BF)
                scores = dot_nt(aug_ref[half, :extent, :], q_aug)
                diagonal = scores[extent - TILE :] + causal
                row_max = jnp.max(diagonal, 0, keepdims=True)
                if block:
                    row_max = jnp.maximum(
                        row_max, jnp.max(scores[: extent - TILE], 0, keepdims=True)
                    )
                expo = jnp.exp(diagonal - row_max)
                if block:
                    expo = jnp.concatenate(
                        [jnp.exp(scores[: extent - TILE] - row_max), expo], axis=0
                    )
                total = jnp.sum(expo, 0, keepdims=True)
                row = pl.multiple_of(pair * 128 + half * 64, 64)
                mixed = dot(vt_ref[pl.ds(row, 64), :extent], expo.astype(BF))
                ctxt_ref[pl.ds(row, 64), columns] = mixed * (1.0 / total)
                lse_ref[pl.ds(pair * 2 + half, 1), columns] = row_max + jnp.log(total)
        turned = pl.ds(pl.multiple_of(pair * 128, 128), 128)
        ctx_ref[:, lanes] = ctxt_ref[turned, :].T.astype(BF)


def attention_forward(own, turn, length, source, gain, shift, bias, pieces):
    slots, model = source.shape
    width = pieces[0].shape[-1]
    outs = []
    if own:
        outs += [out((slots, model), BF), out((model, slots), BF)]
    outs += [out((slots, width), BF)] * 4
    outs += [out((width, slots), F32), out((width // 64, slots), F32)]
    count = len(pieces)
    flops = 2 * slots * model * width * 3 + 2 * slots * slots * width
    return call(
        functools.partial(forward_kernel, own, count),
        "attention_forward_own" if own else "attention_forward_other",
        tuple(outs),
        [smem(), smem()] + [vmem()] * 4 + [anywhere()] * count,
        [
            pltpu.VMEM((3, model, width), BF),
            pltpu.VMEM((width, slots), BF),
            pltpu.VMEM((2, slots, 128), BF),
            pltpu.SemaphoreType.DMA((count,)),
        ],
        flops,
        (turn, length, source, gain, shift, bias, *pieces),
    )


def prepare_kernel(length_ref, cot_ref, gm_ref, gmt_ref, ob_ref):
    slots = cot_ref.shape[0]
    total = jnp.zeros(ob_ref.shape, F32)
    for start in range(0, slots, ROWS):
        rows = slice(start, start + ROWS)
        cot = cot_ref[rows, :].astype(F32)
        position = lax.broadcasted_iota(jnp.int32, cot.shape, 0) + start
        top = jnp.where(position < length_ref[0], cot, 0.0)
        total += jnp.sum(top, 0, keepdims=True)
        low = (BRANCH * top).astype(BF)
        gm_ref[rows, :] = low
        gmt_ref[:, rows] = low.T
    ob_ref[...] = BRANCH * total


def middle_kernel(
    count, turn_ref, x_ref, ctx0_ref, ctx1_ref, proj0_ref, bias_ref, gain_ref, shift_ref, *rest
):
    pieces, rest = rest[:count], rest[count:]
    middle_ref, c_ref, ct_ref, w_ref, sems = rest
    copies = fetch_rows(pieces, w_ref, turn_ref[0], sems)
    for copy in copies:
        copy.start()
    for copy in copies:
        copy.wait()
    slots = x_ref.shape[0]
    for start in range(0, slots, ROWS):
        rows = slice(start, start + ROWS)
        mine = dot(ctx0_ref[rows, :], proj0_ref[...]).astype(BF).astype(F32)
        theirs = dot(ctx1_ref[rows, :], w_ref[...]).astype(BF).astype(F32)
        middle = x_ref[rows, :].astype(F32) + BRANCH * ((mine + theirs) + bias_ref[...])
        middle_ref[rows, :] = middle
        normed, _ = norm_parts(middle)
        low = (normed * gain_ref[...] + shift_ref[...]).astype(BF)
        c_ref[rows, :] = low
        ct_ref[:, rows] = low.T


def mlp_kernel(own, count, turn_ref, c_ref, g_ref, bias_ref, *rest):
    if own:
        ct_ref, gt_ref, rest = rest[0], rest[1], rest[2:]
    fc_pieces, out_pieces, rest = rest[:count], rest[count : 2 * count], rest[2 * count :]
    mlp_ref, gc_ref, rest = rest[0], rest[1], rest[2:]
    if own:
        dwf_ref, dwo_ref, db_ref, rest = rest[0], rest[1], rest[2], rest[3:]
    fc_ref, ow_ref, mlp_acc, gc_acc, act_ref, gh_ref, sems = rest
    copies = fetch_rows(fc_pieces, fc_ref, turn_ref[0], sems.at[0])
    copies += fetch_rows(out_pieces, ow_ref, turn_ref[0], sems.at[1])
    for copy in copies:
        copy.start()
    for copy in copies:
        copy.wait()
    slots = c_ref.shape[0]
    units = fc_ref.shape[1]
    steps = units // HIDDEN

    @pl.loop(0, steps)
    def _(step):
        lanes = pl.ds(pl.multiple_of(step * HIDDEN, HIDDEN), HIDDEN)
        if own:
            total = jnp.zeros((1, HIDDEN), F32)
        for start in range(0, slots, ROWS):
            rows = slice(start, start + ROWS)
            hidden = dot(c_ref[rows, :], fc_ref[:, lanes]) + bias_ref[:, lanes]
            square = hidden * hidden
            tanh = jnp.tanh(hidden * (GELU + GELU * CUBIC * square))
            share = 0.5 + 0.5 * tanh
            value = hidden * share
            slope = share + value * (1.0 - share) * (2.0 * GELU + 6.0 * GELU * CUBIC * square)
            act = value.astype(BF)
            grad = dot_nt(g_ref[rows, :], ow_ref[lanes, :])
            gh = (grad * slope).astype(BF)
            if own:
                act_ref[rows, :] = act
                gh_ref[rows, :] = gh
                total += jnp.sum(gh.astype(F32), 0, keepdims=True)
            mlp_part = dot(act, ow_ref[lanes, :])
            gc_part = dot_nt(gh, fc_ref[:, lanes])

            @pl.when(step == 0)
            def _():
                mlp_acc[rows, :] = mlp_part
                gc_acc[rows, :] = gc_part

            @pl.when(step > 0)
            def _():
                mlp_acc[rows, :] += mlp_part
                gc_acc[rows, :] += gc_part

        if own:
            db_ref[:, lanes] = total
            dwf_ref[:, lanes] = dot(ct_ref[...], gh_ref[...]).astype(BF)
            dwo_ref[:, lanes] = dot(gt_ref[...], act_ref[...]).astype(BF)

    mlp_ref[...] = mlp_acc[...].astype(BF)
    gc_ref[...] = gc_acc[...].astype(BF)


def feed_forward(own, turn, c_low, grad_mlp, bias, c_turned, g_turned, fc_pieces, out_pieces):
    slots, model = c_low.shape
    units = fc_pieces[0].shape[1]
    count = len(fc_pieces)
    outs = [out((slots, model), BF), out((slots, model), BF)]
    args = [turn, c_low, grad_mlp, bias]
    if own:
        outs += [out((model, units), BF), out((model, units), BF), out((1, units), F32)]
        args += [c_turned, g_turned]
    specs = [smem()] + [vmem()] * (len(args) - 1) + [anywhere()] * (2 * count)
    wide = (slots, HIDDEN) if own else (16, 128)
    return call(
        functools.partial(mlp_kernel, own, count),
        "feed_forward_own" if own else "feed_forward_other",
        tuple(outs),
        specs,
        [
            pltpu.VMEM((model, units), BF),
            pltpu.VMEM((units, model), BF),
            pltpu.VMEM((slots, model), F32),
            pltpu.VMEM((slots, model), F32),
            pltpu.VMEM(wide, BF),
            pltpu.VMEM(wide, BF),
            pltpu.SemaphoreType.DMA((2, count)),
        ],
        2 * slots * model * units * (6 if own else 4),
        (*args, *fc_pieces, *out_pieces),
    )


def turn_kernel(
    count,
    turn_ref,
    length_ref,
    middle_ref,
    cot_ref,
    mlp0_ref,
    mlp1_ref,
    gc0_ref,
    gc1_ref,
    gain_ref,
    ob_ref,
    proj0_ref,
    *rest,
):
    pieces, rest = rest[:count], rest[count:]
    y_ref, gmid_ref, ga_ref, do0_ref, do1_ref, sums_ref, w_ref, sems = rest
    copies = fetch_rows(pieces, w_ref, turn_ref[0], sems)
    for copy in copies:
        copy.start()
    for copy in copies:
        copy.wait()
    slots = middle_ref.shape[0]
    gain_sum = jnp.zeros(gain_ref.shape, F32)
    shift_sum = jnp.zeros(gain_ref.shape, F32)
    bias_sum = jnp.zeros(gain_ref.shape, F32)
    for start in range(0, slots, ROWS):
        rows = slice(start, start + ROWS)
        middle = middle_ref[rows, :]
        mlp = mlp0_ref[rows, :].astype(F32) + mlp1_ref[rows, :].astype(F32)
        y_ref[rows, :] = (middle + BRANCH * (mlp + ob_ref[...])).astype(BF)
        grad_c = gc0_ref[rows, :].astype(F32) + gc1_ref[rows, :].astype(F32)
        normed, inverse = norm_parts(middle)
        gain_sum += jnp.sum(grad_c * normed, 0, keepdims=True)
        shift_sum += jnp.sum(grad_c, 0, keepdims=True)
        cot = cot_ref[rows, :].astype(F32)
        position = lax.broadcasted_iota(jnp.int32, cot.shape, 0) + start
        top = jnp.where(position < length_ref[0], cot, 0.0)
        grad_middle = top + norm_back(grad_c, normed, inverse, gain_ref[...])
        bias_sum += jnp.sum(grad_middle, 0, keepdims=True)
        gmid_ref[rows, :] = grad_middle
        low = (BRANCH * grad_middle).astype(BF)
        ga_ref[rows, :] = low
        do0_ref[rows, :] = dot_nt(low, proj0_ref[...]).astype(BF)
        do1_ref[rows, :] = dot_nt(low, w_ref[...]).astype(BF)
    sums_ref[0:1, :] = gain_sum
    sums_ref[1:2, :] = shift_sum
    sums_ref[2:3, :] = BRANCH * bias_sum


def backward_kernel(own, count, turn_ref, length_ref, q_ref, k_ref, v_ref, do_ref, ctxt_ref, lse_ref, *rest):
    if own:
        at_ref, gat_ref, x_ref, rest = rest[0], rest[1], rest[2], rest[3:]
    pieces, rest = rest[:count], rest[count:]
    gin_ref, rest = rest[0], rest[1:]
    if own:
        dw_ref, dp_ref, qvb_ref, sums_ref, rest = rest[0], rest[1], rest[2], rest[3], rest[4:]
    w_ref, dq_ref, dk_ref, dv_ref, dk_acc, dv_acc, aug_ref, kt_ref, delta_ref, sems = rest
    copies = fetch_rows(pieces, w_ref, turn_ref[0], sems)
    for copy in copies:
        copy.start()
    slots, width = q_ref.shape
    length = length_ref[0]

    @pl.loop(0, width // 128)
    def _(pair):
        lanes = pl.ds(pl.multiple_of(pair * 128, 128), 128)
        lane_k = lax.broadcasted_iota(jnp.int32, (slots, 128), 1)
        pos_k = lax.broadcasted_iota(jnp.int32, (slots, 128), 0)
        bias = jnp.where(pos_k < length, 0.0, FILL)
        k_pair = k_ref[:, lanes].astype(F32)
        for half in (0, 1):
            bias_lane = 64 * (1 - half)
            aug_ref[half] = jnp.where(lane_k == bias_lane, bias, k_pair).astype(BF)
        kt_ref[...] = k_ref[:, lanes].T
        product = do_ref[:, lanes].astype(F32).T * ctxt_ref[lanes, :]
        for half in (0, 1):
            delta_ref[half : half + 1, :] = jnp.sum(
                product[64 * half : 64 * half + 64], 0, keepdims=True
            )
        lane_q = lax.broadcasted_iota(jnp.int32, (TILE, 128), 1)
        key_pos = lax.broadcasted_iota(jnp.int32, (TILE, TILE), 0)
        query_pos = lax.broadcasted_iota(jnp.int32, (TILE, TILE), 1)
        causal = jnp.where(key_pos <= query_pos, 0.0, FILL)
        for block in range(slots // TILE):
            columns = slice(block * TILE, (block + 1) * TILE)
            q_pair = q_ref[columns, lanes].astype(F32)
            do_pair = do_ref[columns, lanes].astype(F32)
            q_low, q_aug, do_low, lse, delta = [], [], [], [], []
            for half in (0, 1):
                bias_lane = 64 * (1 - half)
                inside = lane_q // 64 == half
                q_low.append(jnp.where(inside, q_pair, 0.0).astype(BF))
                do_low.append(jnp.where(inside, do_pair, 0.0).astype(BF))
                q_aug.append(
                    jnp.where(inside, q_pair, jnp.where(lane_q == bias_lane, 1.0, 0.0)).astype(BF)
                )
                lse.append(lse_ref[pl.ds(pair * 2 + half, 1), columns])
                delta.append(delta_ref[half : half + 1, columns])
            q_both = jnp.concatenate(q_low, axis=0)
            do_both = jnp.concatenate(do_low, axis=0)
            dqt = [None, None]
            for inner in range(block + 1):
                keys = slice(inner * TILE, (inner + 1) * TILE)
                probs, slopes = [], []
                for half in (0, 1):
                    scores = dot_nt(aug_ref[half, keys, :], q_aug[half])
                    if inner == block:
                        scores = scores + causal
                    prob = jnp.exp(scores - lse[half])
                    grad = dot_nt(v_ref[keys, lanes], do_low[half])
                    slope = (prob * (grad - delta[half])).astype(BF)
                    probs.append(prob.astype(BF))
                    slopes.append(slope)
                    part = dot(kt_ref[64 * half : 64 * half + 64, keys], slope)
                    dqt[half] = part if inner == 0 else dqt[half] + part
                dv_part = dot(jnp.concatenate(probs, axis=1), do_both)
                dk_part = dot(jnp.concatenate(slopes, axis=1), q_both)
                if inner == block:
                    dv_acc[keys, :] = dv_part
                    dk_acc[keys, :] = dk_part
                else:
                    dv_acc[keys, :] += dv_part
                    dk_acc[keys, :] += dk_part
            dq_ref[columns, lanes] = (jnp.concatenate(dqt, axis=0).T * 0.125).astype(BF)
        dk_ref[:, lanes] = dk_acc[...].astype(BF)
        dv_ref[:, lanes] = dv_acc[...].astype(BF)

    for copy in copies:
        copy.wait()
    if own:
        for index, grad_ref in enumerate((dq_ref, dk_ref, dv_ref)):
            dw_ref[index] = dot(at_ref[...], grad_ref[...]).astype(BF)
        qvb_ref[0:1, :] = jnp.sum(dq_ref[...].astype(F32), 0, keepdims=True)
        qvb_ref[1:2, :] = jnp.sum(dv_ref[...].astype(F32), 0, keepdims=True)
        dp_ref[...] = dot(ctxt_ref[...].astype(BF), gat_ref[...]).T.astype(BF)
        gain_sum = jnp.zeros((1, gin_ref.shape[1]), F32)
        shift_sum = jnp.zeros((1, gin_ref.shape[1]), F32)
    for start in range(0, slots, ROWS):
        rows = slice(start, start + ROWS)
        part = dot_nt(dq_ref[rows, :], w_ref[0])
        part += dot_nt(dk_ref[rows, :], w_ref[1])
        part += dot_nt(dv_ref[rows, :], w_ref[2])
        gin_ref[rows, :] = part.astype(BF)
        if own:
            normed, _ = norm_parts(x_ref[rows, :].astype(F32))
            gain_sum += jnp.sum(part * normed, 0, keepdims=True)
            shift_sum += jnp.sum(part, 0, keepdims=True)
    if own:
        sums_ref[0:1, :] = gain_sum
        sums_ref[1:2, :] = shift_sum


def attention_backward(own, turn, length, q, k, v, do, ctxt, lse, extra, pieces):
    slots, width = q.shape
    model = pieces[0].shape[-2] * len(pieces)
    count = len(pieces)
    outs = [out((slots, model), BF)]
    if own:
        outs += [
            out((3, model, width), BF),
            out((model, width), BF),
            out((2, width), F32),
            out((2, model), F32),
        ]
    args = [turn, length, q, k, v, do, ctxt, lse, *extra]
    specs = [smem(), smem()] + [vmem()] * (len(args) - 2) + [anywhere()] * count
    flops = 5 * slots * slots * width + 2 * slots * model * width * (7 if own else 3)
    return call(
        functools.partial(backward_kernel, own, count),
        "attention_backward_own" if own else "attention_backward_other",
        tuple(outs),
        specs,
        [
            pltpu.VMEM((3, model, width), BF),
            pltpu.VMEM((slots, width), BF),
            pltpu.VMEM((slots, width), BF),
            pltpu.VMEM((slots, width), BF),
            pltpu.VMEM((slots, 128), F32),
            pltpu.VMEM((slots, 128), F32),
            pltpu.VMEM((2, slots, 128), BF),
            pltpu.VMEM((128, slots), BF),
            pltpu.VMEM((2, slots), F32),
            pltpu.SemaphoreType.DMA((count,)),
        ],
        flops,
        (*args, *pieces),
    )


def final_kernel(x_ref, gmid_ref, ga0_ref, ga1_ref, gain_ref, gin_ref):
    slots = x_ref.shape[0]
    for start in range(0, slots, ROWS):
        rows = slice(start, start + ROWS)
        normed, inverse = norm_parts(x_ref[rows, :].astype(F32))
        grad_a = ga0_ref[rows, :].astype(F32) + ga1_ref[rows, :].astype(F32)
        gin_ref[rows, :] = gmid_ref[rows, :] + norm_back(grad_a, normed, inverse, gain_ref[...])


def across(value):
    return lax.ppermute(value, "tensor", [(0, 1), (1, 0)])


def swap(value, bit):
    count = lax.axis_size("dp")
    return lax.ppermute(value, "dp", [(i, i ^ bit) for i in range(count)])


def pick(value, index, axis):
    return lax.dynamic_index_in_dim(value, index, axis, keepdims=False)


def split_rows(value, count):
    shape = value.shape
    return value.reshape(*shape[:-2], count, shape[-2] // count, shape[-1])


def halve(total, place, bit):
    pairs = total.reshape(total.shape[0] // 2, 2, *total.shape[1:])
    side = (place // bit) % 2
    return pick(pairs, side, 1), pick(pairs, 1 - side, 1).astype(BF)


def three_parts(value):
    high = lax.reduce_precision(value, 8, 7)
    rest = value - high
    mid = lax.reduce_precision(rest, 8, 7)
    return jnp.concatenate([high, mid, rest - mid], 0).astype(BF)


def two_parts(value):
    high = lax.reduce_precision(value, 8, 7)
    return jnp.concatenate([high, value - high], 0).astype(BF)


def local(
    block_input,
    first_gain,
    first_shift,
    qkv_weight,
    qv_bias,
    proj_weight,
    proj_bias,
    second_gain,
    second_shift,
    fc_weight,
    fc_bias,
    out_weight,
    out_bias,
    cotangent,
    lengths,
):
    slots, model = block_input.shape
    width = qkv_weight.shape[2]
    units = fc_weight.shape[1]
    shards = lax.axis_size("dp")
    place = lax.axis_index("dp")
    quarter = jnp.bitwise_and(place, 3)
    one_bit = jnp.bitwise_and(place, 1)
    turn4 = quarter.reshape(1).astype(jnp.int32)
    turn2 = one_bit.reshape(1).astype(jnp.int32)
    turn0 = jnp.zeros((1,), jnp.int32)
    length = lengths.astype(jnp.int32)
    row = lambda vector: vector.reshape(1, -1)

    biases = jnp.concatenate([qv_bias.reshape(-1), fc_bias]).reshape(-1, model)
    bias_rows = three_parts(biases)
    proj_send = jnp.concatenate([pick(split_rows(proj_weight, 2), one_bit, 0), bias_rows], 0)
    qkv_mine = across(pick(split_rows(qkv_weight, 4), quarter, 1))
    proj_got = across(proj_send)
    fc_mine = across(pick(split_rows(fc_weight, 4), quarter, 0))
    out_mine = across(pick(split_rows(out_weight, 4), quarter, 0))

    def spread(mine):
        side = swap(mine, 2)
        return [mine, swap(mine, 1), side, swap(side, 1)]

    qkv_other = spread(qkv_mine)
    half_rows = width // 2
    proj_mine = proj_got[:half_rows]
    proj_other = [proj_mine, swap(proj_mine, 1)]
    parts = proj_got[half_rows:].astype(F32).reshape(3, -1)
    other_biases = (parts[0] + parts[1]) + parts[2]
    qv_bias_other = other_biases[: 2 * width].reshape(2, width)
    fc_bias_other = other_biases[2 * width :]
    fc_other = spread(fc_mine)
    out_other = spread(out_mine)

    a_low, a_turned, q0, k0, v0, ctx0, ctxt0, lse0 = attention_forward(
        True, turn0, length, block_input, row(first_gain), row(first_shift), qv_bias, [qkv_weight]
    )
    grad_mlp, grad_mlp_turned, grad_out_bias = call(
        prepare_kernel,
        "prepare",
        (out((slots, model), BF), out((model, slots), BF), out((1, model), F32)),
        [smem(), vmem()],
        [],
        8 * slots * model,
        (length, cotangent),
    )
    q1, k1, v1, ctx1, ctxt1, lse1 = attention_forward(
        False, turn4, length, a_low, row(first_gain), row(first_shift), qv_bias_other, qkv_other
    )
    middle, c_low, c_turned = call(
        functools.partial(middle_kernel, 2),
        "middle",
        (out((slots, model), F32), out((slots, model), BF), out((model, slots), BF)),
        [smem()] + [vmem()] * 7 + [anywhere()] * 2,
        [pltpu.VMEM((width, model), BF), pltpu.SemaphoreType.DMA((2,))],
        4 * slots * model * width,
        (
            turn2,
            block_input,
            ctx0,
            ctx1,
            proj_weight,
            row(proj_bias),
            row(second_gain),
            row(second_shift),
            *proj_other,
        ),
    )
    mlp0, gc0, dwf, dwo, grad_fc_bias = feed_forward(
        True, turn0, c_low, grad_mlp, row(fc_bias), c_turned, grad_mlp_turned, [fc_weight], [out_weight]
    )
    mlp1, gc1 = feed_forward(
        False, turn4, c_low, grad_mlp, row(fc_bias_other), None, None, fc_other, out_other
    )

    blocks = jnp.concatenate(
        [dwf.reshape(shards, model // shards, units), dwo.reshape(shards, model // shards, units)], 2
    )
    total = blocks
    bit = 1
    while bit < shards:
        kept, sent = halve(total, place, bit)
        total = kept.astype(F32) + swap(sent, bit).astype(F32)
        bit *= 2
    grad_fc_weight = total[0, :, :units]
    grad_out_weight = total[0, :, units:].T

    block_output, grad_middle, grad_attn, do0, do1, sums2 = call(
        functools.partial(turn_kernel, 2),
        "turn",
        (
            out((slots, model), BF),
            out((slots, model), F32),
            out((slots, model), BF),
            out((slots, width), BF),
            out((slots, width), BF),
            out((3, model), F32),
        ),
        [smem(), smem()] + [vmem()] * 9 + [anywhere()] * 2,
        [pltpu.VMEM((width, model), BF), pltpu.SemaphoreType.DMA((2,))],
        4 * slots * model * width,
        (
            turn2,
            length,
            middle,
            cotangent,
            mlp0,
            mlp1,
            gc0,
            gc1,
            row(second_gain),
            row(out_bias),
            proj_weight,
            *proj_other,
        ),
    )
    ga0, dw, dp, grad_qv, sums1 = attention_backward(
        True,
        turn0,
        length,
        q0,
        k0,
        v0,
        do0,
        ctxt0,
        lse0,
        (a_turned, grad_attn, block_input),
        [qkv_weight],
    )
    (ga1,) = attention_backward(
        False, turn4, length, q1, k1, v1, do1, ctxt1, lse1, (), qkv_other
    )
    (grad_input,) = call(
        final_kernel,
        "final",
        (out((slots, model), F32),),
        [vmem()] * 5,
        [],
        20 * slots * model,
        (block_input, grad_middle, ga0, ga1, row(first_gain)),
    )

    share = model // shards
    blocks = jnp.concatenate(
        [dw[i].reshape(shards, share, width) for i in range(3)] + [dp.reshape(shards, share, width)], 2
    )
    line = 4 * width
    sums1 = sums1 + across(sums1)
    vectors = jnp.concatenate(
        [
            sums1.reshape(-1),
            grad_out_bias.reshape(-1),
            sums2.reshape(-1),
            grad_fc_bias.reshape(-1),
            grad_qv.reshape(-1),
        ]
    )
    used = vectors.shape[0]
    lines = -(-used // line)
    vectors = jnp.pad(vectors, (0, lines * line - used)).reshape(lines, line)
    total = blocks
    bit = 1
    while bit < shards:
        kept, sent = halve(total, place, bit)
        count = sent.shape[0] * share
        sent = jnp.concatenate([sent.reshape(count, line), two_parts(vectors)], 0)
        got = swap(sent, bit).astype(F32)
        total = kept.astype(F32) + got[:count].reshape(kept.shape)
        high = lax.reduce_precision(vectors, 8, 7)
        mine = high + lax.reduce_precision(vectors - high, 8, 7)
        vectors = mine + (got[count : count + lines] + got[count + lines :])
        bit *= 2
    total = total[0]
    grad_qkv_weight = jnp.stack([total[:, i * width : (i + 1) * width] for i in range(3)])
    grad_proj_weight = total[:, 3 * width :].T
    vectors = vectors.reshape(-1)
    sizes = [model] * 6 + [units, 2 * width]
    pieces = []
    start = 0
    for size in sizes:
        pieces.append(vectors[start : start + size])
        start += size
    (
        grad_first_gain,
        grad_first_shift,
        grad_out_bias,
        grad_second_gain,
        grad_second_shift,
        grad_proj_bias,
        grad_fc_bias,
        grad_qv,
    ) = pieces
    return (
        block_output,
        grad_input,
        grad_first_gain,
        grad_first_shift,
        grad_qkv_weight,
        grad_qv.reshape(2, width),
        grad_proj_weight,
        grad_proj_bias,
        grad_second_gain,
        grad_second_shift,
        grad_fc_weight,
        grad_fc_bias,
        grad_out_weight,
        grad_out_bias,
    )


def solution(mesh):
    placed = (
        P("dp", None),
        P(),
        P(),
        P(None, None, "tensor"),
        P(None, "tensor"),
        P("tensor", None),
        P(),
        P(),
        P(),
        P(None, "tensor"),
        P("tensor"),
        P("tensor", None),
        P(),
        P("dp", None),
        P("dp"),
    )
    return jax.shard_map(
        local,
        mesh=mesh,
        in_specs=placed,
        out_specs=(
            P("dp", None),
            P("dp", None),
            P(),
            P(),
            P(None, "dp", "tensor"),
            P(None, "tensor"),
            P("tensor", "dp"),
            P(),
            P(),
            P(),
            P("dp", "tensor"),
            P("tensor"),
            P("tensor", "dp"),
            P(),
        ),
        check_vma=False,
    )
```

```python
import functools

import jax
import jax.numpy as jnp
from jax import lax
from jax.experimental import pallas as pl
from jax.experimental.pallas import tpu as pltpu
from jax.sharding import PartitionSpec as P

EPSILON = 1e-05
BRANCH = 48 ** (-0.5)
GELU = 0.7978845608028654
CUBIC = 0.044715
FILL = -1e30
BF = jnp.bfloat16
F32 = jnp.float32
VMEM_LIMIT = 60 * 1024 * 1024
TILE = 256
HIDDEN = 512
GAIN1, SHIFT1, BIAS_P, GAIN2, SHIFT2, BIAS_O = range(6)
BIAS_QV, BIAS_FC = 8, 9


def dot(left, right):
    return lax.dot_general(left, right, (((1,), (0,)), ((), ())), preferred_element_type=F32)


def dot_nt(left, right):
    return lax.dot_general(left, right, (((1,), (1,)), ((), ())), preferred_element_type=F32)


def norm_parts(values):
    row_mean = jnp.mean(values, -1, keepdims=True)
    centered = values - row_mean
    inverse = lax.rsqrt(jnp.mean(centered * centered, -1, keepdims=True) + EPSILON)
    return centered * inverse, inverse


def norm_back(grad_out, normed, inverse, gain):
    scaled = grad_out * gain
    inner = (
        scaled
        - jnp.mean(scaled, -1, keepdims=True)
        - normed * jnp.mean(scaled * normed, -1, keepdims=True)
    )
    return inverse * inner


def whole(shape):
    return pl.BlockSpec(shape, lambda *_: (0,) * len(shape))


def row_tile(columns):
    return pl.BlockSpec((TILE, columns), lambda i: (i, 0))


def column_tile(rows, size=TILE):
    return pl.BlockSpec((rows, size), lambda i: (0, i))


SMEM = pl.BlockSpec(memory_space=pltpu.SMEM)
HBM = pl.BlockSpec(memory_space=pl.ANY)


def shape_of(shape, dtype):
    return jax.ShapeDtypeStruct(shape, dtype)


def call(body, name, steps, ins, outs, scratch, flops):
    args = [array for array, _ in ins]
    shapes = tuple(shape_of(shape, dtype) for shape, dtype, _ in outs)
    moved = sum(a.size * a.dtype.itemsize for a in args)
    moved += sum(s.size * s.dtype.itemsize for s in shapes)
    return pl.pallas_call(
        body,
        name=name,
        grid=(steps,),
        out_shape=shapes,
        in_specs=[spec for _, spec in ins],
        out_specs=tuple(spec for _, _, spec in outs),
        scratch_shapes=scratch,
        compiler_params=pltpu.CompilerParams(vmem_limit_bytes=VMEM_LIMIT),
        cost_estimate=pl.CostEstimate(flops=flops, bytes_accessed=moved, transcendentals=0),
    )(*args)


def fetch_rows(pieces, turn, target, sems):
    copies = []
    for index, piece in enumerate(pieces):
        rows = piece.shape[-2]
        if len(pieces) > 1:
            place = jnp.bitwise_xor(jnp.int32(index), turn)
            where = pl.ds(pl.multiple_of(place * rows, 32), rows)
        else:
            where = slice(None)
        if len(piece.shape) == 2:
            copies.append(pltpu.make_async_copy(piece, target.at[where, :], sems.at[index]))
            continue
        width = piece.shape[2]
        for matrix in range(3):
            columns = slice(matrix * width, (matrix + 1) * width)
            copies.append(
                pltpu.make_async_copy(
                    piece.at[matrix], target.at[where, columns], sems.at[3 * index + matrix]
                )
            )
    return copies


def start_all(copies):
    for copy in copies:
        copy.start()


def wait_all(copies):
    for copy in copies:
        copy.wait()


def qkv_bias(biases, width):
    bias = jnp.concatenate(
        [biases[:, :width], jnp.zeros((1, width), F32), biases[:, width:]], axis=1
    )
    lane = lax.broadcasted_iota(jnp.int32, (1, 3 * width), 1)
    return bias, jnp.where(lane < width, 0.125, 1.0)


def tiles(source, target, sems, axis=0):
    copies = []
    for index in range(source.shape[axis] // TILE):
        part = slice(index * TILE, (index + 1) * TILE)
        view = (part, slice(None)) if axis == 0 else (slice(None), part)
        copies.append(pltpu.make_async_copy(source.at[view], target.at[view], sems.at[index]))
    return copies


def project_kernel(
    bits_ref,
    x_hbm,
    gain1_ref,
    shift1_ref,
    bias_p_ref,
    gain2_ref,
    shift2_ref,
    bias_o_ref,
    qv_ref,
    fcb_ref,
    qkv_hbm,
    proj_hbm,
    fc_hbm,
    out_hbm,
    vec_ref,
    a_out,
    at_out,
    qkv_out,
    proj_out,
    fc_out,
    out_out,
    x_ref,
    w_ref,
    a_ref,
    at_ref,
    qkv_ref,
    proj_ref,
    fc_ref,
    out_ref,
    x_sems,
    w_sems,
    send_sems,
    a_sems,
    at_sems,
    qkv_sems,
):
    x_in = tiles(x_hbm, x_ref, x_sems)
    x_in[0].start()
    w_in = fetch_rows([qkv_hbm], 0, w_ref, w_sems)
    start_all(w_in)
    start_all(x_in[1:])
    half, quarter, fourth = proj_hbm.shape[0] // 2, fc_hbm.shape[0] // 4, out_hbm.shape[0] // 4
    sends_in = []
    for index, (source, target, place, rows) in enumerate(
        (
            (proj_hbm, proj_ref.at[:half, :], bits_ref[0], half),
            (fc_hbm, fc_ref, bits_ref[1], quarter),
            (out_hbm, out_ref, bits_ref[1], fourth),
        )
    ):
        where = pl.ds(pl.multiple_of(place * rows, 32), rows)
        sends_in.append(pltpu.make_async_copy(source.at[where, :], target, send_sems.at[index]))
    start_all(sends_in)
    sends_out = [
        pltpu.make_async_copy(source, target, send_sems.at[3 + index])
        for index, (source, target) in enumerate(
            ((proj_ref, proj_out), (fc_ref, fc_out), (out_ref, out_out))
        )
    ]
    model = x_ref.shape[1]
    vec_ref[...] = jnp.zeros(vec_ref.shape, F32)
    for index, ref in enumerate(
        (gain1_ref, shift1_ref, bias_p_ref, gain2_ref, shift2_ref, bias_o_ref)
    ):
        vec_ref[index : index + 1, :] = ref[...].reshape(1, model)
    width = qv_ref.shape[1]
    vec_ref[BIAS_QV : BIAS_QV + 1, :width] = qv_ref[0:1, :]
    vec_ref[BIAS_QV : BIAS_QV + 1, width:] = qv_ref[1:2, :]
    fcb = fcb_ref[...].reshape(1, fcb_ref.shape[0])
    for index in range(2):
        vec_ref[BIAS_FC + index : BIAS_FC + index + 1, :] = fcb[:, index * model : (index + 1) * model]
    value = vec_ref[8 * (BIAS_QV // 8) :, :]
    high = value.astype(BF)
    rest = value - high.astype(F32)
    mid = rest.astype(BF)
    low = (rest - mid.astype(F32)).astype(BF)
    lines = value.shape[0]
    for index, part in enumerate((high, mid, low)):
        proj_ref[half + index * lines : half + (index + 1) * lines, :] = part

    def normalize(index):
        x_in[index].wait()
        rows = slice(index * TILE, (index + 1) * TILE)
        normed, _ = norm_parts(x_ref[rows, :].astype(F32))
        low = normed * vec_ref[GAIN1 : GAIN1 + 1, :] + vec_ref[SHIFT1 : SHIFT1 + 1, :]
        low = low.astype(BF)
        a_ref[rows, :] = low
        at_ref[:, rows] = low.T

    count = len(x_in)
    bias, scale = qkv_bias(vec_ref[BIAS_QV : BIAS_QV + 1, :], width)
    a_tiles = tiles(a_ref, a_out, a_sems)
    at_tiles = tiles(at_ref, at_out, at_sems, 1)
    qkv_tiles = tiles(qkv_ref, qkv_out, qkv_sems)
    normalize(0)
    wait_all(w_in)
    for index in range(count):
        rows = slice(index * TILE, (index + 1) * TILE)
        a_tiles[index].start()
        at_tiles[index].start()
        if index + 1 < count:
            normalize(index + 1)
        qkv_ref[rows, :] = ((dot(a_ref[rows, :], w_ref[...]) + bias) * scale).astype(BF)
        qkv_tiles[index].start()
        if index < len(sends_in):
            sends_in[index].wait()
            sends_out[index].start()
    wait_all(sends_out + a_tiles + at_tiles + qkv_tiles)


def project(bits, x, vectors, qkv, proj, fc, ow):
    slots, model = x.shape
    width = qkv.shape[2]
    units = fc.shape[1]
    tokens = slots // TILE
    sends = [
        (width // 2 + 32, model),
        (model // 4, units),
        (units // 4, model),
    ]
    shapes = [(slots, model), (model, slots), (slots, 3 * width)]
    dma = pltpu.SemaphoreType.DMA
    return call(
        project_kernel,
        "project_own",
        1,
        [(bits, SMEM), (x, HBM)]
        + [(vector, whole(vector.shape)) for vector in vectors]
        + [(weight, HBM) for weight in (qkv, proj, fc, ow)],
        [((16, model), F32, whole((16, model)))]
        + [(shape, BF, HBM) for shape in shapes + sends],
        [pltpu.VMEM((slots, model), BF), pltpu.VMEM((model, 3 * width), BF)]
        + [pltpu.VMEM(shape, BF) for shape in shapes + sends]
        + [dma((tokens,)), dma((3,)), dma((6,)), dma((tokens,)), dma((tokens,)), dma((tokens,))],
        6 * slots * model * width,
    )


def causal_fill():
    keys = lax.broadcasted_iota(jnp.int32, (TILE, TILE), 0)
    queries = lax.broadcasted_iota(jnp.int32, (TILE, TILE), 1)
    return jnp.where(keys <= queries, 0.0, FILL)


def masked_pair(pair_keys, pair_queries, length, keys_ref, queries_ref):
    slots = pair_keys.shape[0]
    lane = lax.broadcasted_iota(jnp.int32, (slots, 128), 1)
    position = lax.broadcasted_iota(jnp.int32, (slots, 128), 0)
    fill = jnp.where(position < length, 0.0, FILL)
    pair_keys = pair_keys.astype(F32)
    pair_queries = pair_queries.astype(F32)
    for half in (0, 1):
        spare = 64 * (1 - half)
        keys_ref[half] = jnp.where(lane == spare, fill, pair_keys).astype(BF)
        queries_ref[half] = jnp.where(
            lane // 64 == half, pair_queries, jnp.where(lane == spare, 1.0, 0.0)
        ).astype(BF)


def pair_lanes(pair, offset=0):
    return pl.ds(pl.multiple_of(offset + pair * 128, 128), 128)


def forward_pairs(
    length, qkv_ref, ctx_ref, ctxt_ref, lse_ref, scratch, source_in, ctx_out, ctxt_out, sems
):
    ka_ref, qa_ref, vt_ref, score_ref, expo_ref = scratch
    slots, width = ctx_ref.shape
    causal = causal_fill()

    def results(pair):
        lanes = pair_lanes(pair)
        return (
            pltpu.make_async_copy(ctx_ref.at[:, lanes], ctx_out.at[:, lanes], sems.at[0, pair]),
            pltpu.make_async_copy(ctxt_ref.at[lanes, :], ctxt_out.at[lanes, :], sems.at[1, pair]),
        )

    @pl.loop(0, width // 128)
    def _(pair):
        lanes = pair_lanes(pair)
        if source_in is not None:
            wait_all(source_in(pair))
        masked_pair(
            qkv_ref[:, pair_lanes(pair, width)], qkv_ref[:, lanes], length, ka_ref, qa_ref
        )
        vt_ref[...] = qkv_ref[:, pair_lanes(pair, 2 * width)].T
        items = [(block, half) for block in range(slots // TILE) for half in (0, 1)]
        state = {}

        def score(item):
            block, half = items[item]
            extent = (block + 1) * TILE
            columns = slice(block * TILE, extent)
            scores = dot_nt(ka_ref[half, :extent, :], qa_ref[half, columns, :])
            high = None
            for inner in range(block + 1):
                keys = slice(inner * TILE, (inner + 1) * TILE)
                part = scores[keys]
                if inner == block:
                    part = part + causal
                score_ref[item % 2, keys, :] = part
                most = jnp.max(part.reshape(TILE // 8, 8, TILE), 0)
                high = most if high is None else jnp.maximum(high, most)
            state[item] = jnp.max(high, 0, keepdims=True)

        def exponential(item):
            block, half = items[item]
            high = state[item]
            total = None
            for inner in range(block + 1):
                keys = slice(inner * TILE, (inner + 1) * TILE)
                expo = jnp.exp(score_ref[item % 2, keys, :] - high)
                part = jnp.sum(expo.reshape(TILE // 8, 8, TILE), 0)
                total = part if total is None else total + part
                expo_ref[item % 2, keys, :] = expo.astype(BF)
            state[item] = (high, jnp.sum(total, 0, keepdims=True))

        def mix(item):
            block, half = items[item]
            extent = (block + 1) * TILE
            columns = slice(block * TILE, extent)
            high, total = state[item]
            mixed = dot(vt_ref[64 * half : 64 * half + 64, :extent], expo_ref[item % 2, :extent, :])
            row = pl.multiple_of(pair * 128 + half * 64, 64)
            ctxt_ref[pl.ds(row, 64), columns] = mixed * (1.0 / total)
            lse_ref[pl.ds(pair * 2 + half, 1), columns] = high + jnp.log(total)

        count = len(items)
        score(0)
        for item in range(count + 1):
            if item + 1 < count:
                score(item + 1)
            if item >= 1:
                mix(item - 1)
            if item < count:
                exponential(item)
        ctx_ref[:, lanes] = ctxt_ref[lanes, :].T.astype(BF)
        start_all(results(pair))

    for pair in range(width // 128):
        wait_all(results(pair))


def pair_copies(source, target, pair, width, sems, matrices):
    return [
        pltpu.make_async_copy(
            source.at[:, pair_lanes(pair, matrix * width)],
            target.at[:, pair_lanes(pair, matrix * width)],
            sems.at[matrix, pair],
        )
        for matrix in range(matrices)
    ]


def forward_own_kernel(
    length_ref, qkv_hbm, lse_ref, ctx_out, ctxt_out, qkv_ref, ctx_ref, ctxt_ref, *rest
):
    scratch, in_sems, sems = rest[:5], rest[5], rest[6]
    width = ctx_ref.shape[1]
    source_in = lambda pair: pair_copies(qkv_hbm, qkv_ref, pair, width, in_sems, 3)
    for pair in range(width // 128):
        start_all(source_in(pair))
    forward_pairs(
        length_ref[0], qkv_ref, ctx_ref, ctxt_ref, lse_ref, scratch, source_in, ctx_out, ctxt_out, sems
    )


def forward_other_kernel(length_ref, turn_ref, a_hbm, vec_ref, *rest):
    pieces, rest = rest[:4], rest[4:]
    lse_ref, ctx_out, ctxt_out, qkv_out, qkv_ref, ctx_ref, ctxt_ref, *rest = rest
    scratch, a_ref, w_ref, a_sems, w_sems, qkv_sems, sems = rest[:5], *rest[5:]
    width = ctx_ref.shape[1]
    w_in = fetch_rows(pieces, turn_ref[0], w_ref, w_sems)
    start_all(w_in)
    a_in = tiles(a_hbm, a_ref, a_sems)
    start_all(a_in)
    bias, scale = qkv_bias(vec_ref[0:1, :], width)
    qkv_tiles = tiles(qkv_ref, qkv_out, qkv_sems)
    wait_all(w_in)
    for index, (copy, result) in enumerate(zip(a_in, qkv_tiles)):
        copy.wait()
        rows = slice(index * TILE, (index + 1) * TILE)
        qkv_ref[rows, :] = ((dot(a_ref[rows, :], w_ref[...]) + bias) * scale).astype(BF)
        result.start()
    forward_pairs(
        length_ref[0], qkv_ref, ctx_ref, ctxt_ref, lse_ref, scratch, None, ctx_out, ctxt_out, sems
    )
    wait_all(qkv_tiles)


def attention_forward(own, length, source, width, *rest):
    slots = source.shape[0]
    pairs = width // 128
    heads = width // 64
    tokens = slots // TILE
    dma = pltpu.SemaphoreType.DMA
    ins = [(length, SMEM)]
    outs = [
        ((heads, slots), F32, whole((heads, slots))),
        ((slots, width), BF, HBM),
        ((width, slots), F32, HBM),
    ]
    scratch = [
        pltpu.VMEM((slots, 3 * width), BF),
        pltpu.VMEM((slots, width), BF),
        pltpu.VMEM((width, slots), F32),
        pltpu.VMEM((2, slots, 128), BF),
        pltpu.VMEM((2, slots, 128), BF),
        pltpu.VMEM((128, slots), BF),
        pltpu.VMEM((2, slots, TILE), F32),
        pltpu.VMEM((2, slots, TILE), BF),
    ]
    flops = 6 * slots * slots * width
    if own:
        ins += [(source, HBM)]
        scratch += [dma((3, pairs)), dma((2, pairs))]
        return call(forward_own_kernel, "attention_forward_own", 1, ins, outs, scratch, flops)
    turn, vec, pieces = rest
    model = source.shape[1]
    ins += [(turn, SMEM), (source, HBM), (vec, whole(vec.shape))] + [(p, HBM) for p in pieces]
    outs += [((slots, 3 * width), BF, HBM)]
    scratch += [
        pltpu.VMEM((slots, model), BF),
        pltpu.VMEM((model, 3 * width), BF),
        dma((tokens,)),
        dma((3 * len(pieces),)),
        dma((tokens,)),
        dma((2, pairs)),
    ]
    flops += 6 * slots * model * width
    return call(forward_other_kernel, "attention_forward_other", 1, ins, outs, scratch, flops)


def grad_top_of(cot_ref, length, start):
    cot = cot_ref[...].astype(F32)
    position = lax.broadcasted_iota(jnp.int32, cot.shape, 0) + start
    return jnp.where(position < length, cot, 0.0)


def prepare_kernel(length_ref, cot_ref, gm_ref, gmt_ref, ob_ref):
    step = pl.program_id(0)

    @pl.when(step == 0)
    def _():
        ob_ref[...] = jnp.zeros(ob_ref.shape, F32)

    top = grad_top_of(cot_ref, length_ref[0], step * TILE)
    ob_ref[...] += BRANCH * jnp.sum(top, 0, keepdims=True)
    low = (BRANCH * top).astype(BF)
    gm_ref[...] = low
    gmt_ref[...] = low.T


def middle_kernel(
    count, turn_ref, x_ref, ctx0_ref, ctx1_ref, proj0_ref, vec_ref, *rest
):
    pieces, rest = rest[:count], rest[count:]
    middle_ref, c_ref, ct_ref, w_ref, sems = rest

    copies = fetch_rows(pieces, turn_ref[0], w_ref, sems)

    @pl.when(pl.program_id(0) == 0)
    def _():
        start_all(copies)

    mine = dot(ctx0_ref[...], proj0_ref[...]).astype(BF).astype(F32)

    @pl.when(pl.program_id(0) == 0)
    def _():
        wait_all(copies)

    theirs = dot(ctx1_ref[...], w_ref[...]).astype(BF).astype(F32)
    middle = x_ref[...].astype(F32) + BRANCH * ((mine + theirs) + vec_ref[BIAS_P : BIAS_P + 1, :])
    middle_ref[...] = middle
    normed, _ = norm_parts(middle)
    low = (normed * vec_ref[GAIN2 : GAIN2 + 1, :] + vec_ref[SHIFT2 : SHIFT2 + 1, :]).astype(BF)
    c_ref[...] = low
    ct_ref[...] = low.T


def mlp_kernel(own, count, base, steps, turn_ref, c_ref, g_hbm, vec_ref, *rest):
    if own:
        ct_hbm, gt_hbm, fc_ref, ow_ref, rest = rest[0], rest[1], rest[2], rest[3], rest[4:]
    else:
        fc_pieces, out_pieces, rest = rest[:count], rest[count : 2 * count], rest[2 * count :]
    mlp_ref, gc_ref, rest = rest[0], rest[1], rest[2:]
    if own:
        dwf_ref, dwo_ref, db_ref, rest = rest[0], rest[1], rest[2], rest[3:]
        mlp_acc, gc_acc, bias_ref, g_ref, act_ref, gh_ref, ct_ref, gt_ref, sems = rest
        fc_in = []
        late_in = [pltpu.make_async_copy(g_hbm, g_ref, sems.at[0])]
        last_in = [
            pltpu.make_async_copy(ct_hbm, ct_ref, sems.at[1]),
            pltpu.make_async_copy(gt_hbm, gt_ref, sems.at[2]),
        ]
    else:
        mlp_acc, gc_acc, bias_ref, g_ref, fc_ref, ow_ref, sems = rest
        fc_in = fetch_rows(fc_pieces, turn_ref[0], fc_ref, sems.at[0])
        late_in = [pltpu.make_async_copy(g_hbm, g_ref, sems.at[2, 0])]
        late_in += fetch_rows(out_pieces, turn_ref[0], ow_ref, sems.at[1])
        last_in = []
    step = pl.program_id(0)
    slots, model = c_ref.shape

    @pl.when(step == 0)
    def _():
        start_all(fc_in + late_in + last_in)
        for row in range(bias_ref.shape[1] // model):
            columns = slice(row * model, (row + 1) * model)
            bias_ref[:, columns] = vec_ref[base + row : base + row + 1, :]
        mlp_acc[...] = jnp.zeros(mlp_acc.shape, F32)
        gc_acc[...] = jnp.zeros(gc_acc.shape, F32)
        wait_all(fc_in + late_in + last_in)

    lanes = pl.ds(pl.multiple_of(step * HIDDEN, HIDDEN), HIDDEN)
    if own:
        fc, ow = fc_ref[...], ow_ref[...]
    else:
        fc, ow = fc_ref[:, lanes], ow_ref[lanes, :]
    hidden = dot(c_ref[...], fc) + bias_ref[:, lanes]
    square = hidden * hidden
    tanh = jnp.tanh(hidden * (GELU + GELU * CUBIC * square))
    share = 0.5 + 0.5 * tanh
    value = hidden * share
    slope = share + value * (1.0 - share) * (2.0 * GELU + 6.0 * GELU * CUBIC * square)
    act = value.astype(BF)
    gh = (dot_nt(g_ref[...], ow) * slope).astype(BF)
    if own:
        act_ref[...] = act
        gh_ref[...] = gh
        db_ref[...] = jnp.sum(gh.astype(F32), 0, keepdims=True)
    mlp_acc[...] += dot(act, ow)
    gc_acc[...] += dot_nt(gh, fc)
    if own:
        dwf_ref[...] = dot(ct_ref[...], gh_ref[...]).astype(BF)
        dwo_ref[...] = dot(gt_ref[...], act_ref[...]).astype(BF)

    @pl.when(step == steps - 1)
    def _():
        mlp_ref[...] = mlp_acc[...].astype(BF)
        gc_ref[...] = gc_acc[...].astype(BF)


def feed_forward(own, turn, c_low, grad_mlp, vec, base, turned, fc_pieces, out_pieces):
    slots, model = c_low.shape
    units = fc_pieces[0].shape[1]
    count = len(fc_pieces)
    steps = units // HIDDEN
    act = whole((slots, model))
    dma = pltpu.SemaphoreType.DMA
    ins = [(turn, SMEM), (c_low, act), (grad_mlp, HBM), (vec, whole(vec.shape))]
    outs = [((slots, model), BF, act), ((slots, model), BF, act)]
    scratch = [
        pltpu.VMEM((slots, model), F32),
        pltpu.VMEM((slots, model), F32),
        pltpu.VMEM((1, units), F32),
        pltpu.VMEM((slots, model), BF),
    ]
    if own:
        ins += [(value, HBM) for value in turned]
        ins += [
            (fc_pieces[0], column_tile(model, HIDDEN)),
            (out_pieces[0], pl.BlockSpec((HIDDEN, model), lambda i: (i, 0))),
        ]
        outs += [
            ((model, units), BF, column_tile(model, HIDDEN)),
            ((model, units), BF, column_tile(model, HIDDEN)),
            ((1, units), F32, column_tile(1, HIDDEN)),
        ]
        scratch += [
            pltpu.VMEM((slots, HIDDEN), BF),
            pltpu.VMEM((slots, HIDDEN), BF),
            pltpu.VMEM((model, slots), BF),
            pltpu.VMEM((model, slots), BF),
            dma((3,)),
        ]
    else:
        ins += [(piece, HBM) for piece in (*fc_pieces, *out_pieces)]
        scratch += [
            pltpu.VMEM((model, units), BF),
            pltpu.VMEM((units, model), BF),
            dma((3, count)),
        ]
    return call(
        functools.partial(mlp_kernel, own, count, base, steps),
        "feed_forward_own" if own else "feed_forward_other",
        steps,
        ins,
        outs,
        scratch,
        2 * slots * model * units * (6 if own else 4),
    )


def turn_kernel(
    count,
    turn_ref,
    length_ref,
    middle_ref,
    cot_ref,
    mlp0_ref,
    mlp1_ref,
    gc0_ref,
    gc1_ref,
    vec_ref,
    proj0_ref,
    *rest,
):
    pieces, rest = rest[:count], rest[count:]
    y_ref, gmid_ref, ga_ref, do0_ref, do1_ref, sums_ref, w_ref, sems = rest
    step = pl.program_id(0)

    copies = fetch_rows(pieces, turn_ref[0], w_ref, sems)

    @pl.when(step == 0)
    def _():
        start_all(copies)
        sums_ref[...] = jnp.zeros(sums_ref.shape, F32)

    middle = middle_ref[...]
    mlp = mlp0_ref[...].astype(F32) + mlp1_ref[...].astype(F32)
    y_ref[...] = (middle + BRANCH * (mlp + vec_ref[BIAS_O : BIAS_O + 1, :])).astype(BF)
    grad_c = gc0_ref[...].astype(F32) + gc1_ref[...].astype(F32)
    normed, inverse = norm_parts(middle)
    top = grad_top_of(cot_ref, length_ref[0], step * TILE)
    grad_middle = top + norm_back(grad_c, normed, inverse, vec_ref[GAIN2 : GAIN2 + 1, :])
    sums_ref[0:1, :] += jnp.sum(grad_c * normed, 0, keepdims=True)
    sums_ref[1:2, :] += jnp.sum(grad_c, 0, keepdims=True)
    sums_ref[2:3, :] += BRANCH * jnp.sum(grad_middle, 0, keepdims=True)
    gmid_ref[...] = grad_middle
    low = (BRANCH * grad_middle).astype(BF)
    ga_ref[...] = low
    do0_ref[...] = dot_nt(low, proj0_ref[...]).astype(BF)

    @pl.when(step == 0)
    def _():
        wait_all(copies)

    do1_ref[...] = dot_nt(low, w_ref[...]).astype(BF)


def backward_kernel(own, count, turn_ref, length_ref, lse_ref, qkv_hbm, do_hbm, ctxt_hbm, *rest):
    if own:
        late_hbm, rest = rest[:3], rest[3:]
    pieces, rest = rest[:count], rest[count:]
    gin_out, rest = rest[0], rest[1:]
    if own:
        dw_out, dp_out, qvb_ref, sums_ref, rest = rest[0], rest[1], rest[2], rest[3], rest[4:]
        at_ref, gat_ref, x_ref, dw_ref, dp_ref, late_sems, rest = *rest[:6], rest[6:]
    (
        qkv_ref,
        do_ref,
        ctxt_ref,
        gin_ref,
        w_ref,
        d_ref,
        ka_ref,
        qa_ref,
        do_mask_ref,
        kt_ref,
        qt_ref,
        dot_ref,
        delta_ref,
        dqt_ref,
        dkt_ref,
        dvt_ref,
        score_ref,
        grad_ref,
        prob_ref,
        slope_ref,
        sems,
        in_sems,
        gin_sems,
    ) = rest
    slots, width = do_ref.shape

    def source_in(pair):
        lanes = pair_lanes(pair)
        return pair_copies(qkv_hbm, qkv_ref, pair, width, in_sems, 3) + [
            pltpu.make_async_copy(do_hbm.at[:, lanes], do_ref.at[:, lanes], in_sems.at[3, pair]),
            pltpu.make_async_copy(ctxt_hbm.at[lanes, :], ctxt_ref.at[lanes, :], in_sems.at[4, pair]),
        ]

    for pair in range(width // 128):
        start_all(source_in(pair))
    copies = fetch_rows(pieces, turn_ref[0], w_ref, sems)
    if own:
        copies += [
            pltpu.make_async_copy(source, target, late_sems.at[index])
            for index, (source, target) in enumerate(zip(late_hbm, (at_ref, gat_ref, x_ref)))
        ]
    start_all(copies)
    length = length_ref[0]
    causal = causal_fill()
    blocks = slots // TILE

    @pl.loop(0, width // 128)
    def _(pair):
        lanes = pair_lanes(pair)
        wait_all(source_in(pair))
        keys_low = qkv_ref[:, pair_lanes(pair, width)]
        queries = qkv_ref[:, lanes]
        masked_pair(keys_low, queries, length, ka_ref, qa_ref)
        grads = do_ref[:, lanes]
        lane = lax.broadcasted_iota(jnp.int32, (slots, 128), 1)
        for half in (0, 1):
            do_mask_ref[half] = jnp.where(lane // 64 == half, grads.astype(F32), 0.0).astype(BF)
        kt_ref[...] = keys_low.T
        qt_ref[...] = queries.T
        turned = grads.T
        dot_ref[...] = turned
        product = turned.astype(F32) * ctxt_ref[lanes, :]
        for half in (0, 1):
            delta_ref[half : half + 1, :] = jnp.sum(
                product[64 * half : 64 * half + 64], 0, keepdims=True
            )
        items = [(block, half) for block in reversed(range(blocks)) for half in (0, 1)]

        def score(item):
            block, half = items[item]
            extent = (block + 1) * TILE
            columns = slice(block * TILE, extent)
            score_ref[item % 2, :extent, :] = dot_nt(
                ka_ref[half, :extent, :], qa_ref[half, columns, :]
            )
            grad_ref[item % 2, :extent, :] = dot_nt(
                qkv_ref[:extent, pair_lanes(pair, 2 * width)], do_mask_ref[half, columns, :]
            )

        def softmax(item):
            block, half = items[item]
            columns = slice(block * TILE, (block + 1) * TILE)
            lse = lse_ref[pl.ds(pair * 2 + half, 1), columns]
            delta = delta_ref[half : half + 1, columns]
            for inner in range(block + 1):
                keys = slice(inner * TILE, (inner + 1) * TILE)
                scores = score_ref[item % 2, keys, :]
                if inner == block:
                    scores = scores + causal
                prob = jnp.exp(scores - lse)
                slope_ref[item % 2, keys, :] = (
                    prob * (grad_ref[item % 2, keys, :] - delta)
                ).astype(BF)
                prob_ref[item % 2, keys, :] = prob.astype(BF)

        def gradients(item):
            block, half = items[item]
            extent = (block + 1) * TILE
            columns = slice(block * TILE, extent)
            rows = slice(64 * half, 64 * half + 64)
            dv_part = dot_nt(dot_ref[rows, columns], prob_ref[item % 2, :extent, :])
            dk_part = dot_nt(qt_ref[rows, columns], slope_ref[item % 2, :extent, :])
            if block == blocks - 1:
                dvt_ref[rows, :extent] = dv_part
                dkt_ref[rows, :extent] = dk_part
            else:
                dvt_ref[rows, :extent] += dv_part
                dkt_ref[rows, :extent] += dk_part
            dqt_ref[rows, columns] = dot(kt_ref[rows, :extent], slope_ref[item % 2, :extent, :])

        count_items = len(items)
        score(0)
        for item in range(count_items + 1):
            if item + 1 < count_items:
                score(item + 1)
            if item >= 1:
                gradients(item - 1)
            if item < count_items:
                softmax(item)
        d_ref[:, lanes] = (dqt_ref[...] * 0.125).astype(BF).T
        d_ref[:, pair_lanes(pair, width)] = dkt_ref[...].astype(BF).T
        d_ref[:, pair_lanes(pair, 2 * width)] = dvt_ref[...].astype(BF).T

    wait_all(copies)
    results = []
    if own:
        results = [
            pltpu.make_async_copy(dw_ref, dw_out, late_sems.at[3]),
            pltpu.make_async_copy(dp_ref, dp_out, late_sems.at[4]),
        ]
        dw_ref[...] = dot(at_ref[...], d_ref[...]).astype(BF)
        results[0].start()
        dp_ref[...] = dot(ctxt_ref[...].astype(BF), gat_ref[...]).T.astype(BF)
        results[1].start()
        sums = jnp.sum(d_ref[...].astype(F32), 0, keepdims=True)
        qvb_ref[:, :width] = sums[:, :width]
        qvb_ref[:, width:] = sums[:, 2 * width :]
        sums_ref[...] = jnp.zeros(sums_ref.shape, F32)
    gin_tiles = tiles(gin_ref, gin_out, gin_sems)
    for index, result in enumerate(gin_tiles):
        rows = slice(index * TILE, (index + 1) * TILE)
        part = dot_nt(d_ref[rows, :], w_ref[...])
        gin_ref[rows, :] = part.astype(BF)
        result.start()
        if own:
            normed, _ = norm_parts(x_ref[rows, :].astype(F32))
            sums_ref[0:1, :] += jnp.sum(part * normed, 0, keepdims=True)
            sums_ref[1:2, :] += jnp.sum(part, 0, keepdims=True)
    wait_all(results + gin_tiles)


def attention_backward(own, turn, length, qkv, do, ctxt, lse, extra, pieces):
    slots, width = do.shape
    model = pieces[0].shape[-2] * len(pieces)
    count = len(pieces)
    pairs = width // 128
    dma = pltpu.SemaphoreType.DMA
    ins = [(turn, SMEM), (length, SMEM), (lse, whole(lse.shape))]
    ins += [(value, HBM) for value in (qkv, do, ctxt, *extra, *pieces)]
    outs = [((slots, model), BF, HBM)]
    scratch = []
    if own:
        outs += [
            ((model, 3 * width), BF, HBM),
            ((model, width), BF, HBM),
            ((1, 2 * width), F32, whole((1, 2 * width))),
            ((2, model), F32, whole((2, model))),
        ]
        scratch += [
            pltpu.VMEM((model, slots), BF),
            pltpu.VMEM((slots, model), BF),
            pltpu.VMEM((slots, model), BF),
            pltpu.VMEM((model, 3 * width), BF),
            pltpu.VMEM((model, width), BF),
            dma((5,)),
        ]
    scratch += [
        pltpu.VMEM((slots, 3 * width), BF),
        pltpu.VMEM((slots, width), BF),
        pltpu.VMEM((width, slots), F32),
        pltpu.VMEM((slots, model), BF),
        pltpu.VMEM((model, 3 * width), BF),
        pltpu.VMEM((slots, 3 * width), BF),
        pltpu.VMEM((2, slots, 128), BF),
        pltpu.VMEM((2, slots, 128), BF),
        pltpu.VMEM((2, slots, 128), BF),
        pltpu.VMEM((128, slots), BF),
        pltpu.VMEM((128, slots), BF),
        pltpu.VMEM((128, slots), BF),
        pltpu.VMEM((2, slots), F32),
        pltpu.VMEM((128, slots), F32),
        pltpu.VMEM((128, slots), F32),
        pltpu.VMEM((128, slots), F32),
        pltpu.VMEM((2, slots, TILE), F32),
        pltpu.VMEM((2, slots, TILE), F32),
        pltpu.VMEM((2, slots, TILE), BF),
        pltpu.VMEM((2, slots, TILE), BF),
        dma((3 * count,)),
        dma((5, pairs)),
        dma((slots // TILE,)),
    ]
    return call(
        functools.partial(backward_kernel, own, count),
        "attention_backward_own" if own else "attention_backward_other",
        1,
        ins,
        outs,
        scratch,
        9 * slots * slots * width + 2 * slots * model * width * (7 if own else 3),
    )


def final_kernel(x_ref, gmid_ref, ga0_ref, ga1_ref, vec_ref, gin_ref):
    normed, inverse = norm_parts(x_ref[...].astype(F32))
    grad_a = ga0_ref[...].astype(F32) + ga1_ref[...].astype(F32)
    back = norm_back(grad_a, normed, inverse, vec_ref[GAIN1 : GAIN1 + 1, :])
    gin_ref[...] = gmid_ref[...] + back


def across(value):
    return lax.ppermute(value, "tensor", [(0, 1), (1, 0)])


def swap(value, bit):
    count = lax.axis_size("dp")
    return lax.ppermute(value, "dp", [(i, i ^ bit) for i in range(count)])


def tie(*values):
    return lax.optimization_barrier(values)


def pick(value, index, axis):
    return lax.dynamic_index_in_dim(value, index, axis, keepdims=False)


def split_rows(value, count):
    shape = value.shape
    return value.reshape(*shape[:-2], count, shape[-2] // count, shape[-1])


def halve(total, place, bit):
    pairs = total.reshape(total.shape[0] // 2, 2, *total.shape[1:])
    side = (place // bit) % 2
    return pick(pairs, side, 1), pick(pairs, 1 - side, 1)


def two_parts(value):
    high = lax.reduce_precision(value, 8, 7)
    return jnp.concatenate([high, value - high], 0).astype(BF)


class Reduction:
    def __init__(self, grad, order):
        self.shards = lax.axis_size("dp")
        self.order = order
        self.bits = [bit for bit in reversed(range(self.shards.bit_length() - 1))]
        rows, columns = grad.shape
        self.total = grad.reshape(*[2] * len(self.bits), rows // self.shards, columns)

    def send(self):
        self.bit = self.order.pop(0)
        axis = self.bits.index(self.bit)
        self.bits.remove(self.bit)
        side = (lax.axis_index("dp") >> self.bit) & 1
        sent = pick(self.total, 1 - side, axis)
        self.kept = pick(self.total, side, axis)
        self.shape = sent.shape
        return sent.reshape(-1, sent.shape[-1])

    def receive(self, got):
        total = self.kept.astype(F32) + got.reshape(self.shape).astype(F32)
        self.total = total.astype(BF) if self.bits else total


def local(
    block_input,
    first_gain,
    first_shift,
    qkv_weight,
    qv_bias,
    proj_weight,
    proj_bias,
    second_gain,
    second_shift,
    fc_weight,
    fc_bias,
    out_weight,
    out_bias,
    cotangent,
    lengths,
):
    slots, model = block_input.shape
    width = qkv_weight.shape[2]
    units = fc_weight.shape[1]
    shards = lax.axis_size("dp")
    levels = shards.bit_length() - 1
    place = lax.axis_index("dp")
    quarter = jnp.bitwise_and(place, 3)
    one_bit = jnp.bitwise_and(place, 1)
    turn4 = quarter.reshape(1).astype(jnp.int32)
    turn2 = one_bit.reshape(1).astype(jnp.int32)
    turn0 = jnp.zeros((1,), jnp.int32)
    length = lengths.astype(jnp.int32)
    act = whole((slots, model))

    qkv_mine = across(pick(split_rows(qkv_weight, 4), quarter, 1))
    bits = jnp.stack([one_bit, quarter]).astype(jnp.int32)
    vectors = (first_gain, first_shift, proj_bias, second_gain, second_shift, out_bias)
    vec, a_low, a_turned, qkv0, proj_send, fc_send, out_send = project(
        bits,
        block_input,
        (*vectors, qv_bias, fc_bias),
        qkv_weight,
        proj_weight,
        fc_weight,
        out_weight,
    )

    qkv_mine, qkv0, proj_send, fc_send = tie(qkv_mine, qkv0, proj_send, fc_send)
    qkv_side = swap(qkv_mine, 2)
    qkv_core = swap(qkv_mine, 1)
    proj_got = across(proj_send)
    fc_mine = across(fc_send)
    lse0, ctx0, ctxt0 = attention_forward(True, length, qkv0, width)

    qkv_side, qkv_core, proj_got, ctx0, cot = tie(qkv_side, qkv_core, proj_got, ctx0, cotangent)
    half_rows = width // 2
    proj_mine = proj_got[:half_rows]
    parts = proj_got[half_rows : half_rows + 24].astype(F32).reshape(3, 8, model)
    other_vec = (parts[0] + parts[1]) + parts[2]
    proj_other = [proj_mine, swap(proj_mine, 1)]
    qkv_other = [qkv_mine, qkv_core, qkv_side, swap(qkv_side, 1)]
    grad_mlp, grad_mlp_turned, grad_out_bias = call(
        prepare_kernel,
        "prepare",
        slots // TILE,
        [(length, SMEM), (cot, row_tile(model))],
        [
            ((slots, model), BF, row_tile(model)),
            ((model, slots), BF, column_tile(model)),
            ((1, model), F32, whole((1, model))),
        ],
        [],
        8 * slots * model,
    )

    grad_mlp, a_low, out_send, *qkv_other = tie(grad_mlp, a_low, out_send, *qkv_other)
    out_mine = across(out_send)
    lse1, ctx1, ctxt1, qkv1 = attention_forward(
        False, length, a_low, width, turn4, other_vec, qkv_other
    )

    ctx1, fc_mine = tie(ctx1, fc_mine)
    fc_side = swap(fc_mine, 2)
    fc_core = swap(fc_mine, 1)
    middle, c_low, c_turned = call(
        functools.partial(middle_kernel, 2),
        "middle",
        slots // TILE,
        [
            (turn2, SMEM),
            (block_input, row_tile(model)),
            (ctx0, row_tile(width)),
            (ctx1, row_tile(width)),
            (proj_weight, whole((width, model))),
            (vec, whole(vec.shape)),
            *[(piece, HBM) for piece in proj_other],
        ],
        [
            ((slots, model), F32, row_tile(model)),
            ((slots, model), BF, row_tile(model)),
            ((model, slots), BF, column_tile(model)),
        ],
        [pltpu.VMEM((width, model), BF), pltpu.SemaphoreType.DMA((2,))],
        4 * slots * model * width,
    )

    c_low, out_mine = tie(c_low, out_mine)
    out_side = swap(out_mine, 2)
    out_core = swap(out_mine, 1)
    mlp0, gc0, dwf, dwo, grad_fc_bias = feed_forward(
        True,
        turn0,
        c_low,
        grad_mlp,
        vec,
        BIAS_FC,
        (c_turned, grad_mlp_turned),
        [fc_weight],
        [out_weight],
    )

    dwf, dwo, fc_side, out_side, fc_core, out_core = tie(
        dwf, dwo, fc_side, out_side, fc_core, out_core
    )
    order_a = list(range(levels))
    order_b = [0, 2, 1] + list(range(3, levels))
    fc_sum = Reduction(dwf, list(order_a))
    out_sum = Reduction(dwo, list(order_b))
    fc_other = [fc_mine, fc_core, fc_side, swap(fc_side, 1)]
    out_other = [out_mine, out_core, out_side, swap(out_side, 1)]
    fc_got = swap(fc_sum.send(), 1)
    out_got = swap(out_sum.send(), 1)
    mlp1, gc1 = feed_forward(
        False, turn4, c_low, grad_mlp, other_vec, 1, None, fc_other, out_other
    )

    mlp1, fc_got, out_got = tie(mlp1, fc_got, out_got)
    fc_sum.receive(fc_got)
    out_sum.receive(out_got)
    fc_sent = fc_sum.send()
    out_sent = out_sum.send()
    mlp1, fc_sent, out_sent = tie(mlp1, fc_sent, out_sent)
    fc_got = swap(fc_sent, 1 << fc_sum.bit)
    out_got = swap(out_sent, 1 << out_sum.bit)
    block_output, grad_middle, grad_attn, do0, do1, sums2 = call(
        functools.partial(turn_kernel, 2),
        "turn",
        slots // TILE,
        [
            (turn2, SMEM),
            (length, SMEM),
            (middle, row_tile(model)),
            (cotangent, row_tile(model)),
            (mlp0, row_tile(model)),
            (mlp1, row_tile(model)),
            (gc0, row_tile(model)),
            (gc1, row_tile(model)),
            (vec, whole(vec.shape)),
            (proj_weight, whole((width, model))),
            *[(piece, HBM) for piece in proj_other],
        ],
        [
            ((slots, model), BF, row_tile(model)),
            ((slots, model), F32, row_tile(model)),
            ((slots, model), BF, row_tile(model)),
            ((slots, width), BF, row_tile(width)),
            ((slots, width), BF, row_tile(width)),
            ((3, model), F32, whole((3, model))),
        ],
        [pltpu.VMEM((width, model), BF), pltpu.SemaphoreType.DMA((2,))],
        4 * slots * model * width,
    )
    ga0, dw, dp, grad_qv, sums1 = attention_backward(
        True,
        turn0,
        length,
        qkv0,
        do0,
        ctxt0,
        lse0,
        (a_turned, grad_attn, block_input),
        [qkv_weight],
    )

    dw, dp, sums1, fc_got, out_got = tie(dw, dp, sums1, fc_got, out_got)
    first_sum = Reduction(dw[:, :model], list(order_a))
    second_sum = Reduction(jnp.concatenate([dw[:, model:], dp], 1), list(order_b))
    first_got = swap(first_sum.send(), 1)
    second_got = swap(second_sum.send(), 1)
    sums1_other = across(sums1)
    fc_sum.receive(fc_got)
    out_sum.receive(out_got)
    fc_sent = fc_sum.send()
    out_sent = out_sum.send()
    fc_got = swap(fc_sent, 1 << fc_sum.bit)
    out_got = swap(out_sent, 1 << out_sum.bit)
    vectors = jnp.concatenate(
        [
            (sums1 + sums1_other).reshape(-1),
            grad_out_bias.reshape(-1),
            sums2.reshape(-1),
            grad_fc_bias.reshape(-1),
            grad_qv.reshape(-1),
        ]
    ).reshape(-1, model)
    vectors = vectors + swap(vectors, 1)
    first_sum.receive(first_got)
    second_sum.receive(second_got)

    def with_vectors(sent):
        return jnp.concatenate([sent, two_parts(vectors)], 0)

    def take_vectors(got, vectors):
        lines = vectors.shape[0]
        high = lax.reduce_precision(vectors, 8, 7)
        mine = high + lax.reduce_precision(vectors - high, 8, 7)
        tail = got[-2 * lines :].astype(F32)
        return got[: -2 * lines], mine + (tail[:lines] + tail[lines:])

    first_sent = with_vectors(first_sum.send())
    second_sent = second_sum.send()
    first_sent, second_sent, qkv1 = tie(first_sent, second_sent, qkv1)
    first_got = swap(first_sent, 1 << first_sum.bit)
    second_got = swap(second_sent, 1 << second_sum.bit)
    (ga1,) = attention_backward(False, turn4, length, qkv1, do1, ctxt1, lse1, (), qkv_other)

    ga1, fc_got, out_got, first_got, second_got = tie(ga1, fc_got, out_got, first_got, second_got)
    first_got, vectors = take_vectors(first_got, vectors)
    first_sum.receive(first_got)
    second_sum.receive(second_got)
    first_sent = with_vectors(first_sum.send())
    second_sent = second_sum.send()
    fc_sum.receive(fc_got)
    out_sum.receive(out_got)
    rest_sent = jnp.concatenate([fc_sum.send(), out_sum.send()], 0)
    ga1, first_sent, second_sent, rest_sent = tie(ga1, first_sent, second_sent, rest_sent)
    first_got = swap(first_sent, 1 << first_sum.bit)
    second_got = swap(second_sent, 1 << second_sum.bit)
    rest_got = swap(rest_sent, 1 << fc_sum.bit)
    (grad_input,) = call(
        final_kernel,
        "final",
        slots // TILE,
        [
            (block_input, row_tile(model)),
            (grad_middle, row_tile(model)),
            (ga0, row_tile(model)),
            (ga1, row_tile(model)),
            (vec, whole(vec.shape)),
        ],
        [((slots, model), F32, row_tile(model))],
        [],
        20 * slots * model,
    )

    grad_input, first_got, second_got = tie(grad_input, first_got, second_got)
    first_got, vectors = take_vectors(first_got, vectors)
    first_sum.receive(first_got)
    second_sum.receive(second_got)
    for _ in range(3, levels):
        lines = rest_got.shape[0] // 2
        fc_sum.receive(rest_got[:lines])
        out_sum.receive(rest_got[lines:])
        sent = jnp.concatenate([first_sum.send(), second_sum.send(), two_parts(vectors)], 0)
        got = swap(sent, 1 << first_sum.bit)
        got, vectors = take_vectors(got, vectors)
        lines = got.shape[0] // 2
        first_sum.receive(got[:lines])
        second_sum.receive(got[lines:])
        if fc_sum.order:
            rest_sent = jnp.concatenate([fc_sum.send(), out_sum.send()], 0)
            rest_got = swap(rest_sent, 1 << fc_sum.bit)
    grad_fc_weight = fc_sum.total
    grad_out_weight = out_sum.total.T
    first, second = first_sum.total, second_sum.total
    grad_qkv_weight = jnp.stack([first[:, :width], first[:, width:], second[:, :width]])
    grad_proj_weight = second[:, width:].T
    vectors = vectors.reshape(-1)
    sizes = [model] * 6 + [units, 2 * width]
    pieces = []
    start = 0
    for size in sizes:
        pieces.append(vectors[start : start + size])
        start += size
    (
        grad_first_gain,
        grad_first_shift,
        grad_out_bias,
        grad_second_gain,
        grad_second_shift,
        grad_proj_bias,
        grad_fc_bias,
        grad_qv,
    ) = pieces
    return (
        block_output,
        grad_input,
        grad_first_gain,
        grad_first_shift,
        grad_qkv_weight,
        grad_qv.reshape(2, width),
        grad_proj_weight,
        grad_proj_bias,
        grad_second_gain,
        grad_second_shift,
        grad_fc_weight,
        grad_fc_bias,
        grad_out_weight,
        grad_out_bias,
    )


def solution(mesh):
    placed = (
        P("dp", None),
        P(),
        P(),
        P(None, None, "tensor"),
        P(None, "tensor"),
        P("tensor", None),
        P(),
        P(),
        P(),
        P(None, "tensor"),
        P("tensor"),
        P("tensor", None),
        P(),
        P("dp", None),
        P("dp"),
    )
    return jax.shard_map(
        local,
        mesh=mesh,
        in_specs=placed,
        out_specs=(
            P("dp", None),
            P("dp", None),
            P(),
            P(),
            P(None, "dp", "tensor"),
            P(None, "tensor"),
            P("tensor", "dp"),
            P(),
            P(),
            P(),
            P("dp", "tensor"),
            P("tensor"),
            P("tensor", "dp"),
            P(),
        ),
        check_vma=False,
    )
```

```python
import functools

import jax
import jax.numpy as jnp
from jax import lax
from jax.experimental import pallas as pl
from jax.experimental.pallas import tpu as pltpu
from jax.sharding import PartitionSpec as P

EPSILON = 1e-05
BRANCH = 48 ** (-0.5)
GELU = 0.7978845608028654
CUBIC = 0.044715
FILL = -1e30
BF = jnp.bfloat16
F32 = jnp.float32
MIB = 1024 * 1024
TILE = 256
HIDDEN = 512
GAIN1, SHIFT1, BIAS_P, GAIN2, SHIFT2, BIAS_O = range(6)
BIAS_QV, BIAS_FC = 8, 9


def dot(left, right):
    return lax.dot_general(left, right, (((1,), (0,)), ((), ())), preferred_element_type=F32)


def dot_nt(left, right):
    return lax.dot_general(left, right, (((1,), (1,)), ((), ())), preferred_element_type=F32)


def norm_parts(values):
    row_mean = jnp.mean(values, -1, keepdims=True)
    centered = values - row_mean
    inverse = lax.rsqrt(jnp.mean(centered * centered, -1, keepdims=True) + EPSILON)
    return centered * inverse, inverse


def norm_back(grad_out, normed, inverse, gain):
    scaled = grad_out * gain
    inner = (
        scaled
        - jnp.mean(scaled, -1, keepdims=True)
        - normed * jnp.mean(scaled * normed, -1, keepdims=True)
    )
    return inverse * inner


def whole(shape):
    return pl.BlockSpec(shape, lambda *_: (0,) * len(shape))


def row_tile(columns):
    return pl.BlockSpec((TILE, columns), lambda i: (i, 0))


def column_tile(rows, size=TILE):
    return pl.BlockSpec((rows, size), lambda i: (0, i))


SMEM = pl.BlockSpec(memory_space=pltpu.SMEM)
HBM = pl.BlockSpec(memory_space=pl.ANY)
KEPT = pl.BlockSpec(memory_space=pltpu.VMEM)


def call(body, name, steps, ins, outs, scratch, flops, limit=12):
    args = []
    for array, spec in ins:
        if spec is KEPT:
            array = pltpu.with_memory_space_constraint(array, pltpu.VMEM)
        elif spec is not SMEM:
            array = pltpu.with_memory_space_constraint(array, pltpu.HBM)
        args.append(array)
    moved = sum(a.size * a.dtype.itemsize for a, spec in ins if spec is not KEPT)
    moved += sum(
        jax.ShapeDtypeStruct(shape, dtype).size * jnp.dtype(dtype).itemsize
        for shape, dtype, spec in outs
        if spec is not KEPT
    )
    return pl.pallas_call(
        body,
        name=name,
        grid=(steps,),
        out_shape=tuple(
            (pltpu.VMEM if spec is KEPT else pltpu.HBM)(shape, dtype) for shape, dtype, spec in outs
        ),
        in_specs=[spec for _, spec in ins],
        out_specs=tuple(spec for _, _, spec in outs),
        scratch_shapes=scratch,
        compiler_params=pltpu.CompilerParams(vmem_limit_bytes=limit * MIB),
        cost_estimate=pl.CostEstimate(flops=flops, bytes_accessed=moved, transcendentals=0),
    )(*args)


def tile_of(step):
    return pl.ds(pl.multiple_of(step * TILE, TILE), TILE)


def fetch_rows(pieces, turn, target, sems):
    copies = []
    for index, piece in enumerate(pieces):
        rows = piece.shape[-2]
        if len(pieces) > 1:
            place = jnp.bitwise_xor(jnp.int32(index), turn)
            where = pl.ds(pl.multiple_of(place * rows, 32), rows)
        else:
            where = slice(None)
        if len(piece.shape) == 2:
            copies.append(pltpu.make_async_copy(piece, target.at[where, :], sems.at[index]))
            continue
        width = piece.shape[2]
        for matrix in range(3):
            columns = slice(matrix * width, (matrix + 1) * width)
            copies.append(
                pltpu.make_async_copy(
                    piece.at[matrix], target.at[where, columns], sems.at[3 * index + matrix]
                )
            )
    return copies


def start_all(copies):
    for copy in copies:
        copy.start()


def wait_all(copies):
    for copy in copies:
        copy.wait()


def qkv_bias(biases, width):
    bias = jnp.concatenate(
        [biases[:, :width], jnp.zeros((1, width), F32), biases[:, width:]], axis=1
    )
    lane = lax.broadcasted_iota(jnp.int32, (1, 3 * width), 1)
    return bias, jnp.where(lane < width, 0.125, 1.0)


def tiles(source, target, sems, axis=0):
    copies = []
    for index in range(source.shape[axis] // TILE):
        part = slice(index * TILE, (index + 1) * TILE)
        view = (part, slice(None)) if axis == 0 else (slice(None), part)
        copies.append(pltpu.make_async_copy(source.at[view], target.at[view], sems.at[index]))
    return copies


def tile_copy(source, target, sems, index):
    rows = tile_of(index)
    return pltpu.make_async_copy(source.at[rows, :], target.at[rows, :], sems.at[index])


def clear(*refs):
    @pl.loop(0, refs[0].shape[0] // TILE)
    def _(index):
        for ref in refs:
            ref[tile_of(index), :] = jnp.zeros((TILE, ref.shape[1]), ref.dtype)


def halves(value_ref, side, block, kept_ref, sent_ref):
    @pl.loop(0, value_ref.shape[0] // (2 * block))
    def _(index):
        rows = pl.ds(pl.multiple_of(index * block, 16), block)
        first = 2 * block * index
        here = pl.ds(pl.multiple_of(first + block * side, 16), block)
        there = pl.ds(pl.multiple_of(first + block * (1 - side), 16), block)
        kept_ref[rows, :] = value_ref[here, :]
        sent_ref[rows, :] = value_ref[there, :]


def grad_top_of(cot, length, start):
    rows, model = cot.shape
    position = lax.broadcasted_iota(jnp.int32, (rows, 128), 0) + start
    valid = jnp.where(position < length, 1.0, 0.0)
    return cot.astype(F32) * jnp.concatenate([valid] * (model // 128), axis=1)


def project_kernel(
    bits_ref,
    x_hbm,
    gain1_ref,
    shift1_ref,
    bias_p_ref,
    gain2_ref,
    shift2_ref,
    bias_o_ref,
    qv_ref,
    fcb_ref,
    qkv_hbm,
    proj_hbm,
    fc_hbm,
    out_hbm,
    length_ref,
    cot_hbm,
    vec_ref,
    qkv_ref,
    gm_ref,
    gmt_ref,
    ob_ref,
    a_out,
    at_out,
    proj_out,
    fc_out,
    out_out,
    x_ref,
    w_ref,
    a_ref,
    at_ref,
    proj_ref,
    fc_ref,
    out_ref,
    cot_ref,
    low_ref,
    x_sems,
    w_sems,
    cot_sems,
    send_sems,
    a_sems,
    at_sems,
):
    x_in = tiles(x_hbm, x_ref, x_sems)
    x_in[0].start()
    w_in = fetch_rows([qkv_hbm], 0, w_ref, w_sems)
    start_all(w_in)
    start_all(x_in[1:])
    model = x_ref.shape[1]
    half, quarter, fourth = proj_hbm.shape[0] // 2, fc_hbm.shape[0] // 4, out_hbm.shape[0] // 4
    sends_in = []
    for index, (source, target, place, rows) in enumerate(
        (
            (proj_hbm, proj_ref.at[:half, :], bits_ref[0], half),
            (fc_hbm, fc_ref, bits_ref[1], quarter),
            (out_hbm, out_ref, bits_ref[4], fourth),
        )
    ):
        where = pl.ds(pl.multiple_of(place * rows, 32), rows)
        sends_in.append(pltpu.make_async_copy(source.at[where, :], target, send_sems.at[index]))
    start_all(sends_in)
    sends_out = [
        pltpu.make_async_copy(source, target, send_sems.at[3 + index])
        for index, (source, target) in enumerate(
            ((proj_ref, proj_out), (fc_ref, fc_out), (out_ref, out_out))
        )
    ]
    cot_in = tiles(cot_hbm, cot_ref, cot_sems)
    start_all(cot_in)
    vec_ref[...] = jnp.zeros(vec_ref.shape, F32)
    for index, ref in enumerate(
        (gain1_ref, shift1_ref, bias_p_ref, gain2_ref, shift2_ref, bias_o_ref)
    ):
        vec_ref[index : index + 1, :] = ref[...].reshape(1, model)
    width = qv_ref.shape[1]
    vec_ref[BIAS_QV : BIAS_QV + 1, :width] = qv_ref[0:1, :]
    vec_ref[BIAS_QV : BIAS_QV + 1, width:] = qv_ref[1:2, :]
    fcb = fcb_ref[...].reshape(1, fcb_ref.shape[0])
    for index in range(2):
        vec_ref[BIAS_FC + index : BIAS_FC + index + 1, :] = fcb[:, index * model : (index + 1) * model]
    value = vec_ref[8 * (BIAS_QV // 8) :, :]
    high = value.astype(BF)
    rest = value - high.astype(F32)
    mid = rest.astype(BF)
    low = (rest - mid.astype(F32)).astype(BF)
    lines = value.shape[0]
    for index, part in enumerate((high, mid, low)):
        proj_ref[half + index * lines : half + (index + 1) * lines, :] = part

    def normalize(index):
        rows = tile_of(index)
        normed, _ = norm_parts(x_ref[rows, :].astype(F32))
        low = normed * vec_ref[GAIN1 : GAIN1 + 1, :] + vec_ref[SHIFT1 : SHIFT1 + 1, :]
        low = low.astype(BF)
        low_ref[...] = low
        a_ref[rows, :] = low
        at_ref[:, rows] = low.T

    def gradient(index):
        rows = tile_of(index)
        top = grad_top_of(cot_ref[rows, :], length_ref[0], index * TILE)
        ob_ref[...] += BRANCH * jnp.sum(top, 0, keepdims=True)
        low = (BRANCH * top).astype(BF)
        gm_ref[rows, :] = low
        gmt_ref[:, rows] = low.T

    def multiply(index):
        qkv_ref[tile_of(index), :] = ((dot(low_ref[...], w_ref[...]) + bias) * scale).astype(BF)

    count = len(x_in)
    bias, scale = qkv_bias(vec_ref[BIAS_QV : BIAS_QV + 1, :], width)
    a_tiles = tiles(a_ref, a_out, a_sems)
    at_tiles = tiles(at_ref, at_out, at_sems, 1)
    ob_ref[...] = jnp.zeros(ob_ref.shape, F32)
    x_in[0].wait()
    normalize(0)
    wait_all(w_in + x_in[1:])

    @pl.loop(0, count - 1)
    def _(index):
        multiply(index)
        normalize(index + 1)

    start_all(a_tiles + at_tiles)
    wait_all(sends_in + cot_in)
    start_all(sends_out)
    multiply(count - 1)

    @pl.loop(0, count)
    def _(index):
        gradient(index)

    wait_all(sends_out + a_tiles + at_tiles)


def project(bits, length, x, cot, vectors, qkv, proj, fc, ow):
    slots, model = x.shape
    width = qkv.shape[2]
    units = fc.shape[1]
    tokens = slots // TILE
    sends = [
        (width // 2 + 32, model),
        (model // 4, units),
        (units // 4, model),
    ]
    shapes = [(slots, model), (model, slots)]
    dma = pltpu.SemaphoreType.DMA
    return call(
        project_kernel,
        "project_own",
        1,
        [(bits, SMEM), (x, HBM)]
        + [(vector, whole(vector.shape)) for vector in vectors]
        + [(weight, HBM) for weight in (qkv, proj, fc, ow)]
        + [(length, SMEM), (cot, HBM)],
        [
            ((16, model), F32, whole((16, model))),
            ((slots, 3 * width), BF, KEPT),
            ((slots, model), BF, KEPT),
            ((model, slots), BF, KEPT),
            ((1, model), F32, whole((1, model))),
        ]
        + [(shape, BF, HBM) for shape in shapes + sends],
        [pltpu.VMEM((slots, model), BF), pltpu.VMEM((model, 3 * width), BF)]
        + [pltpu.VMEM(shape, BF) for shape in shapes + sends]
        + [pltpu.VMEM((slots, model), BF), pltpu.VMEM((TILE, model), BF)]
        + [dma((tokens,)), dma((3,)), dma((tokens,)), dma((6,)), dma((tokens,)), dma((tokens,))],
        6 * slots * model * width,
        20,
    )


def causal_fill():
    keys = lax.broadcasted_iota(jnp.int32, (TILE, TILE), 0)
    queries = lax.broadcasted_iota(jnp.int32, (TILE, TILE), 1)
    return jnp.where(keys <= queries, 0.0, FILL)


def masked_pair(pair_keys, pair_queries, length, keys_ref, queries_ref):
    slots = pair_keys.shape[0]
    lane = lax.broadcasted_iota(jnp.int32, (slots, 128), 1)
    position = lax.broadcasted_iota(jnp.int32, (slots, 128), 0)
    fill = jnp.where(position < length, 0.0, FILL)
    pair_keys = pair_keys.astype(F32)
    pair_queries = pair_queries.astype(F32)
    for half in (0, 1):
        spare = 64 * (1 - half)
        keys_ref[half] = jnp.where(lane == spare, fill, pair_keys).astype(BF)
        queries_ref[half] = jnp.where(
            lane // 64 == half, pair_queries, jnp.where(lane == spare, 1.0, 0.0)
        ).astype(BF)


def pair_lanes(pair, offset=0):
    return pl.ds(pl.multiple_of(offset + pair * 128, 128), 128)


def forward_pairs(length, qkv_ref, ctx_ref, ctxt_ref, lse_ref, scratch, results):
    ka_ref, qa_ref, vt_ref, score_ref, expo_ref = scratch
    width, slots = ctxt_ref.shape
    causal = causal_fill()

    @pl.loop(0, width // 128)
    def _(pair):
        lanes = pair_lanes(pair)
        masked_pair(
            qkv_ref[:, pair_lanes(pair, width)], qkv_ref[:, lanes], length, ka_ref, qa_ref
        )
        vt_ref[...] = qkv_ref[:, pair_lanes(pair, 2 * width)].T
        items = [(block, half) for block in range(slots // TILE) for half in (0, 1)]
        state = {}

        def score(item):
            block, half = items[item]
            extent = (block + 1) * TILE
            columns = slice(block * TILE, extent)
            scores = dot_nt(ka_ref[half, :extent, :], qa_ref[half, columns, :])
            high = None
            for inner in range(block + 1):
                keys = slice(inner * TILE, (inner + 1) * TILE)
                part = scores[keys]
                if inner == block:
                    part = part + causal
                score_ref[item % 2, keys, :] = part
                most = jnp.max(part.reshape(TILE // 8, 8, TILE), 0)
                high = most if high is None else jnp.maximum(high, most)
            state[item] = jnp.max(high, 0, keepdims=True)

        def exponential(item):
            block, half = items[item]
            high = state[item]
            total = None
            for inner in range(block + 1):
                keys = slice(inner * TILE, (inner + 1) * TILE)
                expo = jnp.exp(score_ref[item % 2, keys, :] - high)
                part = jnp.sum(expo.reshape(TILE // 8, 8, TILE), 0)
                total = part if total is None else total + part
                expo_ref[item % 2, keys, :] = expo.astype(BF)
            state[item] = (high, jnp.sum(total, 0, keepdims=True))

        def mix(item):
            block, half = items[item]
            extent = (block + 1) * TILE
            columns = slice(block * TILE, extent)
            high, total = state[item]
            mixed = dot(vt_ref[64 * half : 64 * half + 64, :extent], expo_ref[item % 2, :extent, :])
            row = pl.multiple_of(pair * 128 + half * 64, 64)
            ctxt_ref[pl.ds(row, 64), columns] = mixed * (1.0 / total)
            lse_ref[pl.ds(pair * 2 + half, 1), columns] = high + jnp.log(total)

        count = len(items)
        score(0)
        for item in range(count + 1):
            if item + 1 < count:
                score(item + 1)
            if item >= 1:
                mix(item - 1)
            if item < count:
                exponential(item)
        ctx_ref[:, lanes] = ctxt_ref[lanes, :].T.astype(BF)
        start_all(results(pair))


def forward_own_kernel(
    length_ref, qkv_ref, lse_ref, ctx_out, ctxt_out, qkv_out, ctx_ref, ctxt_ref, *rest
):
    scratch, sems = rest[:5], rest[5]
    saved = pltpu.make_async_copy(qkv_ref, qkv_out, sems.at[2, 0])
    saved.start()

    def results(pair):
        lanes = pair_lanes(pair)
        return [
            pltpu.make_async_copy(ctx_ref.at[:, lanes], ctx_out.at[:, lanes], sems.at[0, pair]),
            pltpu.make_async_copy(ctxt_ref.at[lanes, :], ctxt_out.at[lanes, :], sems.at[1, pair]),
        ]

    forward_pairs(length_ref[0], qkv_ref, ctx_ref, ctxt_ref, lse_ref, scratch, results)
    for pair in range(ctx_ref.shape[1] // 128):
        wait_all(results(pair))
    saved.wait()


def forward_other_kernel(
    bits_ref, length_ref, other_vec_ref, vec_ref, a_hbm, x_hbm, ctx0_hbm, proj0_hbm, *rest
):
    pieces, proj_pieces, rest = rest[:4], rest[4:6], rest[6:]
    lse_ref, c_ref, ct_ref, middle_out, ctxt_out, qkv_out, *rest = rest
    both_ref, ctxt_ref, *rest = rest
    scratch, rest = rest[:5], rest[5:]
    qkv_ref, a_ref, w_ref, x_ref, proj_ref, middle_ref, sum_ref, *rest = rest
    a_sems, w_sems, qkv_sems, sems, late_sems, proj_sems, middle_sems = rest
    slots, width = ctx0_hbm.shape
    own = pl.ds(pl.multiple_of(bits_ref[3] * width, 128), width)
    other = pl.ds(pl.multiple_of((1 - bits_ref[3]) * width, 128), width)
    ctx_ref = both_ref.at[:, other]
    w_in = fetch_rows(pieces, bits_ref[1], w_ref, w_sems)
    start_all(w_in)
    a_in = tiles(a_hbm, a_ref, a_sems)
    start_all(a_in)
    late = [
        pltpu.make_async_copy(source, target, late_sems.at[index])
        for index, (source, target) in enumerate(
            ((x_hbm, x_ref), (ctx0_hbm, both_ref.at[:, own]), (proj0_hbm, proj_ref.at[own, :]))
        )
    ]
    halves_in = [piece.at[: width // 2, :] for piece in proj_pieces]
    late += fetch_rows(halves_in, bits_ref[0], proj_ref.at[other, :], proj_sems)
    start_all(late)
    bias, scale = qkv_bias(other_vec_ref[0:1, :], width)
    qkv_tiles = tiles(qkv_ref, qkv_out, qkv_sems)
    wait_all(w_in + a_in)

    @pl.loop(0, len(a_in))
    def _(index):
        rows = tile_of(index)
        product = dot(a_ref[rows, :], w_ref[...])
        qkv_ref[rows, :] = ((product + bias) * scale).astype(BF)

    start_all(qkv_tiles)

    def results(pair):
        lanes = pair_lanes(pair)
        return [
            pltpu.make_async_copy(ctxt_ref.at[lanes, :], ctxt_out.at[lanes, :], sems.at[pair])
        ]

    forward_pairs(length_ref[0], qkv_ref, ctx_ref, ctxt_ref, lse_ref, scratch, results)
    wait_all(late)
    count = slots // TILE

    def branch(index):
        return dot(both_ref[tile_of(index), :], proj_ref[...])

    def normalize(index):
        rows = tile_of(index)
        total = sum_ref[...] + vec_ref[BIAS_P : BIAS_P + 1, :]
        middle = x_ref[rows, :].astype(F32) + BRANCH * total
        middle_ref[rows, :] = middle
        normed, _ = norm_parts(middle)
        low = (normed * vec_ref[GAIN2 : GAIN2 + 1, :] + vec_ref[SHIFT2 : SHIFT2 + 1, :]).astype(BF)
        c_ref[rows, :] = low
        ct_ref[:, rows] = low.T

    sum_ref[...] = branch(0)

    @pl.loop(0, count - 1)
    def _(index):
        normalize(index)
        sum_ref[...] = branch(index + 1)
        tile_copy(middle_ref, middle_out, middle_sems, index).start()

    normalize(count - 1)
    middle_tiles = tiles(middle_ref, middle_out, middle_sems)
    middle_tiles[-1].start()
    for pair in range(width // 128):
        wait_all(results(pair))
    wait_all(qkv_tiles + middle_tiles)


def forward_scratch(slots, width):
    return [
        pltpu.VMEM((slots, width), BF),
        pltpu.VMEM((width, slots), F32),
        pltpu.VMEM((2, slots, 128), BF),
        pltpu.VMEM((2, slots, 128), BF),
        pltpu.VMEM((128, slots), BF),
        pltpu.VMEM((2, slots, TILE), F32),
        pltpu.VMEM((2, slots, TILE), BF),
    ]


def attention_forward_own(length, qkv):
    slots = qkv.shape[0]
    width = qkv.shape[1] // 3
    heads = width // 64
    return call(
        forward_own_kernel,
        "attention_forward_own",
        1,
        [(length, SMEM), (qkv, KEPT)],
        [
            ((heads, slots), F32, whole((heads, slots))),
            ((slots, width), BF, HBM),
            ((width, slots), F32, HBM),
            ((slots, 3 * width), BF, HBM),
        ],
        [*forward_scratch(slots, width), pltpu.SemaphoreType.DMA((3, width // 128))],
        6 * slots * slots * width,
    )


def attention_forward_other(bits, length, other_vec, vec, a_low, x, ctx, proj, pieces, proj_pieces):
    slots, model = x.shape
    width = ctx.shape[1]
    heads = width // 64
    tokens = slots // TILE
    dma = pltpu.SemaphoreType.DMA
    ins = [(bits, SMEM), (length, SMEM)]
    ins += [(value, whole(value.shape)) for value in (other_vec, vec)]
    ins += [(value, HBM) for value in (a_low, x, ctx, proj, *pieces, *proj_pieces)]
    return call(
        forward_other_kernel,
        "attention_forward_other",
        1,
        ins,
        [
            ((heads, slots), F32, whole((heads, slots))),
            ((slots, model), BF, KEPT),
            ((model, slots), BF, KEPT),
            ((slots, model), F32, HBM),
            ((width, slots), F32, HBM),
            ((slots, 3 * width), BF, HBM),
        ],
        [
            pltpu.VMEM((slots, 2 * width), BF),
            *forward_scratch(slots, width)[1:],
            pltpu.VMEM((slots, 3 * width), BF),
            pltpu.VMEM((slots, model), BF),
            pltpu.VMEM((model, 3 * width), BF),
            pltpu.VMEM((slots, model), BF),
            pltpu.VMEM((2 * width, model), BF),
            pltpu.VMEM((slots, model), F32),
            pltpu.VMEM((TILE, model), F32),
            dma((tokens,)),
            dma((12,)),
            dma((tokens,)),
            dma((width // 128,)),
            dma((3,)),
            dma((2,)),
            dma((tokens,)),
        ],
        6 * slots * slots * width + 10 * slots * model * width,
        28,
    )


def mlp_step(c_ref, g_ref, fc, ow, bias):
    hidden = dot(c_ref[...], fc) + bias
    square = hidden * hidden
    tanh = jnp.tanh(hidden * (GELU + GELU * CUBIC * square))
    share = 0.5 + 0.5 * tanh
    value = hidden * share
    slope = share + value * (1.0 - share) * (2.0 * GELU + 6.0 * GELU * CUBIC * square)
    return value.astype(BF), (dot_nt(g_ref[...], ow) * slope).astype(BF)


def unit_bias(vec_ref, base, bias_ref):
    model = vec_ref.shape[1]
    for row in range(bias_ref.shape[1] // model):
        columns = slice(row * model, (row + 1) * model)
        bias_ref[:, columns] = vec_ref[base + row : base + row + 1, :]


def mlp_own_kernel(
    steps,
    block,
    bits_ref,
    c_ref,
    g_ref,
    ct_ref,
    gt_ref,
    vec_ref,
    fc_ref,
    ow_ref,
    gc_out,
    act_ref,
    fc_kept_ref,
    out_kept_ref,
    fc_sent_ref,
    out_sent_ref,
    db_ref,
    gc_ref,
    gc_low_ref,
    bias_ref,
    gh_ref,
    dw_ref,
    sem,
):
    step = pl.program_id(0)

    @pl.when(step == 0)
    def _():
        unit_bias(vec_ref, BIAS_FC, bias_ref)
        clear(gc_ref)

    lanes = pl.ds(pl.multiple_of(step * HIDDEN, HIDDEN), HIDDEN)
    act, gh = mlp_step(c_ref, g_ref, fc_ref[...], ow_ref[...], bias_ref[:, lanes])
    act_ref[...] = act
    gh_ref[...] = gh
    db_ref[...] = jnp.sum(gh.astype(F32), 0, keepdims=True)
    gc_ref[...] += dot_nt(gh, fc_ref[...])
    results = [pltpu.make_async_copy(gc_low_ref, gc_out, sem)]

    @pl.when(step == steps - 1)
    def _():
        gc_low_ref[...] = gc_ref[...].astype(BF)
        start_all(results)

    dw_ref[0] = dot(ct_ref[...], gh_ref[...]).astype(BF)
    halves(dw_ref.at[0], bits_ref[2], block, fc_kept_ref, fc_sent_ref.at[:, lanes])
    dw_ref[1] = dot(gt_ref[...], act_ref[...]).astype(BF)
    halves(dw_ref.at[1], bits_ref[2], block, out_kept_ref, out_sent_ref.at[:, lanes])

    @pl.when(step == steps - 1)
    def _():
        wait_all(results)


def feed_forward_own(bits, block, c_low, grad_mlp, c_turned, grad_turned, vec, fc, ow):
    slots, model = c_low.shape
    units = fc.shape[1]
    steps = units // HIDDEN
    half = column_tile(model // 2, HIDDEN)
    return call(
        functools.partial(mlp_own_kernel, steps, block),
        "feed_forward_own",
        steps,
        [(bits, SMEM)]
        + [(value, KEPT) for value in (c_low, grad_mlp, c_turned, grad_turned)]
        + [
            (vec, whole(vec.shape)),
            (fc, column_tile(model, HIDDEN)),
            (ow, pl.BlockSpec((HIDDEN, model), lambda i: (i, 0))),
        ],
        [((slots, model), BF, HBM), ((slots, units), BF, column_tile(slots, HIDDEN))]
        + [((model // 2, units), BF, half)] * 2
        + [((model // 2, units), BF, KEPT)] * 2
        + [((1, units), F32, column_tile(1, HIDDEN))],
        [
            pltpu.VMEM((slots, model), F32),
            pltpu.VMEM((slots, model), BF),
            pltpu.VMEM((1, units), F32),
            pltpu.VMEM((slots, HIDDEN), BF),
            pltpu.VMEM((2, model, HIDDEN), BF),
            pltpu.SemaphoreType.DMA,
        ],
        10 * slots * model * units,
        32,
    )


def mlp_other_kernel(
    steps,
    bits_ref,
    length_ref,
    c_ref,
    g_ref,
    other_vec_ref,
    vec_ref,
    gc0_hbm,
    middle_hbm,
    cot_hbm,
    proj0_hbm,
    fc_kept_hbm,
    out_kept_hbm,
    *rest,
):
    fc_pieces, out_pieces, proj_pieces, rest = rest[:4], rest[4:8], rest[8:10], rest[10:]
    do0_ref, fc_kept_ref, out_kept_ref, sums_ref, act_ref, gmid_out, ga_out, do1_out, *rest = rest
    gc_ref, bias_ref, fc_ref, ow_ref, *rest = rest
    late_refs, (gmid_ref, ga_ref, low_ref, do1_ref, proj1_ref, *rest) = rest[:4], rest[4:]
    sems, late_sems, proj_sems, out_sems = rest
    step = pl.program_id(0)
    slots, model = c_ref.shape
    copies = fetch_rows(fc_pieces, bits_ref[1], fc_ref, sems.at[0])
    copies += fetch_rows(out_pieces, bits_ref[4], ow_ref, sems.at[1])
    late = [
        pltpu.make_async_copy(source, target, late_sems.at[index])
        for index, (source, target) in enumerate(
            zip(
                (gc0_hbm, middle_hbm, cot_hbm, proj0_hbm, fc_kept_hbm, out_kept_hbm),
                (*late_refs, fc_kept_ref, out_kept_ref),
            )
        )
    ]
    half = proj1_ref.shape[0] // 2
    halves_in = [piece.at[:half, :] for piece in proj_pieces]
    late += fetch_rows(halves_in, bits_ref[0], proj1_ref, proj_sems)

    @pl.when(step == 0)
    def _():
        start_all(copies)
        unit_bias(other_vec_ref, 1, bias_ref)
        clear(gc_ref)
        wait_all(copies)
        start_all(late)

    lanes = pl.ds(pl.multiple_of(step * HIDDEN, HIDDEN), HIDDEN)
    act, gh = mlp_step(c_ref, g_ref, fc_ref[:, lanes], ow_ref[lanes, :], bias_ref[:, lanes])
    act_ref[...] = act
    gc_ref[...] += dot_nt(gh, fc_ref[:, lanes])

    @pl.when(step == steps - 1)
    def _():
        wait_all(late)
        gc0_ref, middle_ref, cot_ref, proj0_ref = late_refs
        pairs = ((gmid_ref, gmid_out), (ga_ref, ga_out), (do1_ref, do1_out))
        outs = [(*pair, out_sems.at[index]) for index, pair in enumerate(pairs)]
        count = slots // TILE
        sums_ref[...] = jnp.zeros(sums_ref.shape, F32)

        def elementwise(index):
            rows = tile_of(index)
            grad_c = gc_ref[rows, :].astype(BF).astype(F32) + gc0_ref[rows, :].astype(F32)
            normed, inverse = norm_parts(middle_ref[rows, :])
            top = grad_top_of(cot_ref[rows, :], length_ref[0], index * TILE)
            grad_middle = top + norm_back(grad_c, normed, inverse, vec_ref[GAIN2 : GAIN2 + 1, :])
            sums_ref[0:1, :] += jnp.sum(grad_c * normed, 0, keepdims=True)
            sums_ref[1:2, :] += jnp.sum(grad_c, 0, keepdims=True)
            sums_ref[2:3, :] += BRANCH * jnp.sum(grad_middle, 0, keepdims=True)
            gmid_ref[rows, :] = grad_middle
            low = (BRANCH * grad_middle).astype(BF)
            ga_ref[rows, :] = low
            low_ref[...] = low

        def project_back(index):
            rows = tile_of(index)
            do0_ref[rows, :] = dot_nt(low_ref[...], proj0_ref[...]).astype(BF)
            do1_ref[rows, :] = dot_nt(low_ref[...], proj1_ref[...]).astype(BF)

        elementwise(0)

        @pl.loop(0, count - 1)
        def _(index):
            project_back(index)
            elementwise(index + 1)
            for group in outs:
                tile_copy(*group, index).start()

        project_back(count - 1)
        for group in outs:
            tile_copy(*group, count - 1).start()
        for group in outs:
            wait_all(tiles(*group))


def feed_forward_other(
    bits, length, c_low, grad_mlp, other_vec, vec, grad_c, middle, cot, proj, kept, fc, ow, proj_pieces
):
    slots, model = c_low.shape
    width = proj.shape[0]
    units = fc[0].shape[1]
    steps = units // HIDDEN
    tokens = slots // TILE
    dma = pltpu.SemaphoreType.DMA
    return call(
        functools.partial(mlp_other_kernel, steps),
        "feed_forward_other",
        steps,
        [(bits, SMEM), (length, SMEM), (c_low, KEPT), (grad_mlp, KEPT)]
        + [(value, whole(value.shape)) for value in (other_vec, vec)]
        + [(value, HBM) for value in (grad_c, middle, cot, proj, *kept, *fc, *ow, *proj_pieces)],
        [
            ((slots, width), BF, KEPT),
            *[(value.shape, BF, KEPT) for value in kept],
            ((3, model), F32, whole((3, model))),
            ((slots, units), BF, column_tile(slots, HIDDEN)),
            ((slots, model), F32, HBM),
            ((slots, model), BF, HBM),
            ((slots, width), BF, HBM),
        ],
        [
            pltpu.VMEM((slots, model), F32),
            pltpu.VMEM((1, units), F32),
            pltpu.VMEM((model, units), BF),
            pltpu.VMEM((units, model), BF),
            pltpu.VMEM((slots, model), BF),
            pltpu.VMEM((slots, model), F32),
            pltpu.VMEM((slots, model), BF),
            pltpu.VMEM((width, model), BF),
            pltpu.VMEM((slots, model), F32),
            pltpu.VMEM((slots, model), BF),
            pltpu.VMEM((TILE, model), BF),
            pltpu.VMEM((slots, width), BF),
            pltpu.VMEM((width, model), BF),
            dma((2, 4)),
            dma((6,)),
            dma((2,)),
            dma((3, tokens)),
        ],
        6 * slots * model * units + 4 * slots * model * width,
        42,
    )


def output_kernel(bits_ref, vec_ref, act0_hbm, act1_hbm, middle_hbm, ow_hbm, *rest):
    pieces, (y_out, act_ref, ow_ref, middle_ref, y_ref, act_sems, sems, m_sem, y_sems) = (
        rest[:4],
        rest[4:],
    )
    slots, units = act0_hbm.shape
    own = pl.ds(pl.multiple_of(bits_ref[3] * units, 128), units)
    other = pl.ds(pl.multiple_of((1 - bits_ref[3]) * units, 128), units)
    copies = fetch_rows([ow_hbm], 0, ow_ref.at[own, :], sems.at[0])
    copies += fetch_rows(pieces, bits_ref[4], ow_ref.at[other, :], sems.at[1])
    acts = []
    for index in range(slots // TILE):
        rows = slice(index * TILE, (index + 1) * TILE)
        for group, (source, lanes) in enumerate(((act0_hbm, own), (act1_hbm, other))):
            acts.append(
                pltpu.make_async_copy(
                    source.at[rows, :], act_ref.at[rows, lanes], act_sems.at[group, index]
                )
            )
    middle_in = tiles(middle_hbm, middle_ref, m_sem)
    start_all(acts[:2] + copies)
    for index, copy in enumerate(middle_in):
        copy.start()
        start_all(acts[2 * index + 2 : 2 * index + 4])
    wait_all(copies)

    @pl.loop(0, slots // TILE)
    def _(index):
        rows = tile_of(index)
        for group, (source, lanes) in enumerate(((act0_hbm, own), (act1_hbm, other))):
            pltpu.make_async_copy(
                source.at[rows, :], act_ref.at[rows, lanes], act_sems.at[group, index]
            ).wait()
        tile_copy(middle_hbm, middle_ref, m_sem, index).wait()
        mlp = dot(act_ref[rows, :], ow_ref[...]) + vec_ref[BIAS_O : BIAS_O + 1, :]
        y_ref[rows, :] = (middle_ref[rows, :] + BRANCH * mlp).astype(BF)
        tile_copy(y_ref, y_out, y_sems, index).start()

    wait_all(tiles(y_ref, y_out, y_sems))


def block_result(bits, vec, act0, act1, middle, ow, pieces):
    slots, model = middle.shape
    units = act0.shape[1]
    tokens = slots // TILE
    dma = pltpu.SemaphoreType.DMA
    return call(
        output_kernel,
        "output",
        1,
        [(bits, SMEM), (vec, whole(vec.shape))]
        + [(value, HBM) for value in (act0, act1, middle, ow, *pieces)],
        [((slots, model), BF, HBM)],
        [
            pltpu.VMEM((slots, 2 * units), BF),
            pltpu.VMEM((2 * units, model), BF),
            pltpu.VMEM((slots, model), F32),
            pltpu.VMEM((slots, model), BF),
            dma((2, tokens)),
            dma((2, 4)),
            dma((tokens,)),
            dma((tokens,)),
        ],
        4 * slots * model * units,
        24,
    )[0]


def backward_pairs(length, qkv_ref, do_ref, ctxt_ref, lse_ref, d_ref, scratch, sources):
    (
        ka_ref,
        qa_ref,
        do_mask_ref,
        kt_ref,
        qt_ref,
        dot_ref,
        delta_ref,
        dqt_ref,
        dkt_ref,
        dvt_ref,
        score_ref,
        grad_ref,
        prob_ref,
        slope_ref,
    ) = scratch
    slots, width = do_ref.shape
    causal = causal_fill()
    blocks = slots // TILE

    @pl.loop(0, width // 128)
    def _(pair):
        lanes = pair_lanes(pair)
        wait_all(sources(pair))
        keys_low = qkv_ref[:, pair_lanes(pair, width)]
        queries = qkv_ref[:, lanes]
        masked_pair(keys_low, queries, length, ka_ref, qa_ref)
        grads = do_ref[:, lanes]
        lane = lax.broadcasted_iota(jnp.int32, (slots, 128), 1)
        for half in (0, 1):
            do_mask_ref[half] = jnp.where(lane // 64 == half, grads.astype(F32), 0.0).astype(BF)
        kt_ref[...] = keys_low.T
        qt_ref[...] = queries.T
        turned = grads.T
        dot_ref[...] = turned
        product = turned.astype(F32) * ctxt_ref[lanes, :]
        for half in (0, 1):
            delta_ref[half : half + 1, :] = jnp.sum(
                product[64 * half : 64 * half + 64], 0, keepdims=True
            )
        items = [(block, half) for block in reversed(range(blocks)) for half in (0, 1)]

        def score(item):
            block, half = items[item]
            extent = (block + 1) * TILE
            columns = slice(block * TILE, extent)
            score_ref[item % 2, :extent, :] = dot_nt(
                ka_ref[half, :extent, :], qa_ref[half, columns, :]
            )
            grad_ref[item % 2, :extent, :] = dot_nt(
                qkv_ref[:extent, pair_lanes(pair, 2 * width)], do_mask_ref[half, columns, :]
            )

        def softmax(item):
            block, half = items[item]
            columns = slice(block * TILE, (block + 1) * TILE)
            lse = lse_ref[pl.ds(pair * 2 + half, 1), columns]
            delta = delta_ref[half : half + 1, columns]
            for inner in range(block + 1):
                keys = slice(inner * TILE, (inner + 1) * TILE)
                scores = score_ref[item % 2, keys, :]
                if inner == block:
                    scores = scores + causal
                prob = jnp.exp(scores - lse)
                slope_ref[item % 2, keys, :] = (
                    prob * (grad_ref[item % 2, keys, :] - delta)
                ).astype(BF)
                prob_ref[item % 2, keys, :] = prob.astype(BF)

        def gradients(item):
            block, half = items[item]
            extent = (block + 1) * TILE
            columns = slice(block * TILE, extent)
            rows = slice(64 * half, 64 * half + 64)
            dv_part = dot_nt(dot_ref[rows, columns], prob_ref[item % 2, :extent, :])
            dk_part = dot_nt(qt_ref[rows, columns], slope_ref[item % 2, :extent, :])
            if block == blocks - 1:
                dvt_ref[rows, :extent] = dv_part
                dkt_ref[rows, :extent] = dk_part
            else:
                dvt_ref[rows, :extent] += dv_part
                dkt_ref[rows, :extent] += dk_part
            dqt_ref[rows, columns] = dot(kt_ref[rows, :extent], slope_ref[item % 2, :extent, :])

        count_items = len(items)
        score(0)
        for item in range(count_items + 1):
            if item + 1 < count_items:
                score(item + 1)
            if item >= 1:
                gradients(item - 1)
            if item < count_items:
                softmax(item)
        d_ref[:, lanes] = (dqt_ref[...] * 0.125).astype(BF).T
        d_ref[:, pair_lanes(pair, width)] = dkt_ref[...].astype(BF).T
        d_ref[:, pair_lanes(pair, 2 * width)] = dvt_ref[...].astype(BF).T


def pair_sources(pair, width, qkv, ctxt, do, sems):
    lanes = pair_lanes(pair)
    moves = []
    for matrix in range(3):
        columns = pair_lanes(pair, matrix * width)
        moves.append((qkv[0].at[:, columns], qkv[1].at[:, columns]))
    moves.append((ctxt[0].at[lanes, :], ctxt[1].at[lanes, :]))
    if do is not None:
        moves.append((do[0].at[:, lanes], do[1].at[:, lanes]))
    return [
        pltpu.make_async_copy(source, target, sems.at[index, pair])
        for index, (source, target) in enumerate(moves)
    ]


def backward_other_kernel(
    length_ref, lse_ref, qkv_hbm, ctxt_hbm, do_hbm, d_ref, qkv_ref, ctxt_ref, do_ref, *rest
):
    scratch, sems = rest[:14], rest[14]
    width = do_ref.shape[1]
    sources = lambda pair: pair_sources(
        pair, width, (qkv_hbm, qkv_ref), (ctxt_hbm, ctxt_ref), (do_hbm, do_ref), sems
    )
    for pair in range(width // 128):
        start_all(sources(pair))
    backward_pairs(length_ref[0], qkv_ref, do_ref, ctxt_ref, lse_ref, d_ref, scratch, sources)


def lane_sums(value):
    total = value[:, :128]
    for start in range(128, value.shape[1], 128):
        total = total + value[:, start : start + 128]
    return jnp.sum(total.T, 0, keepdims=True)


def backward_own_kernel(
    block,
    bits_ref,
    length_ref,
    lse_ref,
    vec_ref,
    ob_ref,
    sums_ref,
    db_ref,
    do_ref,
    qkv_hbm,
    ctxt_hbm,
    at_hbm,
    gat_hbm,
    w_hbm,
    lead_ref,
    vectors_ref,
    d_out,
    first_kept_out,
    first_sent_out,
    second_kept_out,
    second_sent_out,
    qkv_ref,
    ctxt_ref,
    *rest,
):
    scratch, rest = rest[:14], rest[14:]
    d_ref, at_ref, gat_ref, w_ref, dw_ref, half_ref, total_ref, sems, w_sems, late_sems, out_sems = rest
    width = do_ref.shape[1]
    model = at_ref.shape[0]
    sources = lambda pair: pair_sources(
        pair, width, (qkv_hbm, qkv_ref), (ctxt_hbm, ctxt_ref), None, sems
    )
    for pair in range(width // 128):
        start_all(sources(pair))
    late = fetch_rows([w_hbm], 0, w_ref, w_sems)
    late += [
        pltpu.make_async_copy(at_hbm, at_ref, late_sems.at[0]),
        pltpu.make_async_copy(gat_hbm, gat_ref, late_sems.at[1]),
    ]
    start_all(late)
    backward_pairs(length_ref[0], qkv_ref, do_ref, ctxt_ref, lse_ref, d_ref, scratch, sources)
    results = [pltpu.make_async_copy(d_ref, d_out, out_sems.at[4])]
    results[0].start()
    lead_ref[...] = jnp.zeros(lead_ref.shape, F32)
    wait_all(late)
    side = bits_ref[2]
    outs = (first_kept_out, first_sent_out, second_kept_out, second_sent_out)

    def give(index):
        halves(dw_ref.at[index], side, block, half_ref.at[2 * index], half_ref.at[2 * index + 1])
        for part in (2 * index, 2 * index + 1):
            results.append(pltpu.make_async_copy(half_ref.at[part], outs[part], out_sems.at[part]))
            results[-1].start()

    low = ctxt_ref[...].astype(BF)
    dw_ref[1, :, width:] = dot(low, gat_ref[...]).T.astype(BF)
    total_ref[...] = jnp.zeros(total_ref.shape, F32)

    @pl.loop(0, d_ref.shape[0] // TILE)
    def _(index):
        total_ref[...] += jnp.sum(d_ref[tile_of(index), :].astype(F32), 0, keepdims=True)

    sums = total_ref[...]

    @pl.loop(0, model // TILE)
    def _(index):
        rows = tile_of(index)
        part = dot(at_ref[rows, :], d_ref[...])
        dw_ref[0, rows, :] = part[:, :model].astype(BF)
        dw_ref[1, rows, :width] = part[:, model:].astype(BF)
        weight = w_ref[rows, :].astype(F32)
        lead_ref[0:1, rows] = lane_sums(part * weight)
        lead_ref[1:2, rows] = lane_sums(weight * sums)

    give(0)
    give(1)
    scaled, shift = lead_ref[0:1, :], lead_ref[1:2, :]
    gain1, shift1 = vec_ref[GAIN1 : GAIN1 + 1, :], vec_ref[SHIFT1 : SHIFT1 + 1, :]
    vectors_ref[...] = jnp.zeros(vectors_ref.shape, F32)
    lead_ref[0:1, :] = (scaled - shift1 * shift) / gain1
    vectors_ref[2:3, :] = ob_ref[...]
    vectors_ref[3:6, :] = sums_ref[...]
    for index in range(2):
        vectors_ref[6 + index : 7 + index, :] = db_ref[:, index * model : (index + 1) * model]
    vectors_ref[8:9, :width] = sums[:, :width]
    vectors_ref[8:9, width:] = sums[:, 2 * width :]
    wait_all(results)


def backward_scratch(slots):
    return [
        pltpu.VMEM((2, slots, 128), BF),
        pltpu.VMEM((2, slots, 128), BF),
        pltpu.VMEM((2, slots, 128), BF),
        pltpu.VMEM((128, slots), BF),
        pltpu.VMEM((128, slots), BF),
        pltpu.VMEM((128, slots), BF),
        pltpu.VMEM((2, slots), F32),
        pltpu.VMEM((128, slots), F32),
        pltpu.VMEM((128, slots), F32),
        pltpu.VMEM((128, slots), F32),
        pltpu.VMEM((2, slots, TILE), F32),
        pltpu.VMEM((2, slots, TILE), F32),
        pltpu.VMEM((2, slots, TILE), BF),
        pltpu.VMEM((2, slots, TILE), BF),
    ]


def attention_backward_other(length, lse, qkv, ctxt, do):
    slots, width = do.shape
    ins = [(length, SMEM), (lse, whole(lse.shape)), (qkv, HBM), (ctxt, HBM), (do, HBM)]
    return call(
        backward_other_kernel,
        "attention_backward_other",
        1,
        ins,
        [((slots, 3 * width), BF, KEPT)],
        [
            pltpu.VMEM((slots, 3 * width), BF),
            pltpu.VMEM((width, slots), F32),
            pltpu.VMEM((slots, width), BF),
            *backward_scratch(slots),
            pltpu.SemaphoreType.DMA((5, width // 128)),
        ],
        9 * slots * slots * width,
        18,
    )[0]


def attention_backward_own(bits, length, block, lse, vec, sums, do, qkv, ctxt, at, gat, weight):
    slots, width = do.shape
    model = at.shape[0]
    dma = pltpu.SemaphoreType.DMA
    ins = [(bits, SMEM), (length, SMEM)]
    ins += [(value, whole(value.shape)) for value in (lse, vec, *sums)]
    ins += [(do, KEPT)] + [(value, HBM) for value in (qkv, ctxt, at, gat, weight)]
    outs = [((rows, model), F32, KEPT) for rows in (8, 16)] + [((slots, 3 * width), BF, HBM)]
    outs += [((model // 2, model), BF, HBM)] * 4
    return call(
        functools.partial(backward_own_kernel, block),
        "attention_backward_own",
        1,
        ins,
        outs,
        [
            pltpu.VMEM((slots, 3 * width), BF),
            pltpu.VMEM((width, slots), F32),
            *backward_scratch(slots),
            pltpu.VMEM((slots, 3 * width), BF),
            pltpu.VMEM((model, slots), BF),
            pltpu.VMEM((slots, model), BF),
            pltpu.VMEM((model, 3 * width), BF),
            pltpu.VMEM((2, model, model), BF),
            pltpu.VMEM((4, model // 2, model), BF),
            pltpu.VMEM((1, 3 * width), F32),
            dma((4, width // 128)),
            dma((3,)),
            dma((2,)),
            dma((5,)),
        ],
        9 * slots * slots * width + 8 * slots * model * width,
        32,
    )


def final_kernel(bits_ref, vec_ref, d1_ref, d0_hbm, x_hbm, gmid_hbm, w_hbm, *rest):
    pieces, (gin_out, d_ref, x_ref, gmid_ref, w_ref, gin_ref, product_ref, *rest) = (
        rest[:4],
        rest[4:],
    )
    w_sems, d_sems, x_sems, gmid_sems, gin_sems = rest
    total = d1_ref.shape[1]
    own = pl.ds(pl.multiple_of(bits_ref[3] * total, 128), total)
    other = pl.ds(pl.multiple_of((1 - bits_ref[3]) * total, 128), total)
    copies = fetch_rows([w_hbm], 0, w_ref.at[:, own], w_sems.at[0])
    copies += fetch_rows(pieces, bits_ref[1], w_ref.at[:, other], w_sems.at[1])
    d_in = tiles(d0_hbm, d_ref.at[:, own], d_sems)
    x_in = tiles(x_hbm, x_ref, x_sems)
    gmid_in = tiles(gmid_hbm, gmid_ref, gmid_sems)
    gin_tiles = tiles(gin_ref, gin_out, gin_sems)
    d_in[0].start()
    start_all(copies)
    start_all(d_in[1:] + x_in + gmid_in)
    count = len(d_in)

    @pl.loop(0, count)
    def _(index):
        d_ref[tile_of(index), other] = d1_ref[tile_of(index), :]

    def product(index):
        return dot_nt(d_ref[tile_of(index), :], w_ref[...])

    def norm(index):
        rows = tile_of(index)
        normed, inverse = norm_parts(x_ref[rows, :].astype(F32))
        back = norm_back(product_ref[...], normed, inverse, vec_ref[GAIN1 : GAIN1 + 1, :])
        gin_ref[rows, :] = gmid_ref[rows, :] + back

    wait_all(copies + d_in)
    product_ref[...] = product(0)
    wait_all(x_in + gmid_in)

    @pl.loop(0, count - 1)
    def _(index):
        norm(index)
        product_ref[...] = product(index + 1)
        tile_copy(gin_ref, gin_out, gin_sems, index).start()

    norm(count - 1)
    gin_tiles[-1].start()
    wait_all(gin_tiles)


def gradient_of_input(bits, vec, d1, d0, x, gmid, weight, pieces):
    slots, model = x.shape
    total = d1.shape[1]
    tokens = slots // TILE
    dma = pltpu.SemaphoreType.DMA
    return call(
        final_kernel,
        "final",
        1,
        [(bits, SMEM), (vec, whole(vec.shape)), (d1, KEPT)]
        + [(value, HBM) for value in (d0, x, gmid, weight, *pieces)],
        [((slots, model), F32, HBM)],
        [
            pltpu.VMEM((slots, 2 * total), BF),
            pltpu.VMEM((slots, model), BF),
            pltpu.VMEM((slots, model), F32),
            pltpu.VMEM((model, 2 * total), BF),
            pltpu.VMEM((slots, model), F32),
            pltpu.VMEM((TILE, model), F32),
            dma((2, 12)),
            dma((tokens,)),
            dma((tokens,)),
            dma((tokens,)),
            dma((tokens,)),
        ],
        4 * slots * model * total,
        28,
    )[0]


def across(value):
    return lax.ppermute(value, "tensor", [(0, 1), (1, 0)])


def swap(value, bit):
    count = lax.axis_size("dp")
    return lax.ppermute(value, "dp", [(i, i ^ bit) for i in range(count)])


def tie(*values):
    return lax.optimization_barrier(values)


def pick(value, index, axis):
    return lax.dynamic_index_in_dim(value, index, axis, keepdims=False)


def split_rows(value, count):
    shape = value.shape
    return value.reshape(*shape[:-2], count, shape[-2] // count, shape[-1])


class Reduction:
    def __init__(self, kept, first_bit, order):
        self.order = order
        self.bits = [bit for bit in reversed(range(len(order) + 1)) if bit != first_bit]
        rows = kept.shape[0] >> len(self.bits)
        self.kept = kept.reshape(*[2] * len(self.bits), rows, kept.shape[1])

    def advance(self, got):
        got = got.reshape(self.kept.shape)
        self.bit = self.order.pop(0)
        axis = self.bits.index(self.bit)
        self.bits.remove(self.bit)
        side = (lax.axis_index("dp") >> self.bit) & 1

        def part(index):
            total = pick(self.kept, index, axis).astype(F32) + pick(got, index, axis).astype(F32)
            return total.astype(BF)

        sent = part(1 - side)
        self.kept = part(side)
        return sent.reshape(-1, sent.shape[-1])

    def finish(self, got):
        return self.kept.astype(F32) + got.reshape(self.kept.shape).astype(F32)


def local(
    block_input,
    first_gain,
    first_shift,
    qkv_weight,
    qv_bias,
    proj_weight,
    proj_bias,
    second_gain,
    second_shift,
    fc_weight,
    fc_bias,
    out_weight,
    out_bias,
    cotangent,
    lengths,
):
    slots, model = block_input.shape
    width = qkv_weight.shape[2]
    units = fc_weight.shape[1]
    shards = lax.axis_size("dp")
    levels = shards.bit_length() - 1
    share = model // shards
    first_bit = next(bit for bit in range(levels) if (share << bit) % 16 == 0)
    block = share << first_bit
    later = [bit for bit in range(levels) if bit != first_bit]
    order_a = list(later)
    order_b = [later[1], later[0]] + later[2:]
    place = lax.axis_index("dp")
    quarter = jnp.bitwise_and(place, 3)
    one_bit = jnp.bitwise_and(place, 1)
    bits = jnp.stack(
        [
            one_bit,
            quarter,
            (place >> first_bit) & 1,
            lax.axis_index("tensor"),
            ((place >> 2) & 1) * 2 + one_bit,
        ]
    ).astype(jnp.int32)
    length = lengths.astype(jnp.int32)

    qkv_mine = across(pick(split_rows(qkv_weight, 4), quarter, 1))
    vectors = (first_gain, first_shift, proj_bias, second_gain, second_shift, out_bias)
    (
        vec,
        qkv0,
        grad_mlp,
        grad_mlp_turned,
        grad_out_bias,
        a_low,
        a_turned,
        proj_send,
        fc_send,
        out_send,
    ) = project(
        bits,
        length,
        block_input,
        cotangent,
        (*vectors, qv_bias, fc_bias),
        qkv_weight,
        proj_weight,
        fc_weight,
        out_weight,
    )

    qkv_mine, qkv0, proj_send, fc_send = tie(qkv_mine, qkv0, proj_send, fc_send)
    qkv_side = swap(qkv_mine, 2)
    qkv_core = swap(qkv_mine, 1)
    proj_got = across(proj_send)
    fc_mine = across(fc_send)
    lse0, ctx0, ctxt0, qkv0 = attention_forward_own(length, qkv0)

    qkv_side, qkv_core, proj_got, ctx0, out_send = tie(
        qkv_side, qkv_core, proj_got, ctx0, out_send
    )
    half_rows = width // 2
    parts = proj_got[half_rows : half_rows + 24].astype(F32).reshape(3, 8, model)
    other_vec = (parts[0] + parts[1]) + parts[2]
    proj_other = [proj_got, swap(proj_got, 1)]
    qkv_other = [qkv_mine, qkv_core, qkv_side, swap(qkv_side, 1)]
    out_mine = across(out_send)
    lse1, c_low, c_turned, middle, ctxt1, qkv1 = attention_forward_other(
        bits,
        length,
        other_vec,
        vec,
        a_low,
        block_input,
        ctx0,
        proj_weight,
        qkv_other,
        proj_other,
    )

    c_low, fc_mine, out_mine = tie(c_low, fc_mine, out_mine)
    fc_side = swap(fc_mine, 2)
    fc_core = swap(fc_mine, 1)
    out_side = swap(out_mine, 4)
    out_core = swap(out_mine, 1)
    gc0, act0, fc_kept, out_kept, fc_sent, out_sent, grad_fc_bias = feed_forward_own(
        bits, block, c_low, grad_mlp, c_turned, grad_mlp_turned, vec, fc_weight, out_weight
    )

    fc_sent, out_sent, fc_side, fc_core, out_side, out_core = tie(
        fc_sent, out_sent, fc_side, fc_core, out_side, out_core
    )
    fc_other = [fc_mine, fc_core, fc_side, swap(fc_side, 1)]
    out_other = [out_mine, out_core, out_side, swap(out_side, 1)]
    fc_got = swap(fc_sent, 1 << first_bit)
    out_got = swap(out_sent, 1 << first_bit)
    do0, fc_kept, out_kept, sums2, act1, grad_middle, grad_attn, do1 = feed_forward_other(
        bits,
        length,
        c_low,
        grad_mlp,
        other_vec,
        vec,
        gc0,
        middle,
        cotangent,
        proj_weight,
        (fc_kept, out_kept),
        fc_other,
        out_other,
        proj_other,
    )

    fc_sum = Reduction(fc_kept, first_bit, list(order_a))
    out_sum = Reduction(out_kept, first_bit, list(order_b))
    do0, fc_got, out_got = tie(do0, fc_got, out_got)
    fc_sent = fc_sum.advance(fc_got)
    out_sent = out_sum.advance(out_got)
    do0, fc_sent, out_sent = tie(do0, fc_sent, out_sent)
    fc_got = swap(fc_sent, 1 << fc_sum.bit)
    out_got = swap(out_sent, 1 << out_sum.bit)
    lead, vectors, d0, first_kept, first_sent, second_kept, second_sent = attention_backward_own(
        bits,
        length,
        block,
        lse0,
        vec,
        (grad_out_bias, sums2, grad_fc_bias),
        do0,
        qkv0,
        ctxt0,
        a_turned,
        grad_attn,
        qkv_weight,
    )

    first_sent, second_sent, lead, fc_got, out_got = tie(
        first_sent, second_sent, lead, fc_got, out_got
    )
    first_sum = Reduction(first_kept, first_bit, list(order_a))
    second_sum = Reduction(second_kept, first_bit, list(order_b))
    first_got = swap(first_sent, 1 << first_bit)
    second_got = swap(second_sent, 1 << first_bit)
    lead_got = across(lead)
    fc_sent = fc_sum.advance(fc_got)
    out_sent = out_sum.advance(out_got)
    fc_got = swap(fc_sent, 1 << fc_sum.bit)
    out_got = swap(out_sent, 1 << out_sum.bit)
    vectors = jnp.concatenate([(lead + lead_got)[:2], vectors[2:]], 0)

    def rounded(vectors):
        return lax.reduce_precision(vectors, 8, 7)

    def join(vectors, got):
        return rounded(vectors) + got.astype(F32)

    lines = vectors.shape[0]
    vectors = join(vectors, swap(vectors.astype(BF), 1 << first_bit))
    first_sent = jnp.concatenate([first_sum.advance(first_got), vectors.astype(BF)], 0)
    second_sent = second_sum.advance(second_got)
    first_sent, second_sent, qkv1 = tie(first_sent, second_sent, qkv1)
    first_got = swap(first_sent, 1 << first_sum.bit)
    second_got = swap(second_sent, 1 << second_sum.bit)
    d1 = attention_backward_other(length, lse1, qkv1, ctxt1, do1)

    d1, fc_got, out_got, first_got, second_got = tie(d1, fc_got, out_got, first_got, second_got)
    vectors = join(vectors, first_got[-lines:])
    first_sent = jnp.concatenate(
        [first_sum.advance(first_got[:-lines]), vectors.astype(BF)], 0
    )
    second_sent = second_sum.advance(second_got)
    rest_sent = jnp.concatenate([fc_sum.advance(fc_got), out_sum.advance(out_got)], 0)
    d1, first_sent, second_sent, rest_sent = tie(d1, first_sent, second_sent, rest_sent)
    first_got = swap(first_sent, 1 << first_sum.bit)
    second_got = swap(second_sent, 1 << second_sum.bit)
    rest_got = swap(rest_sent, 1 << fc_sum.bit)
    grad_input = gradient_of_input(
        bits, vec, d1, d0, block_input, grad_middle, qkv_weight, qkv_other
    )

    grad_input, first_got, second_got, act1 = tie(grad_input, first_got, second_got, act1)
    late = act1
    for level in range(3, levels):
        vectors = join(vectors, first_got[-lines:])
        sent = [first_sum.advance(first_got[:-lines]), second_sum.advance(second_got)]
        rows = sent[0].shape[0]
        sent = jnp.concatenate([*sent, vectors.astype(BF)], 0)
        sent, late = tie(sent, late)
        got = swap(sent, 1 << first_sum.bit)
        first_got = jnp.concatenate([got[:rows], got[2 * rows :]], 0)
        second_got = got[rows : 2 * rows]
        if fc_sum.order:
            rows = rest_got.shape[0] // 2
            rest_sent = [fc_sum.advance(rest_got[:rows]), out_sum.advance(rest_got[rows:])]
            rest_got = swap(jnp.concatenate(rest_sent, 0), 1 << fc_sum.bit)
    block_output = block_result(bits, vec, act0, late, middle, out_weight, out_other)
    vectors = join(vectors, first_got[-lines:])
    first = first_sum.finish(first_got[:-lines])
    second = second_sum.finish(second_got)
    rows = rest_got.shape[0] // 2
    grad_fc_weight = fc_sum.finish(rest_got[:rows])
    grad_out_weight = out_sum.finish(rest_got[rows:]).T
    grad_qkv_weight = jnp.stack([first[:, :width], first[:, width:], second[:, :width]])
    grad_proj_weight = second[:, width:].T
    return (
        block_output,
        grad_input,
        vectors[0],
        vectors[1],
        grad_qkv_weight,
        vectors[8].reshape(2, width),
        grad_proj_weight,
        vectors[5],
        vectors[3],
        vectors[4],
        grad_fc_weight,
        vectors[6:8].reshape(units),
        grad_out_weight,
        vectors[2],
    )


def solution(mesh):
    placed = (
        P("dp", None),
        P(),
        P(),
        P(None, None, "tensor"),
        P(None, "tensor"),
        P("tensor", None),
        P(),
        P(),
        P(),
        P(None, "tensor"),
        P("tensor"),
        P("tensor", None),
        P(),
        P("dp", None),
        P("dp"),
    )
    return jax.shard_map(
        local,
        mesh=mesh,
        in_specs=placed,
        out_specs=(
            P("dp", None),
            P("dp", None),
            P(),
            P(),
            P(None, "dp", "tensor"),
            P(None, "tensor"),
            P("tensor", "dp"),
            P(),
            P(),
            P(),
            P("dp", "tensor"),
            P("tensor"),
            P("tensor", "dp"),
            P(),
        ),
        check_vma=False,
    )
```

```python
import functools

import jax
import jax.numpy as jnp
from jax import lax
from jax.experimental import pallas as pl
from jax.experimental.pallas import tpu as pltpu
from jax.sharding import PartitionSpec as P

EPSILON = 1e-05
BRANCH = 48 ** (-0.5)
GELU = 0.7978845608028654
CUBIC = 0.044715
FILL = -1e30
BF = jnp.bfloat16
F32 = jnp.float32
MIB = 1024 * 1024
TILE = 256
HIDDEN = 512
GAIN1, SHIFT1, BIAS_P, GAIN2, SHIFT2, BIAS_O = range(6)
BIAS_QV, BIAS_FC = 8, 9


def dot(left, right):
    return lax.dot_general(left, right, (((1,), (0,)), ((), ())), preferred_element_type=F32)


def dot_nt(left, right):
    return lax.dot_general(left, right, (((1,), (1,)), ((), ())), preferred_element_type=F32)


def norm_parts(values):
    row_mean = jnp.mean(values, -1, keepdims=True)
    centered = values - row_mean
    inverse = lax.rsqrt(jnp.mean(centered * centered, -1, keepdims=True) + EPSILON)
    return centered * inverse, inverse


def norm_back(grad_out, normed, inverse, gain):
    scaled = grad_out * gain
    inner = (
        scaled
        - jnp.mean(scaled, -1, keepdims=True)
        - normed * jnp.mean(scaled * normed, -1, keepdims=True)
    )
    return inverse * inner


def whole(shape):
    return pl.BlockSpec(shape, lambda *_: (0,) * len(shape))


def row_tile(columns):
    return pl.BlockSpec((TILE, columns), lambda i: (i, 0))


def column_tile(rows, size=TILE):
    return pl.BlockSpec((rows, size), lambda i: (0, i))


SMEM = pl.BlockSpec(memory_space=pltpu.SMEM)
HBM = pl.BlockSpec(memory_space=pl.ANY)
KEPT = pl.BlockSpec(memory_space=pltpu.VMEM)


def call(body, name, steps, ins, outs, scratch, flops, limit=12):
    args = []
    for array, spec in ins:
        if spec is KEPT:
            array = pltpu.with_memory_space_constraint(array, pltpu.VMEM)
        elif spec is not SMEM:
            array = pltpu.with_memory_space_constraint(array, pltpu.HBM)
        args.append(array)
    moved = sum(a.size * a.dtype.itemsize for a, spec in ins if spec is not KEPT)
    moved += sum(
        jax.ShapeDtypeStruct(shape, dtype).size * jnp.dtype(dtype).itemsize
        for shape, dtype, spec in outs
        if spec is not KEPT
    )
    return pl.pallas_call(
        body,
        name=name,
        grid=(steps,),
        out_shape=tuple(
            (pltpu.VMEM if spec is KEPT else pltpu.HBM)(shape, dtype) for shape, dtype, spec in outs
        ),
        in_specs=[spec for _, spec in ins],
        out_specs=tuple(spec for _, _, spec in outs),
        scratch_shapes=scratch,
        compiler_params=pltpu.CompilerParams(vmem_limit_bytes=limit * MIB),
        cost_estimate=pl.CostEstimate(flops=flops, bytes_accessed=moved, transcendentals=0),
    )(*args)


def tile_of(step):
    return pl.ds(pl.multiple_of(step * TILE, TILE), TILE)


def fetch_rows(pieces, turn, target, sems):
    copies = []
    for index, piece in enumerate(pieces):
        rows = piece.shape[-2]
        if len(pieces) > 1:
            place = jnp.bitwise_xor(jnp.int32(index), turn)
            where = pl.ds(pl.multiple_of(place * rows, 32), rows)
        else:
            where = slice(None)
        if len(piece.shape) == 2:
            copies.append(pltpu.make_async_copy(piece, target.at[where, :], sems.at[index]))
            continue
        width = piece.shape[2]
        for matrix in range(3):
            columns = slice(matrix * width, (matrix + 1) * width)
            copies.append(
                pltpu.make_async_copy(
                    piece.at[matrix], target.at[where, columns], sems.at[3 * index + matrix]
                )
            )
    return copies


def start_all(copies):
    for copy in copies:
        copy.start()


def wait_all(copies):
    for copy in copies:
        copy.wait()


def qkv_bias(biases, width):
    bias = jnp.concatenate(
        [biases[:, :width], jnp.zeros((1, width), F32), biases[:, width:]], axis=1
    )
    lane = lax.broadcasted_iota(jnp.int32, (1, 3 * width), 1)
    return bias, jnp.where(lane < width, 0.125, 1.0)


def tiles(source, target, sems, axis=0):
    copies = []
    for index in range(source.shape[axis] // TILE):
        part = slice(index * TILE, (index + 1) * TILE)
        view = (part, slice(None)) if axis == 0 else (slice(None), part)
        copies.append(pltpu.make_async_copy(source.at[view], target.at[view], sems.at[index]))
    return copies


def tile_copy(source, target, sems, index):
    rows = tile_of(index)
    return pltpu.make_async_copy(source.at[rows, :], target.at[rows, :], sems.at[index])


def clear(*refs):
    @pl.loop(0, refs[0].shape[0] // TILE)
    def _(index):
        for ref in refs:
            ref[tile_of(index), :] = jnp.zeros((TILE, ref.shape[1]), ref.dtype)


def halves(value_ref, side, block, kept_ref, sent_ref):
    @pl.loop(0, value_ref.shape[0] // (2 * block))
    def _(index):
        rows = pl.ds(pl.multiple_of(index * block, 16), block)
        first = 2 * block * index
        here = pl.ds(pl.multiple_of(first + block * side, 16), block)
        there = pl.ds(pl.multiple_of(first + block * (1 - side), 16), block)
        kept_ref[rows, :] = value_ref[here, :]
        sent_ref[rows, :] = value_ref[there, :]


def grad_top_of(cot, length, start):
    rows, model = cot.shape
    position = lax.broadcasted_iota(jnp.int32, (rows, 128), 0) + start
    valid = jnp.where(position < length, 1.0, 0.0)
    return cot.astype(F32) * jnp.concatenate([valid] * (model // 128), axis=1)


def project_kernel(
    bits_ref,
    x_hbm,
    gain1_ref,
    shift1_ref,
    bias_p_ref,
    gain2_ref,
    shift2_ref,
    bias_o_ref,
    qv_ref,
    fcb_ref,
    qkv_hbm,
    proj_hbm,
    fc_hbm,
    out_hbm,
    length_ref,
    cot_hbm,
    vec_ref,
    qkv_ref,
    gm_ref,
    gmt_ref,
    ob_ref,
    a_out,
    at_out,
    proj_out,
    fc_out,
    out_out,
    x_ref,
    w_ref,
    a_ref,
    at_ref,
    proj_ref,
    fc_ref,
    out_ref,
    cot_ref,
    low_ref,
    x_sems,
    w_sems,
    cot_sems,
    send_sems,
    a_sems,
    at_sems,
):
    x_in = tiles(x_hbm, x_ref, x_sems)
    x_in[0].start()
    w_in = fetch_rows([qkv_hbm], 0, w_ref, w_sems)
    start_all(w_in)
    start_all(x_in[1:])
    model = x_ref.shape[1]
    half, quarter, fourth = proj_hbm.shape[0] // 2, fc_hbm.shape[0] // 4, out_hbm.shape[0] // 4
    sends_in = []
    for index, (source, target, place, rows) in enumerate(
        (
            (proj_hbm, proj_ref.at[:half, :], bits_ref[0], half),
            (fc_hbm, fc_ref, bits_ref[1], quarter),
            (out_hbm, out_ref, bits_ref[4], fourth),
        )
    ):
        where = pl.ds(pl.multiple_of(place * rows, 32), rows)
        sends_in.append(pltpu.make_async_copy(source.at[where, :], target, send_sems.at[index]))
    start_all(sends_in)
    sends_out = [
        pltpu.make_async_copy(source, target, send_sems.at[3 + index])
        for index, (source, target) in enumerate(
            ((proj_ref, proj_out), (fc_ref, fc_out), (out_ref, out_out))
        )
    ]
    cot_in = tiles(cot_hbm, cot_ref, cot_sems)
    start_all(cot_in)
    vec_ref[...] = jnp.zeros(vec_ref.shape, F32)
    for index, ref in enumerate(
        (gain1_ref, shift1_ref, bias_p_ref, gain2_ref, shift2_ref, bias_o_ref)
    ):
        vec_ref[index : index + 1, :] = ref[...].reshape(1, model)
    width = qv_ref.shape[1]
    vec_ref[BIAS_QV : BIAS_QV + 1, :width] = qv_ref[0:1, :]
    vec_ref[BIAS_QV : BIAS_QV + 1, width:] = qv_ref[1:2, :]
    fcb = fcb_ref[...].reshape(1, fcb_ref.shape[0])
    for index in range(2):
        vec_ref[BIAS_FC + index : BIAS_FC + index + 1, :] = fcb[:, index * model : (index + 1) * model]
    value = vec_ref[8 * (BIAS_QV // 8) :, :]
    high = value.astype(BF)
    rest = value - high.astype(F32)
    mid = rest.astype(BF)
    low = (rest - mid.astype(F32)).astype(BF)
    lines = value.shape[0]
    for index, part in enumerate((high, mid, low)):
        proj_ref[half + index * lines : half + (index + 1) * lines, :] = part

    def normalize(index):
        rows = tile_of(index)
        normed, _ = norm_parts(x_ref[rows, :].astype(F32))
        low = normed * vec_ref[GAIN1 : GAIN1 + 1, :] + vec_ref[SHIFT1 : SHIFT1 + 1, :]
        low = low.astype(BF)
        low_ref[...] = low
        a_ref[rows, :] = low
        at_ref[:, rows] = low.T

    def gradient(index):
        rows = tile_of(index)
        top = grad_top_of(cot_ref[rows, :], length_ref[0], index * TILE)
        ob_ref[...] += BRANCH * jnp.sum(top, 0, keepdims=True)
        low = (BRANCH * top).astype(BF)
        gm_ref[rows, :] = low
        gmt_ref[:, rows] = low.T

    def multiply(index):
        qkv_ref[tile_of(index), :] = ((dot(low_ref[...], w_ref[...]) + bias) * scale).astype(BF)

    count = len(x_in)
    bias, scale = qkv_bias(vec_ref[BIAS_QV : BIAS_QV + 1, :], width)
    a_tiles = tiles(a_ref, a_out, a_sems)
    at_tiles = tiles(at_ref, at_out, at_sems, 1)
    ob_ref[...] = jnp.zeros(ob_ref.shape, F32)
    x_in[0].wait()
    normalize(0)
    wait_all(w_in + x_in[1:])

    @pl.loop(0, count - 1)
    def _(index):
        multiply(index)
        normalize(index + 1)

    start_all(a_tiles + at_tiles)
    wait_all(sends_in + cot_in)
    start_all(sends_out)
    multiply(count - 1)

    @pl.loop(0, count)
    def _(index):
        gradient(index)

    wait_all(sends_out + a_tiles + at_tiles)


def project(bits, length, x, cot, vectors, qkv, proj, fc, ow):
    slots, model = x.shape
    width = qkv.shape[2]
    units = fc.shape[1]
    tokens = slots // TILE
    sends = [
        (width // 2 + 32, model),
        (model // 4, units),
        (units // 4, model),
    ]
    shapes = [(slots, model), (model, slots)]
    dma = pltpu.SemaphoreType.DMA
    return call(
        project_kernel,
        "project_own",
        1,
        [(bits, SMEM), (x, HBM)]
        + [(vector, whole(vector.shape)) for vector in vectors]
        + [(weight, HBM) for weight in (qkv, proj, fc, ow)]
        + [(length, SMEM), (cot, HBM)],
        [
            ((16, model), F32, whole((16, model))),
            ((slots, 3 * width), BF, KEPT),
            ((slots, model), BF, KEPT),
            ((model, slots), BF, KEPT),
            ((1, model), F32, whole((1, model))),
        ]
        + [(shape, BF, HBM) for shape in shapes + sends],
        [pltpu.VMEM((slots, model), BF), pltpu.VMEM((model, 3 * width), BF)]
        + [pltpu.VMEM(shape, BF) for shape in shapes + sends]
        + [pltpu.VMEM((slots, model), BF), pltpu.VMEM((TILE, model), BF)]
        + [dma((tokens,)), dma((3,)), dma((tokens,)), dma((6,)), dma((tokens,)), dma((tokens,))],
        6 * slots * model * width,
        12,
    )


def causal_fill():
    keys = lax.broadcasted_iota(jnp.int32, (TILE, TILE), 0)
    queries = lax.broadcasted_iota(jnp.int32, (TILE, TILE), 1)
    return jnp.where(keys <= queries, 0.0, FILL)


def masked_pair(pair_keys, pair_queries, length, keys_ref, queries_ref):
    slots = pair_keys.shape[0]
    lane = lax.broadcasted_iota(jnp.int32, (slots, 128), 1)
    position = lax.broadcasted_iota(jnp.int32, (slots, 128), 0)
    fill = jnp.where(position < length, 0.0, FILL)
    pair_keys = pair_keys.astype(F32)
    pair_queries = pair_queries.astype(F32)
    for half in (0, 1):
        spare = 64 * (1 - half)
        keys_ref[half] = jnp.where(lane == spare, fill, pair_keys).astype(BF)
        queries_ref[half] = jnp.where(
            lane // 64 == half, pair_queries, jnp.where(lane == spare, 1.0, 0.0)
        ).astype(BF)


def block_order(blocks):
    return [(block, 0) for block in range(blocks)] + [(block, 1) for block in reversed(range(blocks))]


def pair_lanes(pair, offset=0):
    return pl.ds(pl.multiple_of(offset + pair * 128, 128), 128)


def forward_pairs(length, qkv_ref, ctx_ref, ctxt_ref, lse_ref, scratch, results):
    ka_ref, qa_ref, vt_ref, score_ref, expo_ref = scratch
    width, slots = ctxt_ref.shape
    causal = causal_fill()

    @pl.loop(0, width // 128)
    def _(pair):
        lanes = pair_lanes(pair)
        masked_pair(
            qkv_ref[:, pair_lanes(pair, width)], qkv_ref[:, lanes], length, ka_ref, qa_ref
        )
        vt_ref[...] = qkv_ref[:, pair_lanes(pair, 2 * width)].T
        items = block_order(slots // TILE)
        state = {}

        def score(item):
            block, half = items[item]
            extent = (block + 1) * TILE
            columns = slice(block * TILE, extent)
            scores = dot_nt(ka_ref[half, :extent, :], qa_ref[half, columns, :])
            high = None
            for inner in range(block + 1):
                keys = slice(inner * TILE, (inner + 1) * TILE)
                part = scores[keys]
                if inner == block:
                    part = part + causal
                score_ref[item % 2, keys, :] = part
                most = jnp.max(part.reshape(TILE // 8, 8, TILE), 0)
                high = most if high is None else jnp.maximum(high, most)
            state[item] = jnp.max(high, 0, keepdims=True)

        def exponential(item):
            block, half = items[item]
            high = state[item]
            total = None
            for inner in range(block + 1):
                keys = slice(inner * TILE, (inner + 1) * TILE)
                expo = jnp.exp(score_ref[item % 2, keys, :] - high)
                part = jnp.sum(expo.reshape(TILE // 8, 8, TILE), 0)
                total = part if total is None else total + part
                expo_ref[item % 2, keys, :] = expo.astype(BF)
            state[item] = (high, jnp.sum(total, 0, keepdims=True))

        def mix(item):
            block, half = items[item]
            extent = (block + 1) * TILE
            columns = slice(block * TILE, extent)
            high, total = state[item]
            mixed = dot(vt_ref[64 * half : 64 * half + 64, :extent], expo_ref[item % 2, :extent, :])
            row = pl.multiple_of(pair * 128 + half * 64, 64)
            ctxt_ref[pl.ds(row, 64), columns] = mixed * (1.0 / total)
            lse_ref[pl.ds(pair * 2 + half, 1), columns] = high + jnp.log(total)

        count = len(items)
        score(0)
        for item in range(count + 1):
            if item + 1 < count:
                score(item + 1)
            if item >= 1:
                mix(item - 1)
            if item < count:
                exponential(item)
        ctx_ref[:, lanes] = ctxt_ref[lanes, :].T.astype(BF)
        start_all(results(pair))


def forward_own_kernel(
    length_ref, qkv_ref, lse_ref, ctx_out, ctxt_out, qkv_out, ctx_ref, ctxt_ref, *rest
):
    scratch, sems = rest[:5], rest[5]
    saved = pltpu.make_async_copy(qkv_ref, qkv_out, sems.at[2, 0])
    saved.start()

    def results(pair):
        lanes = pair_lanes(pair)
        return [
            pltpu.make_async_copy(ctx_ref.at[:, lanes], ctx_out.at[:, lanes], sems.at[0, pair]),
            pltpu.make_async_copy(ctxt_ref.at[lanes, :], ctxt_out.at[lanes, :], sems.at[1, pair]),
        ]

    forward_pairs(length_ref[0], qkv_ref, ctx_ref, ctxt_ref, lse_ref, scratch, results)
    for pair in range(ctx_ref.shape[1] // 128):
        wait_all(results(pair))
    saved.wait()


def forward_other_kernel(
    bits_ref, length_ref, other_vec_ref, vec_ref, a_hbm, x_hbm, ctx0_hbm, proj0_hbm, *rest
):
    pieces, proj_pieces, rest = rest[:4], rest[4:6], rest[6:]
    lse_ref, c_ref, ct_ref, middle_out, ctxt_out, qkv_out, *rest = rest
    both_ref, ctxt_ref, *rest = rest
    scratch, rest = rest[:5], rest[5:]
    qkv_ref, a_ref, w_ref, x_ref, proj_ref, middle_ref, sum_ref, *rest = rest
    a_sems, w_sems, qkv_sems, sems, late_sems, proj_sems, middle_sems = rest
    slots, width = ctx0_hbm.shape
    own = pl.ds(pl.multiple_of(bits_ref[3] * width, 128), width)
    other = pl.ds(pl.multiple_of((1 - bits_ref[3]) * width, 128), width)
    ctx_ref = both_ref.at[:, other]
    w_in = fetch_rows(pieces, bits_ref[1], w_ref, w_sems)
    start_all(w_in)
    a_in = tiles(a_hbm, a_ref, a_sems)
    start_all(a_in)
    late = [
        pltpu.make_async_copy(source, target, late_sems.at[index])
        for index, (source, target) in enumerate(
            ((x_hbm, x_ref), (ctx0_hbm, both_ref.at[:, own]), (proj0_hbm, proj_ref.at[own, :]))
        )
    ]
    halves_in = [piece.at[: width // 2, :] for piece in proj_pieces]
    late += fetch_rows(halves_in, bits_ref[0], proj_ref.at[other, :], proj_sems)
    start_all(late)
    bias, scale = qkv_bias(other_vec_ref[0:1, :], width)
    qkv_tiles = tiles(qkv_ref, qkv_out, qkv_sems)
    wait_all(w_in + a_in)

    @pl.loop(0, len(a_in))
    def _(index):
        rows = tile_of(index)
        product = dot(a_ref[rows, :], w_ref[...])
        qkv_ref[rows, :] = ((product + bias) * scale).astype(BF)

    start_all(qkv_tiles)

    def results(pair):
        lanes = pair_lanes(pair)
        return [
            pltpu.make_async_copy(ctxt_ref.at[lanes, :], ctxt_out.at[lanes, :], sems.at[pair])
        ]

    forward_pairs(length_ref[0], qkv_ref, ctx_ref, ctxt_ref, lse_ref, scratch, results)
    wait_all(late)
    count = slots // TILE

    def branch(index):
        return dot(both_ref[tile_of(index), :], proj_ref[...])

    def normalize(index):
        rows = tile_of(index)
        total = sum_ref[...] + vec_ref[BIAS_P : BIAS_P + 1, :]
        middle = x_ref[rows, :].astype(F32) + BRANCH * total
        middle_ref[rows, :] = middle
        normed, _ = norm_parts(middle)
        low = (normed * vec_ref[GAIN2 : GAIN2 + 1, :] + vec_ref[SHIFT2 : SHIFT2 + 1, :]).astype(BF)
        c_ref[rows, :] = low
        ct_ref[:, rows] = low.T

    sum_ref[...] = branch(0)

    @pl.loop(0, count - 1)
    def _(index):
        normalize(index)
        sum_ref[...] = branch(index + 1)
        tile_copy(middle_ref, middle_out, middle_sems, index).start()

    normalize(count - 1)
    middle_tiles = tiles(middle_ref, middle_out, middle_sems)
    middle_tiles[-1].start()
    for pair in range(width // 128):
        wait_all(results(pair))
    wait_all(qkv_tiles + middle_tiles)


def forward_scratch(slots, width):
    return [
        pltpu.VMEM((slots, width), BF),
        pltpu.VMEM((width, slots), F32),
        pltpu.VMEM((2, slots, 128), BF),
        pltpu.VMEM((2, slots, 128), BF),
        pltpu.VMEM((128, slots), BF),
        pltpu.VMEM((2, slots, TILE), F32),
        pltpu.VMEM((2, slots, TILE), BF),
    ]


def attention_forward_own(length, qkv):
    slots = qkv.shape[0]
    width = qkv.shape[1] // 3
    heads = width // 64
    return call(
        forward_own_kernel,
        "attention_forward_own",
        1,
        [(length, SMEM), (qkv, KEPT)],
        [
            ((heads, slots), F32, whole((heads, slots))),
            ((slots, width), BF, HBM),
            ((width, slots), F32, HBM),
            ((slots, 3 * width), BF, HBM),
        ],
        [*forward_scratch(slots, width), pltpu.SemaphoreType.DMA((3, width // 128))],
        6 * slots * slots * width,
        6,
    )


def attention_forward_other(bits, length, other_vec, vec, a_low, x, ctx, proj, pieces, proj_pieces):
    slots, model = x.shape
    width = ctx.shape[1]
    heads = width // 64
    tokens = slots // TILE
    dma = pltpu.SemaphoreType.DMA
    ins = [(bits, SMEM), (length, SMEM)]
    ins += [(value, whole(value.shape)) for value in (other_vec, vec)]
    ins += [(value, HBM) for value in (a_low, x, ctx, proj, *pieces, *proj_pieces)]
    return call(
        forward_other_kernel,
        "attention_forward_other",
        1,
        ins,
        [
            ((heads, slots), F32, whole((heads, slots))),
            ((slots, model), BF, KEPT),
            ((model, slots), BF, KEPT),
            ((slots, model), F32, HBM),
            ((width, slots), F32, HBM),
            ((slots, 3 * width), BF, HBM),
        ],
        [
            pltpu.VMEM((slots, 2 * width), BF),
            *forward_scratch(slots, width)[1:],
            pltpu.VMEM((slots, 3 * width), BF),
            pltpu.VMEM((slots, model), BF),
            pltpu.VMEM((model, 3 * width), BF),
            pltpu.VMEM((slots, model), BF),
            pltpu.VMEM((2 * width, model), BF),
            pltpu.VMEM((slots, model), F32),
            pltpu.VMEM((TILE, model), F32),
            dma((tokens,)),
            dma((12,)),
            dma((tokens,)),
            dma((width // 128,)),
            dma((3,)),
            dma((2,)),
            dma((tokens,)),
        ],
        6 * slots * slots * width + 10 * slots * model * width,
        20,
    )


def mlp_step(c_ref, g_ref, fc, ow, bias):
    hidden = dot(c_ref[...], fc) + bias
    square = hidden * hidden
    tanh = jnp.tanh(hidden * (GELU + GELU * CUBIC * square))
    share = 0.5 + 0.5 * tanh
    value = hidden * share
    slope = share + value * (1.0 - share) * (2.0 * GELU + 6.0 * GELU * CUBIC * square)
    return value.astype(BF), (dot_nt(g_ref[...], ow) * slope).astype(BF)


def unit_bias(vec_ref, base, bias_ref):
    model = vec_ref.shape[1]
    for row in range(bias_ref.shape[1] // model):
        columns = slice(row * model, (row + 1) * model)
        bias_ref[:, columns] = vec_ref[base + row : base + row + 1, :]


def mlp_own_kernel(
    steps,
    block,
    bits_ref,
    c_ref,
    g_ref,
    ct_ref,
    gt_ref,
    vec_ref,
    fc_ref,
    ow_ref,
    gc_out,
    act_ref,
    fc_kept_ref,
    out_kept_ref,
    fc_sent_ref,
    out_sent_ref,
    db_ref,
    gc_ref,
    gc_low_ref,
    bias_ref,
    gh_ref,
    dw_ref,
    sem,
):
    step = pl.program_id(0)

    @pl.when(step == 0)
    def _():
        unit_bias(vec_ref, BIAS_FC, bias_ref)
        clear(gc_ref)

    lanes = pl.ds(pl.multiple_of(step * HIDDEN, HIDDEN), HIDDEN)
    act, gh = mlp_step(c_ref, g_ref, fc_ref[...], ow_ref[...], bias_ref[:, lanes])
    act_ref[...] = act
    gh_ref[...] = gh
    db_ref[...] = jnp.sum(gh.astype(F32), 0, keepdims=True)
    gc_ref[...] += dot_nt(gh, fc_ref[...])
    results = [pltpu.make_async_copy(gc_low_ref, gc_out, sem)]

    @pl.when(step == steps - 1)
    def _():
        gc_low_ref[...] = gc_ref[...].astype(BF)
        start_all(results)

    dw_ref[0] = dot(ct_ref[...], gh_ref[...]).astype(BF)
    halves(dw_ref.at[0], bits_ref[2], block, fc_kept_ref, fc_sent_ref.at[:, lanes])
    dw_ref[1] = dot(gt_ref[...], act_ref[...]).astype(BF)
    halves(dw_ref.at[1], bits_ref[2], block, out_kept_ref, out_sent_ref.at[:, lanes])

    @pl.when(step == steps - 1)
    def _():
        wait_all(results)


def feed_forward_own(bits, block, c_low, grad_mlp, c_turned, grad_turned, vec, fc, ow):
    slots, model = c_low.shape
    units = fc.shape[1]
    steps = units // HIDDEN
    half = column_tile(model // 2, HIDDEN)
    return call(
        functools.partial(mlp_own_kernel, steps, block),
        "feed_forward_own",
        steps,
        [(bits, SMEM)]
        + [(value, KEPT) for value in (c_low, grad_mlp, c_turned, grad_turned)]
        + [
            (vec, whole(vec.shape)),
            (fc, column_tile(model, HIDDEN)),
            (ow, pl.BlockSpec((HIDDEN, model), lambda i: (i, 0))),
        ],
        [((slots, model), BF, HBM), ((slots, units), BF, column_tile(slots, HIDDEN))]
        + [((model // 2, units), BF, half)] * 2
        + [((model // 2, units), BF, KEPT)] * 2
        + [((1, units), F32, column_tile(1, HIDDEN))],
        [
            pltpu.VMEM((slots, model), F32),
            pltpu.VMEM((slots, model), BF),
            pltpu.VMEM((1, units), F32),
            pltpu.VMEM((slots, HIDDEN), BF),
            pltpu.VMEM((2, model, HIDDEN), BF),
            pltpu.SemaphoreType.DMA,
        ],
        10 * slots * model * units,
        19,
    )


def mlp_other_kernel(
    steps,
    bits_ref,
    length_ref,
    c_ref,
    g_ref,
    other_vec_ref,
    vec_ref,
    gc0_hbm,
    middle_hbm,
    cot_hbm,
    proj0_hbm,
    fc_kept_hbm,
    out_kept_hbm,
    *rest,
):
    fc_pieces, out_pieces, proj_pieces, rest = rest[:4], rest[4:8], rest[8:10], rest[10:]
    do0_ref, fc_kept_ref, out_kept_ref, sums_ref, act_ref, gmid_out, ga_out, do1_out, *rest = rest
    gc_ref, bias_ref, fc_ref, ow_ref, *rest = rest
    late_refs, (gmid_ref, ga_ref, low_ref, do1_ref, proj1_ref, *rest) = rest[:4], rest[4:]
    sems, late_sems, proj_sems, out_sems = rest
    step = pl.program_id(0)
    slots, model = c_ref.shape
    copies = fetch_rows(fc_pieces, bits_ref[1], fc_ref, sems.at[0])
    copies += fetch_rows(out_pieces, bits_ref[4], ow_ref, sems.at[1])
    late = [
        pltpu.make_async_copy(source, target, late_sems.at[index])
        for index, (source, target) in enumerate(
            zip(
                (gc0_hbm, middle_hbm, cot_hbm, proj0_hbm, fc_kept_hbm, out_kept_hbm),
                (*late_refs, fc_kept_ref, out_kept_ref),
            )
        )
    ]
    half = proj1_ref.shape[0] // 2
    halves_in = [piece.at[:half, :] for piece in proj_pieces]
    late += fetch_rows(halves_in, bits_ref[0], proj1_ref, proj_sems)

    @pl.when(step == 0)
    def _():
        start_all(copies)
        unit_bias(other_vec_ref, 1, bias_ref)
        clear(gc_ref)
        wait_all(copies)
        start_all(late)

    lanes = pl.ds(pl.multiple_of(step * HIDDEN, HIDDEN), HIDDEN)
    act, gh = mlp_step(c_ref, g_ref, fc_ref[:, lanes], ow_ref[lanes, :], bias_ref[:, lanes])
    act_ref[...] = act
    gc_ref[...] += dot_nt(gh, fc_ref[:, lanes])

    @pl.when(step == steps - 1)
    def _():
        wait_all(late)
        gc0_ref, middle_ref, cot_ref, proj0_ref = late_refs
        pairs = ((gmid_ref, gmid_out), (ga_ref, ga_out), (do1_ref, do1_out))
        outs = [(*pair, out_sems.at[index]) for index, pair in enumerate(pairs)]
        count = slots // TILE
        sums_ref[...] = jnp.zeros(sums_ref.shape, F32)

        def elementwise(index):
            rows = tile_of(index)
            grad_c = gc_ref[rows, :].astype(BF).astype(F32) + gc0_ref[rows, :].astype(F32)
            normed, inverse = norm_parts(middle_ref[rows, :])
            top = grad_top_of(cot_ref[rows, :], length_ref[0], index * TILE)
            grad_middle = top + norm_back(grad_c, normed, inverse, vec_ref[GAIN2 : GAIN2 + 1, :])
            sums_ref[0:1, :] += jnp.sum(grad_c * normed, 0, keepdims=True)
            sums_ref[1:2, :] += jnp.sum(grad_c, 0, keepdims=True)
            sums_ref[2:3, :] += BRANCH * jnp.sum(grad_middle, 0, keepdims=True)
            gmid_ref[rows, :] = grad_middle
            low = (BRANCH * grad_middle).astype(BF)
            ga_ref[rows, :] = low
            low_ref[...] = low

        def project_back(index):
            rows = tile_of(index)
            do0_ref[rows, :] = dot_nt(low_ref[...], proj0_ref[...]).astype(BF)
            do1_ref[rows, :] = dot_nt(low_ref[...], proj1_ref[...]).astype(BF)

        elementwise(0)

        @pl.loop(0, count - 1)
        def _(index):
            project_back(index)
            elementwise(index + 1)
            for group in outs:
                tile_copy(*group, index).start()

        project_back(count - 1)
        for group in outs:
            tile_copy(*group, count - 1).start()
        for group in outs:
            wait_all(tiles(*group))


def feed_forward_other(
    bits, length, c_low, grad_mlp, other_vec, vec, grad_c, middle, cot, proj, kept, fc, ow, proj_pieces
):
    slots, model = c_low.shape
    width = proj.shape[0]
    units = fc[0].shape[1]
    steps = units // HIDDEN
    tokens = slots // TILE
    dma = pltpu.SemaphoreType.DMA
    return call(
        functools.partial(mlp_other_kernel, steps),
        "feed_forward_other",
        steps,
        [(bits, SMEM), (length, SMEM), (c_low, KEPT), (grad_mlp, KEPT)]
        + [(value, whole(value.shape)) for value in (other_vec, vec)]
        + [(value, HBM) for value in (grad_c, middle, cot, proj, *kept, *fc, *ow, *proj_pieces)],
        [
            ((slots, width), BF, KEPT),
            *[(value.shape, BF, KEPT) for value in kept],
            ((3, model), F32, whole((3, model))),
            ((slots, units), BF, column_tile(slots, HIDDEN)),
            ((slots, model), F32, HBM),
            ((slots, model), BF, HBM),
            ((slots, width), BF, HBM),
        ],
        [
            pltpu.VMEM((slots, model), F32),
            pltpu.VMEM((1, units), F32),
            pltpu.VMEM((model, units), BF),
            pltpu.VMEM((units, model), BF),
            pltpu.VMEM((slots, model), BF),
            pltpu.VMEM((slots, model), F32),
            pltpu.VMEM((slots, model), BF),
            pltpu.VMEM((width, model), BF),
            pltpu.VMEM((slots, model), F32),
            pltpu.VMEM((slots, model), BF),
            pltpu.VMEM((TILE, model), BF),
            pltpu.VMEM((slots, width), BF),
            pltpu.VMEM((width, model), BF),
            dma((2, 4)),
            dma((6,)),
            dma((2,)),
            dma((3, tokens)),
        ],
        6 * slots * model * units + 4 * slots * model * width,
        31,
    )


def output_kernel(vec_ref, act_ref, ow_ref, middle_ref, y_ref):
    mlp = dot(act_ref[tile_of(pl.program_id(0)), :], ow_ref[...]) + vec_ref[BIAS_O : BIAS_O + 1, :]
    y_ref[...] = (middle_ref[...] + BRANCH * mlp).astype(BF)


def block_result(vec, act, ow, middle):
    slots, model = middle.shape
    return call(
        output_kernel,
        "output",
        slots // TILE,
        [(vec, whole(vec.shape)), (act, KEPT), (ow, KEPT), (middle, row_tile(model))],
        [((slots, model), BF, row_tile(model))],
        [],
        2 * slots * model * act.shape[1],
        5,
    )[0]


def backward_pairs(length, qkv_ref, do_ref, ctxt_ref, lse_ref, d_ref, scratch, sources):
    (
        ka_ref,
        qa_ref,
        do_mask_ref,
        kt_ref,
        qt_ref,
        dot_ref,
        delta_ref,
        dqt_ref,
        dkt_ref,
        dvt_ref,
        score_ref,
        grad_ref,
        prob_ref,
        slope_ref,
    ) = scratch
    slots, width = do_ref.shape
    causal = causal_fill()
    blocks = slots // TILE

    @pl.loop(0, width // 128)
    def _(pair):
        lanes = pair_lanes(pair)
        wait_all(sources(pair))
        keys_low = qkv_ref[:, pair_lanes(pair, width)]
        queries = qkv_ref[:, lanes]
        masked_pair(keys_low, queries, length, ka_ref, qa_ref)
        grads = do_ref[:, lanes]
        lane = lax.broadcasted_iota(jnp.int32, (slots, 128), 1)
        for half in (0, 1):
            do_mask_ref[half] = jnp.where(lane // 64 == half, grads.astype(F32), 0.0).astype(BF)
        kt_ref[...] = keys_low.T
        qt_ref[...] = queries.T
        turned = grads.T
        dot_ref[...] = turned
        product = turned.astype(F32) * ctxt_ref[lanes, :]
        for half in (0, 1):
            delta_ref[half : half + 1, :] = jnp.sum(
                product[64 * half : 64 * half + 64], 0, keepdims=True
            )
        items = block_order(blocks)

        def score(item):
            block, half = items[item]
            extent = (block + 1) * TILE
            columns = slice(block * TILE, extent)
            score_ref[item % 2, :extent, :] = dot_nt(
                ka_ref[half, :extent, :], qa_ref[half, columns, :]
            )
            grad_ref[item % 2, :extent, :] = dot_nt(
                qkv_ref[:extent, pair_lanes(pair, 2 * width)], do_mask_ref[half, columns, :]
            )

        def softmax(item):
            block, half = items[item]
            columns = slice(block * TILE, (block + 1) * TILE)
            lse = lse_ref[pl.ds(pair * 2 + half, 1), columns]
            delta = delta_ref[half : half + 1, columns]
            for inner in range(block + 1):
                keys = slice(inner * TILE, (inner + 1) * TILE)
                scores = score_ref[item % 2, keys, :]
                if inner == block:
                    scores = scores + causal
                prob = jnp.exp(scores - lse)
                slope_ref[item % 2, keys, :] = (
                    prob * (grad_ref[item % 2, keys, :] - delta)
                ).astype(BF)
                prob_ref[item % 2, keys, :] = prob.astype(BF)

        def gradients(item):
            block, half = items[item]
            extent = (block + 1) * TILE
            columns = slice(block * TILE, extent)
            rows = slice(64 * half, 64 * half + 64)
            dv_part = dot_nt(dot_ref[rows, columns], prob_ref[item % 2, :extent, :])
            dk_part = dot_nt(qt_ref[rows, columns], slope_ref[item % 2, :extent, :])
            fresh = block * TILE if half == 0 else (0 if block == blocks - 1 else extent)
            if fresh < extent:
                dvt_ref[rows, fresh:extent] = dv_part[:, fresh:]
                dkt_ref[rows, fresh:extent] = dk_part[:, fresh:]
            if fresh:
                dvt_ref[rows, :fresh] += dv_part[:, :fresh]
                dkt_ref[rows, :fresh] += dk_part[:, :fresh]
            dqt_ref[rows, columns] = dot(kt_ref[rows, :extent], slope_ref[item % 2, :extent, :])

        count_items = len(items)
        score(0)
        for item in range(count_items + 1):
            if item + 1 < count_items:
                score(item + 1)
            if item >= 1:
                gradients(item - 1)
            if item < count_items:
                softmax(item)
        d_ref[:, lanes] = (dqt_ref[...] * 0.125).astype(BF).T
        d_ref[:, pair_lanes(pair, width)] = dkt_ref[...].astype(BF).T
        d_ref[:, pair_lanes(pair, 2 * width)] = dvt_ref[...].astype(BF).T


def pair_sources(pair, width, qkv, ctxt, do, sems):
    lanes = pair_lanes(pair)
    moves = []
    for matrix in range(3):
        columns = pair_lanes(pair, matrix * width)
        moves.append((qkv[0].at[:, columns], qkv[1].at[:, columns]))
    moves.append((ctxt[0].at[lanes, :], ctxt[1].at[lanes, :]))
    if do is not None:
        moves.append((do[0].at[:, lanes], do[1].at[:, lanes]))
    return [
        pltpu.make_async_copy(source, target, sems.at[index, pair])
        for index, (source, target) in enumerate(moves)
    ]


def backward_other_kernel(
    bits_ref, length_ref, lse_ref, qkv_hbm, ctxt_hbm, do_hbm, d0_hbm, w_hbm, ow_hbm, *rest
):
    pieces, out_pieces, rest = rest[:4], rest[4:8], rest[8:]
    both_ref, weight_ref, ow_ref, qkv_ref, ctxt_ref, do_ref, *rest = rest
    scratch, (sems, late_sem, w_sems, ow_sems) = rest[:14], rest[14:]
    width = do_ref.shape[1]
    sources = lambda pair: pair_sources(
        pair, width, (qkv_hbm, qkv_ref), (ctxt_hbm, ctxt_ref), (do_hbm, do_ref), sems
    )
    for pair in range(width // 128):
        start_all(sources(pair))
    own = pl.ds(pl.multiple_of(bits_ref[3] * 3 * width, 128), 3 * width)
    other = pl.ds(pl.multiple_of((1 - bits_ref[3]) * 3 * width, 128), 3 * width)
    late = [pltpu.make_async_copy(d0_hbm, both_ref.at[:, own], late_sem)]
    late += fetch_rows([w_hbm], 0, weight_ref.at[:, own], w_sems.at[0])
    late += fetch_rows(pieces, bits_ref[1], weight_ref.at[:, other], w_sems.at[1])
    units = ow_hbm.shape[0]
    rows = pl.ds(pl.multiple_of(bits_ref[3] * units, 128), units)
    late += fetch_rows([ow_hbm], 0, ow_ref.at[rows, :], ow_sems.at[0])
    rows = pl.ds(pl.multiple_of((1 - bits_ref[3]) * units, 128), units)
    late += fetch_rows(out_pieces, bits_ref[4], ow_ref.at[rows, :], ow_sems.at[1])
    start_all(late)
    d_ref = both_ref.at[:, other]
    backward_pairs(length_ref[0], qkv_ref, do_ref, ctxt_ref, lse_ref, d_ref, scratch, sources)
    wait_all(late)


def lane_sums(value):
    total = value[:, :128]
    for start in range(128, value.shape[1], 128):
        total = total + value[:, start : start + 128]
    return jnp.sum(total.T, 0, keepdims=True)


def backward_own_kernel(
    block,
    bits_ref,
    length_ref,
    lse_ref,
    vec_ref,
    ob_ref,
    sums_ref,
    db_ref,
    do_ref,
    qkv_hbm,
    ctxt_hbm,
    at_hbm,
    gat_hbm,
    w_hbm,
    lead_ref,
    vectors_ref,
    kept_ref,
    sent_ref,
    d_out,
    qkv_ref,
    ctxt_ref,
    *rest,
):
    scratch, rest = rest[:14], rest[14:]
    d_ref, at_ref, gat_ref, w_ref, dw_ref, total_ref, sems, w_sems, late_sems, out_sem = rest
    width = do_ref.shape[1]
    model = at_ref.shape[0]
    sources = lambda pair: pair_sources(
        pair, width, (qkv_hbm, qkv_ref), (ctxt_hbm, ctxt_ref), None, sems
    )
    for pair in range(width // 128):
        start_all(sources(pair))
    late = fetch_rows([w_hbm], 0, w_ref, w_sems)
    late += [
        pltpu.make_async_copy(at_hbm, at_ref, late_sems.at[0]),
        pltpu.make_async_copy(gat_hbm, gat_ref, late_sems.at[1]),
    ]
    start_all(late)
    backward_pairs(length_ref[0], qkv_ref, do_ref, ctxt_ref, lse_ref, d_ref, scratch, sources)
    saved = pltpu.make_async_copy(d_ref, d_out, out_sem)
    saved.start()
    lead_ref[...] = jnp.zeros(lead_ref.shape, F32)
    wait_all(late)
    low = ctxt_ref[...].astype(BF)
    dw_ref[:, 3 * width :] = dot(low, gat_ref[...]).T.astype(BF)
    total_ref[...] = jnp.zeros(total_ref.shape, F32)

    @pl.loop(0, d_ref.shape[0] // TILE)
    def _(index):
        total_ref[...] += jnp.sum(d_ref[tile_of(index), :].astype(F32), 0, keepdims=True)

    sums = total_ref[...]

    @pl.loop(0, model // TILE)
    def _(index):
        rows = tile_of(index)
        part = dot(at_ref[rows, :], d_ref[...])
        dw_ref[rows, : 3 * width] = part.astype(BF)
        weight = w_ref[rows, :].astype(F32)
        lead_ref[0:1, rows] = lane_sums(part * weight)
        lead_ref[1:2, rows] = lane_sums(weight * sums)

    halves(dw_ref, bits_ref[2], block, kept_ref, sent_ref)
    scaled, shift = lead_ref[0:1, :], lead_ref[1:2, :]
    gain1, shift1 = vec_ref[GAIN1 : GAIN1 + 1, :], vec_ref[SHIFT1 : SHIFT1 + 1, :]
    vectors_ref[...] = jnp.zeros(vectors_ref.shape, F32)
    lead_ref[0:1, :] = (scaled - shift1 * shift) / gain1
    vectors_ref[2:3, :] = ob_ref[...]
    vectors_ref[3:6, :] = sums_ref[...]
    for index in range(2):
        vectors_ref[6 + index : 7 + index, :] = db_ref[:, index * model : (index + 1) * model]
    vectors_ref[8:9, :width] = sums[:, :width]
    vectors_ref[8:9, width:] = sums[:, 2 * width :]
    saved.wait()


def backward_scratch(slots):
    return [
        pltpu.VMEM((2, slots, 128), BF),
        pltpu.VMEM((2, slots, 128), BF),
        pltpu.VMEM((2, slots, 128), BF),
        pltpu.VMEM((128, slots), BF),
        pltpu.VMEM((128, slots), BF),
        pltpu.VMEM((128, slots), BF),
        pltpu.VMEM((2, slots), F32),
        pltpu.VMEM((128, slots), F32),
        pltpu.VMEM((128, slots), F32),
        pltpu.VMEM((128, slots), F32),
        pltpu.VMEM((2, slots, TILE), F32),
        pltpu.VMEM((2, slots, TILE), F32),
        pltpu.VMEM((2, slots, TILE), BF),
        pltpu.VMEM((2, slots, TILE), BF),
    ]


def attention_backward_other(bits, length, lse, qkv, ctxt, do, d0, weight, ow, pieces, out_pieces):
    slots, width = do.shape
    model = weight.shape[1]
    dma = pltpu.SemaphoreType.DMA
    ins = [(bits, SMEM), (length, SMEM), (lse, whole(lse.shape))]
    ins += [(value, HBM) for value in (qkv, ctxt, do, d0, weight, ow, *pieces, *out_pieces)]
    return call(
        backward_other_kernel,
        "attention_backward_other",
        1,
        ins,
        [
            ((slots, 6 * width), BF, KEPT),
            ((model, 6 * width), BF, KEPT),
            ((2 * ow.shape[0], model), BF, KEPT),
        ],
        [
            pltpu.VMEM((slots, 3 * width), BF),
            pltpu.VMEM((width, slots), F32),
            pltpu.VMEM((slots, width), BF),
            *backward_scratch(slots),
            dma((5, width // 128)),
            dma,
            dma((2, 12)),
            dma((2, 4)),
        ],
        9 * slots * slots * width,
        12,
    )


def attention_backward_own(bits, length, block, lse, vec, sums, do, qkv, ctxt, at, gat, weight):
    slots, width = do.shape
    model = at.shape[0]
    dma = pltpu.SemaphoreType.DMA
    ins = [(bits, SMEM), (length, SMEM)]
    ins += [(value, whole(value.shape)) for value in (lse, vec, *sums)]
    ins += [(do, KEPT)] + [(value, HBM) for value in (qkv, ctxt, at, gat, weight)]
    outs = [((rows, model), F32, KEPT) for rows in (8, 16)] + [((model // 2, 4 * width), BF, KEPT)] * 2
    outs += [((slots, 3 * width), BF, HBM)]
    return call(
        functools.partial(backward_own_kernel, block),
        "attention_backward_own",
        1,
        ins,
        outs,
        [
            pltpu.VMEM((slots, 3 * width), BF),
            pltpu.VMEM((width, slots), F32),
            *backward_scratch(slots),
            pltpu.VMEM((slots, 3 * width), BF),
            pltpu.VMEM((model, slots), BF),
            pltpu.VMEM((slots, model), BF),
            pltpu.VMEM((model, 3 * width), BF),
            pltpu.VMEM((model, 4 * width), BF),
            pltpu.VMEM((1, 3 * width), F32),
            dma((4, width // 128)),
            dma((3,)),
            dma((2,)),
            dma,
        ],
        9 * slots * slots * width + 8 * slots * model * width,
        21,
    )


def final_kernel(
    bits_ref, vec_ref, d_ref, w_ref, x_hbm, gmid_hbm, act0_hbm, act1_hbm, *rest
):
    gin_out, act_ref, x_ref, gmid_ref, gin_ref, product_ref, *rest = rest
    x_sems, gmid_sems, gin_sems, act_sems = rest
    x_in = tiles(x_hbm, x_ref, x_sems)
    gmid_in = tiles(gmid_hbm, gmid_ref, gmid_sems)
    gin_tiles = tiles(gin_ref, gin_out, gin_sems)
    start_all(x_in + gmid_in)
    units = act0_hbm.shape[1]
    own = pl.ds(pl.multiple_of(bits_ref[3] * units, 128), units)
    other = pl.ds(pl.multiple_of((1 - bits_ref[3]) * units, 128), units)
    late = [
        pltpu.make_async_copy(act0_hbm, act_ref.at[:, own], act_sems.at[0]),
        pltpu.make_async_copy(act1_hbm, act_ref.at[:, other], act_sems.at[1]),
    ]
    start_all(late)
    count = len(x_in)

    def product(index):
        return dot_nt(d_ref[tile_of(index), :], w_ref[...])

    def norm(index):
        rows = tile_of(index)
        normed, inverse = norm_parts(x_ref[rows, :].astype(F32))
        back = norm_back(product_ref[...], normed, inverse, vec_ref[GAIN1 : GAIN1 + 1, :])
        gin_ref[rows, :] = gmid_ref[rows, :] + back

    product_ref[...] = product(0)
    wait_all(x_in + gmid_in)

    @pl.loop(0, count - 1)
    def _(index):
        norm(index)
        product_ref[...] = product(index + 1)
        tile_copy(gin_ref, gin_out, gin_sems, index).start()

    norm(count - 1)
    gin_tiles[-1].start()
    wait_all(late + gin_tiles)


def gradient_of_input(bits, vec, both, weight, x, gmid, act0, act1):
    slots, model = x.shape
    units = act0.shape[1]
    tokens = slots // TILE
    dma = pltpu.SemaphoreType.DMA
    return call(
        final_kernel,
        "final",
        1,
        [(bits, SMEM), (vec, whole(vec.shape)), (both, KEPT), (weight, KEPT)]
        + [(value, HBM) for value in (x, gmid, act0, act1)],
        [
            ((slots, model), F32, HBM),
            ((slots, 2 * units), BF, KEPT),
        ],
        [
            pltpu.VMEM((slots, model), BF),
            pltpu.VMEM((slots, model), F32),
            pltpu.VMEM((slots, model), F32),
            pltpu.VMEM((TILE, model), F32),
            dma((tokens,)),
            dma((tokens,)),
            dma((tokens,)),
            dma((2,)),
        ],
        2 * slots * model * both.shape[1],
        13,
    )


def across(value):
    return lax.ppermute(value, "tensor", [(0, 1), (1, 0)])


def swap(value, bit):
    count = lax.axis_size("dp")
    return lax.ppermute(value, "dp", [(i, i ^ bit) for i in range(count)])


def tie(*values):
    return lax.optimization_barrier(values)


def pick(value, index, axis):
    return lax.dynamic_index_in_dim(value, index, axis, keepdims=False)


def split_rows(value, count):
    shape = value.shape
    return value.reshape(*shape[:-2], count, shape[-2] // count, shape[-1])


class Reduction:
    def __init__(self, kept, first_bit, order):
        self.order = order
        self.bits = [bit for bit in reversed(range(len(order) + 1)) if bit != first_bit]
        rows = kept.shape[0] >> len(self.bits)
        self.kept = kept.reshape(*[2] * len(self.bits), rows, kept.shape[1])

    def advance(self, got):
        got = got.reshape(self.kept.shape)
        self.bit = self.order.pop(0)
        axis = self.bits.index(self.bit)
        self.bits.remove(self.bit)
        side = (lax.axis_index("dp") >> self.bit) & 1

        def part(index):
            total = pick(self.kept, index, axis).astype(F32) + pick(got, index, axis).astype(F32)
            return total.astype(BF)

        sent = part(1 - side)
        self.kept = part(side)
        return sent.reshape(-1, sent.shape[-1])

    def finish(self, got):
        return self.kept.astype(F32) + got.reshape(self.kept.shape).astype(F32)


def local(
    block_input,
    first_gain,
    first_shift,
    qkv_weight,
    qv_bias,
    proj_weight,
    proj_bias,
    second_gain,
    second_shift,
    fc_weight,
    fc_bias,
    out_weight,
    out_bias,
    cotangent,
    lengths,
):
    slots, model = block_input.shape
    width = qkv_weight.shape[2]
    units = fc_weight.shape[1]
    shards = lax.axis_size("dp")
    levels = shards.bit_length() - 1
    share = model // shards
    first_bit = next(bit for bit in range(levels) if (share << bit) % 16 == 0)
    block = share << first_bit
    later = [bit for bit in range(levels) if bit != first_bit]
    order_a = list(later)
    order_b = [later[1], later[0]] + later[2:]
    place = lax.axis_index("dp")
    quarter = jnp.bitwise_and(place, 3)
    one_bit = jnp.bitwise_and(place, 1)
    bits = jnp.stack(
        [
            one_bit,
            quarter,
            (place >> first_bit) & 1,
            lax.axis_index("tensor"),
            ((place >> 2) & 1) * 2 + one_bit,
        ]
    ).astype(jnp.int32)
    length = lengths.astype(jnp.int32)

    qkv_mine = across(pick(split_rows(qkv_weight, 4), quarter, 1))
    vectors = (first_gain, first_shift, proj_bias, second_gain, second_shift, out_bias)
    (
        vec,
        qkv0,
        grad_mlp,
        grad_mlp_turned,
        grad_out_bias,
        a_low,
        a_turned,
        proj_send,
        fc_send,
        out_send,
    ) = project(
        bits,
        length,
        block_input,
        cotangent,
        (*vectors, qv_bias, fc_bias),
        qkv_weight,
        proj_weight,
        fc_weight,
        out_weight,
    )

    qkv_mine, qkv0, proj_send, fc_send = tie(qkv_mine, qkv0, proj_send, fc_send)
    qkv_side = swap(qkv_mine, 2)
    qkv_core = swap(qkv_mine, 1)
    proj_got = across(proj_send)
    fc_mine = across(fc_send)
    lse0, ctx0, ctxt0, qkv0 = attention_forward_own(length, qkv0)

    qkv_side, qkv_core, proj_got, ctx0, out_send = tie(
        qkv_side, qkv_core, proj_got, ctx0, out_send
    )
    half_rows = width // 2
    parts = proj_got[half_rows : half_rows + 24].astype(F32).reshape(3, 8, model)
    other_vec = (parts[0] + parts[1]) + parts[2]
    proj_other = [proj_got, swap(proj_got, 1)]
    qkv_other = [qkv_mine, qkv_core, qkv_side, swap(qkv_side, 1)]
    out_mine = across(out_send)
    lse1, c_low, c_turned, middle, ctxt1, qkv1 = attention_forward_other(
        bits,
        length,
        other_vec,
        vec,
        a_low,
        block_input,
        ctx0,
        proj_weight,
        qkv_other,
        proj_other,
    )

    c_low, fc_mine, out_mine = tie(c_low, fc_mine, out_mine)
    fc_side = swap(fc_mine, 2)
    fc_core = swap(fc_mine, 1)
    out_side = swap(out_mine, 4)
    out_core = swap(out_mine, 1)
    gc0, act0, fc_kept, out_kept, fc_sent, out_sent, grad_fc_bias = feed_forward_own(
        bits, block, c_low, grad_mlp, c_turned, grad_mlp_turned, vec, fc_weight, out_weight
    )

    fc_sent, out_sent, fc_side, fc_core, out_side, out_core = tie(
        fc_sent, out_sent, fc_side, fc_core, out_side, out_core
    )
    fc_other = [fc_mine, fc_core, fc_side, swap(fc_side, 1)]
    out_other = [out_mine, out_core, out_side, swap(out_side, 1)]
    fc_got = swap(fc_sent, 1 << first_bit)
    out_got = swap(out_sent, 1 << first_bit)
    do0, fc_kept, out_kept, sums2, act1, grad_middle, grad_attn, do1 = feed_forward_other(
        bits,
        length,
        c_low,
        grad_mlp,
        other_vec,
        vec,
        gc0,
        middle,
        cotangent,
        proj_weight,
        (fc_kept, out_kept),
        fc_other,
        out_other,
        proj_other,
    )

    fc_sum = Reduction(fc_kept, first_bit, list(order_a))
    out_sum = Reduction(out_kept, first_bit, list(order_b))
    do0, fc_got, out_got = tie(do0, fc_got, out_got)
    fc_sent = fc_sum.advance(fc_got)
    out_sent = out_sum.advance(out_got)
    do0, fc_sent, out_sent = tie(do0, fc_sent, out_sent)
    fc_got = swap(fc_sent, 1 << fc_sum.bit)
    out_got = swap(out_sent, 1 << out_sum.bit)
    lead, vectors, kept, sent, d0 = attention_backward_own(
        bits,
        length,
        block,
        lse0,
        vec,
        (grad_out_bias, sums2, grad_fc_bias),
        do0,
        qkv0,
        ctxt0,
        a_turned,
        grad_attn,
        qkv_weight,
    )

    sent, lead, fc_got, out_got = tie(sent, lead, fc_got, out_got)
    attn_got = swap(sent, 1 << first_bit)
    lead_got = across(lead)
    fc_sent = fc_sum.advance(fc_got)
    out_sent = out_sum.advance(out_got)
    fc_got = swap(fc_sent, 1 << fc_sum.bit)
    out_got = swap(out_sent, 1 << out_sum.bit)

    def rounded(vectors):
        return lax.reduce_precision(vectors, 8, 7)

    def join(vectors, got):
        return rounded(vectors) + got.astype(F32)

    vectors = jnp.concatenate([(lead + lead_got)[:2], vectors[2:]], 0)
    lines = vectors.shape[0]
    vectors = join(vectors, swap(vectors.astype(BF), 1 << first_bit))
    first_sum = Reduction(kept[:, :model], first_bit, list(order_a))
    second_sum = Reduction(kept[:, model:], first_bit, list(order_b))
    first_sent = jnp.concatenate(
        [first_sum.advance(attn_got[:, :model]), vectors.astype(BF)], 0
    )
    second_sent = second_sum.advance(attn_got[:, model:])
    first_sent, second_sent, qkv1 = tie(first_sent, second_sent, qkv1)
    first_got = swap(first_sent, 1 << first_sum.bit)
    second_got = swap(second_sent, 1 << second_sum.bit)
    both, weights, ow = attention_backward_other(
        bits, length, lse1, qkv1, ctxt1, do1, d0, qkv_weight, out_weight, qkv_other, out_other
    )

    both, fc_got, out_got, first_got, second_got = tie(both, fc_got, out_got, first_got, second_got)
    vectors = join(vectors, first_got[-lines:])
    first_sent = jnp.concatenate(
        [first_sum.advance(first_got[:-lines]), vectors.astype(BF)], 0
    )
    second_sent = second_sum.advance(second_got)
    rest_sent = jnp.concatenate([fc_sum.advance(fc_got), out_sum.advance(out_got)], 0)
    both, first_sent, second_sent, rest_sent = tie(both, first_sent, second_sent, rest_sent)
    first_got = swap(first_sent, 1 << first_sum.bit)
    second_got = swap(second_sent, 1 << second_sum.bit)
    rest_got = swap(rest_sent, 1 << fc_sum.bit)
    grad_input, act = gradient_of_input(
        bits, vec, both, weights, block_input, grad_middle, act0, act1
    )

    grad_input, first_got, second_got, act = tie(grad_input, first_got, second_got, act)
    for level in range(3, levels):
        vectors = join(vectors, first_got[-lines:])
        sent = [first_sum.advance(first_got[:-lines]), second_sum.advance(second_got)]
        rows = sent[0].shape[0]
        sent = jnp.concatenate([*sent, vectors.astype(BF)], 0)
        sent, act = tie(sent, act)
        got = swap(sent, 1 << first_sum.bit)
        first_got = jnp.concatenate([got[:rows], got[2 * rows :]], 0)
        second_got = got[rows : 2 * rows]
        if fc_sum.order:
            rows = rest_got.shape[0] // 2
            rest_sent = [fc_sum.advance(rest_got[:rows]), out_sum.advance(rest_got[rows:])]
            rest_got = swap(jnp.concatenate(rest_sent, 0), 1 << fc_sum.bit)
    block_output = block_result(vec, act, ow, middle)
    vectors = join(vectors, first_got[-lines:])
    first = first_sum.finish(first_got[:-lines])
    second = second_sum.finish(second_got)
    rows = rest_got.shape[0] // 2
    grad_fc_weight = fc_sum.finish(rest_got[:rows])
    grad_out_weight = out_sum.finish(rest_got[rows:]).T
    grad_qkv_weight = jnp.stack([first[:, :width], first[:, width:], second[:, :width]])
    grad_proj_weight = second[:, width:].T
    return (
        block_output,
        grad_input,
        vectors[0],
        vectors[1],
        grad_qkv_weight,
        vectors[8].reshape(2, width),
        grad_proj_weight,
        vectors[5],
        vectors[3],
        vectors[4],
        grad_fc_weight,
        vectors[6:8].reshape(units),
        grad_out_weight,
        vectors[2],
    )


def solution(mesh):
    placed = (
        P("dp", None),
        P(),
        P(),
        P(None, None, "tensor"),
        P(None, "tensor"),
        P("tensor", None),
        P(),
        P(),
        P(),
        P(None, "tensor"),
        P("tensor"),
        P("tensor", None),
        P(),
        P("dp", None),
        P("dp"),
    )
    return jax.shard_map(
        local,
        mesh=mesh,
        in_specs=placed,
        out_specs=(
            P("dp", None),
            P("dp", None),
            P(),
            P(),
            P(None, "dp", "tensor"),
            P(None, "tensor"),
            P("tensor", "dp"),
            P(),
            P(),
            P(),
            P("dp", "tensor"),
            P("tensor"),
            P("tensor", "dp"),
            P(),
        ),
        check_vma=False,
    )
```

```python
import functools

import jax
import jax.numpy as jnp
from jax import lax
from jax.experimental import pallas as pl
from jax.experimental.pallas import tpu as pltpu
from jax.sharding import PartitionSpec as P

EPSILON = 1e-05
BRANCH = 48 ** (-0.5)
GELU = 0.7978845608028654
CUBIC = 0.044715
FILL = -1e30
BF = jnp.bfloat16
F32 = jnp.float32
MIB = 1024 * 1024
TILE = 256
HIDDEN = 512
GAIN1, SHIFT1, BIAS_P, GAIN2, SHIFT2, BIAS_O = range(6)
BIAS_QV, BIAS_FC = 8, 9


def dot(left, right):
    return lax.dot_general(left, right, (((1,), (0,)), ((), ())), preferred_element_type=F32)


def dot_nt(left, right):
    return lax.dot_general(left, right, (((1,), (1,)), ((), ())), preferred_element_type=F32)


def norm_parts(values):
    row_mean = jnp.mean(values, -1, keepdims=True)
    centered = values - row_mean
    inverse = lax.rsqrt(jnp.mean(centered * centered, -1, keepdims=True) + EPSILON)
    return centered * inverse, inverse


def norm_back(grad_out, normed, inverse, gain):
    scaled = grad_out * gain
    inner = (
        scaled
        - jnp.mean(scaled, -1, keepdims=True)
        - normed * jnp.mean(scaled * normed, -1, keepdims=True)
    )
    return inverse * inner


def whole(shape):
    return pl.BlockSpec(shape, lambda *_: (0,) * len(shape))


def row_tile(columns):
    return pl.BlockSpec((TILE, columns), lambda i: (i, 0))


def column_tile(rows, size=TILE):
    return pl.BlockSpec((rows, size), lambda i: (0, i))


SMEM = pl.BlockSpec(memory_space=pltpu.SMEM)
HBM = pl.BlockSpec(memory_space=pl.ANY)
LOOSE = pl.BlockSpec(memory_space=pl.ANY)
KEPT = pl.BlockSpec(memory_space=pltpu.VMEM)


def call(body, name, steps, ins, outs, scratch, flops, limit=12):
    args = []
    for array, spec in ins:
        if spec is KEPT:
            array = pltpu.with_memory_space_constraint(array, pltpu.VMEM)
        elif spec is not SMEM and spec is not LOOSE:
            array = pltpu.with_memory_space_constraint(array, pltpu.HBM)
        args.append(array)
    moved = sum(a.size * a.dtype.itemsize for a, spec in ins if spec is not KEPT)
    moved += sum(
        jax.ShapeDtypeStruct(shape, dtype).size * jnp.dtype(dtype).itemsize
        for shape, dtype, spec in outs
        if spec is not KEPT
    )
    return pl.pallas_call(
        body,
        name=name,
        grid=(steps,),
        out_shape=tuple(
            (pltpu.VMEM if spec is KEPT else pltpu.HBM)(shape, dtype) for shape, dtype, spec in outs
        ),
        in_specs=[spec for _, spec in ins],
        out_specs=tuple(spec for _, _, spec in outs),
        scratch_shapes=scratch,
        compiler_params=pltpu.CompilerParams(vmem_limit_bytes=limit * MIB),
        cost_estimate=pl.CostEstimate(flops=flops, bytes_accessed=moved, transcendentals=0),
    )(*args)


def tile_of(step):
    return pl.ds(pl.multiple_of(step * TILE, TILE), TILE)


def fetch_rows(pieces, turn, target, sems):
    copies = []
    for index, piece in enumerate(pieces):
        rows = piece.shape[-2]
        if len(pieces) > 1:
            place = jnp.bitwise_xor(jnp.int32(index), turn)
            where = pl.ds(pl.multiple_of(place * rows, 32), rows)
        else:
            where = slice(None)
        if len(piece.shape) == 2:
            copies.append(pltpu.make_async_copy(piece, target.at[where, :], sems.at[index]))
            continue
        width = piece.shape[2]
        for matrix in range(3):
            columns = slice(matrix * width, (matrix + 1) * width)
            copies.append(
                pltpu.make_async_copy(
                    piece.at[matrix], target.at[where, columns], sems.at[3 * index + matrix]
                )
            )
    return copies


def start_all(copies):
    for copy in copies:
        copy.start()


def wait_all(copies):
    for copy in copies:
        copy.wait()


def qkv_bias(biases, width):
    bias = jnp.concatenate(
        [biases[:, :width], jnp.zeros((1, width), F32), biases[:, width:]], axis=1
    )
    lane = lax.broadcasted_iota(jnp.int32, (1, 3 * width), 1)
    return bias, jnp.where(lane < width, 0.125, 1.0)


def tiles(source, target, sems, axis=0):
    copies = []
    for index in range(source.shape[axis] // TILE):
        part = slice(index * TILE, (index + 1) * TILE)
        view = (part, slice(None)) if axis == 0 else (slice(None), part)
        copies.append(pltpu.make_async_copy(source.at[view], target.at[view], sems.at[index]))
    return copies


def tile_copy(source, target, sems, index):
    rows = tile_of(index)
    return pltpu.make_async_copy(source.at[rows, :], target.at[rows, :], sems.at[index])


def clear(*refs):
    @pl.loop(0, refs[0].shape[0] // TILE)
    def _(index):
        for ref in refs:
            ref[tile_of(index), :] = jnp.zeros((TILE, ref.shape[1]), ref.dtype)


def halves(value_ref, side, block, kept_ref, sent_ref):
    for index in range(value_ref.shape[0] // (2 * block)):
        rows = slice(index * block, (index + 1) * block)
        first = 2 * block * index
        here = pl.ds(pl.multiple_of(first + block * side, 16), block)
        there = pl.ds(pl.multiple_of(first + block * (1 - side), 16), block)
        kept_ref[rows, :] = value_ref[here, :]
        sent_ref[rows, :] = value_ref[there, :]


def grad_top_of(cot, length, start):
    rows, model = cot.shape
    position = lax.broadcasted_iota(jnp.int32, (rows, 128), 0) + start
    valid = jnp.where(position < length, 1.0, 0.0)
    return cot.astype(F32) * jnp.concatenate([valid] * (model // 128), axis=1)


def project_kernel(
    bits_ref,
    x_hbm,
    gain1_ref,
    shift1_ref,
    bias_p_ref,
    gain2_ref,
    shift2_ref,
    bias_o_ref,
    qv_ref,
    fcb_ref,
    qkv_hbm,
    proj_hbm,
    fc_hbm,
    out_hbm,
    length_ref,
    cot_hbm,
    vec_ref,
    qkv_ref,
    gm_ref,
    gmt_ref,
    ob_ref,
    a_out,
    at_out,
    proj_out,
    fc_out,
    out_out,
    x_ref,
    w_ref,
    a_ref,
    at_ref,
    proj_ref,
    fc_ref,
    out_ref,
    cot_ref,
    low_ref,
    x_sems,
    w_sems,
    cot_sems,
    send_sems,
    a_sems,
    at_sems,
):
    x_in = tiles(x_hbm, x_ref, x_sems)
    x_in[0].start()
    w_in = fetch_rows([qkv_hbm], 0, w_ref, w_sems)
    start_all(w_in)
    start_all(x_in[1:])
    model = x_ref.shape[1]
    half, quarter, fourth = proj_hbm.shape[0] // 2, fc_hbm.shape[0] // 4, out_hbm.shape[0] // 4
    sends_in = []
    for index, (source, target, place, rows) in enumerate(
        (
            (proj_hbm, proj_ref.at[:half, :], bits_ref[0], half),
            (fc_hbm, fc_ref, bits_ref[1], quarter),
            (out_hbm, out_ref, bits_ref[4], fourth),
        )
    ):
        where = pl.ds(pl.multiple_of(place * rows, 32), rows)
        sends_in.append(pltpu.make_async_copy(source.at[where, :], target, send_sems.at[index]))
    start_all(sends_in)
    sends_out = [
        pltpu.make_async_copy(source, target, send_sems.at[3 + index])
        for index, (source, target) in enumerate(
            ((proj_ref, proj_out), (fc_ref, fc_out), (out_ref, out_out))
        )
    ]
    cot_in = tiles(cot_hbm, cot_ref, cot_sems)
    start_all(cot_in)
    vec_ref[...] = jnp.zeros(vec_ref.shape, F32)
    for index, ref in enumerate(
        (gain1_ref, shift1_ref, bias_p_ref, gain2_ref, shift2_ref, bias_o_ref)
    ):
        vec_ref[index : index + 1, :] = ref[...].reshape(1, model)
    width = qv_ref.shape[1]
    vec_ref[BIAS_QV : BIAS_QV + 1, :width] = qv_ref[0:1, :]
    vec_ref[BIAS_QV : BIAS_QV + 1, width:] = qv_ref[1:2, :]
    fcb = fcb_ref[...].reshape(1, fcb_ref.shape[0])
    for index in range(2):
        vec_ref[BIAS_FC + index : BIAS_FC + index + 1, :] = fcb[:, index * model : (index + 1) * model]
    value = vec_ref[8 * (BIAS_QV // 8) :, :]
    high = value.astype(BF)
    rest = value - high.astype(F32)
    mid = rest.astype(BF)
    low = (rest - mid.astype(F32)).astype(BF)
    lines = value.shape[0]
    for index, part in enumerate((high, mid, low)):
        proj_ref[half + index * lines : half + (index + 1) * lines, :] = part

    def normalize(index):
        rows = tile_of(index)
        normed, _ = norm_parts(x_ref[rows, :].astype(F32))
        low = normed * vec_ref[GAIN1 : GAIN1 + 1, :] + vec_ref[SHIFT1 : SHIFT1 + 1, :]
        low = low.astype(BF)
        low_ref[...] = low
        a_ref[rows, :] = low
        at_ref[:, rows] = low.T

    def gradient(index):
        rows = tile_of(index)
        top = grad_top_of(cot_ref[rows, :], length_ref[0], index * TILE)
        ob_ref[...] += BRANCH * jnp.sum(top, 0, keepdims=True)
        low = (BRANCH * top).astype(BF)
        gm_ref[rows, :] = low
        gmt_ref[:, rows] = low.T

    def multiply(index):
        qkv_ref[tile_of(index), :] = ((dot(low_ref[...], w_ref[...]) + bias) * scale).astype(BF)

    count = len(x_in)
    bias, scale = qkv_bias(vec_ref[BIAS_QV : BIAS_QV + 1, :], width)
    a_tiles = tiles(a_ref, a_out, a_sems)
    at_tiles = tiles(at_ref, at_out, at_sems, 1)
    ob_ref[...] = jnp.zeros(ob_ref.shape, F32)
    x_in[0].wait()
    normalize(0)
    wait_all(w_in + x_in[1:])

    @pl.loop(0, count - 1)
    def _(index):
        multiply(index)
        normalize(index + 1)

    start_all(a_tiles + at_tiles)
    wait_all(sends_in + cot_in)
    start_all(sends_out)
    multiply(count - 1)

    @pl.loop(0, count)
    def _(index):
        gradient(index)

    wait_all(sends_out + a_tiles + at_tiles)


def project(bits, length, x, cot, vectors, qkv, proj, fc, ow):
    slots, model = x.shape
    width = qkv.shape[2]
    units = fc.shape[1]
    tokens = slots // TILE
    sends = [
        (width // 2 + 32, model),
        (model // 4, units),
        (units // 4, model),
    ]
    shapes = [(slots, model), (model, slots)]
    dma = pltpu.SemaphoreType.DMA
    return call(
        project_kernel,
        "project_own",
        1,
        [(bits, SMEM), (x, HBM)]
        + [(vector, whole(vector.shape)) for vector in vectors]
        + [(weight, HBM) for weight in (qkv, proj, fc, ow)]
        + [(length, SMEM), (cot, HBM)],
        [
            ((16, model), F32, whole((16, model))),
            ((slots, 3 * width), BF, KEPT),
            ((slots, model), BF, KEPT),
            ((model, slots), BF, KEPT),
            ((1, model), F32, whole((1, model))),
        ]
        + [(shape, BF, HBM) for shape in shapes + sends],
        [pltpu.VMEM((slots, model), BF), pltpu.VMEM((model, 3 * width), BF)]
        + [pltpu.VMEM(shape, BF) for shape in shapes + sends]
        + [pltpu.VMEM((slots, model), BF), pltpu.VMEM((TILE, model), BF)]
        + [dma((tokens,)), dma((3,)), dma((tokens,)), dma((6,)), dma((tokens,)), dma((tokens,))],
        6 * slots * model * width,
        12,
    )


def causal_fill():
    keys = lax.broadcasted_iota(jnp.int32, (TILE, TILE), 0)
    queries = lax.broadcasted_iota(jnp.int32, (TILE, TILE), 1)
    return jnp.where(keys <= queries, 0.0, FILL)


def masked_pair(pair_keys, pair_queries, length, keys_ref, queries_ref):
    slots = pair_keys.shape[0]
    lane = lax.broadcasted_iota(jnp.int32, (slots, 128), 1)
    position = lax.broadcasted_iota(jnp.int32, (slots, 128), 0)
    fill = jnp.where(position < length, 0.0, FILL)
    pair_keys = pair_keys.astype(F32)
    pair_queries = pair_queries.astype(F32)
    for half in (0, 1):
        spare = 64 * (1 - half)
        keys_ref[half] = jnp.where(lane == spare, fill, pair_keys).astype(BF)
        queries_ref[half] = jnp.where(
            lane // 64 == half, pair_queries, jnp.where(lane == spare, 1.0, 0.0)
        ).astype(BF)


def block_order(blocks):
    return [(block, 0) for block in range(blocks)] + [(block, 1) for block in reversed(range(blocks))]


def pair_lanes(pair, offset=0):
    return pl.ds(pl.multiple_of(offset + pair * 128, 128), 128)


def forward_pairs(length, qkv_ref, ctx_ref, ctxt_ref, lse_ref, scratch, results):
    ka_ref, qa_ref, vt_ref, score_ref, expo_ref = scratch
    width, slots = ctxt_ref.shape
    causal = causal_fill()

    @pl.loop(0, width // 128)
    def _(pair):
        lanes = pair_lanes(pair)
        masked_pair(
            qkv_ref[:, pair_lanes(pair, width)], qkv_ref[:, lanes], length, ka_ref, qa_ref
        )
        vt_ref[...] = qkv_ref[:, pair_lanes(pair, 2 * width)].T
        items = block_order(slots // TILE)
        state = {}

        def score(item):
            block, half = items[item]
            extent = (block + 1) * TILE
            columns = slice(block * TILE, extent)
            scores = dot_nt(ka_ref[half, :extent, :], qa_ref[half, columns, :])
            high = None
            for inner in range(block + 1):
                keys = slice(inner * TILE, (inner + 1) * TILE)
                part = scores[keys]
                if inner == block:
                    part = part + causal
                score_ref[item % 2, keys, :] = part
                most = jnp.max(part.reshape(TILE // 8, 8, TILE), 0)
                high = most if high is None else jnp.maximum(high, most)
            state[item] = jnp.max(high, 0, keepdims=True)

        def exponential(item):
            block, half = items[item]
            high = state[item]
            total = None
            for inner in range(block + 1):
                keys = slice(inner * TILE, (inner + 1) * TILE)
                expo = jnp.exp(score_ref[item % 2, keys, :] - high)
                part = jnp.sum(expo.reshape(TILE // 8, 8, TILE), 0)
                total = part if total is None else total + part
                expo_ref[item % 2, keys, :] = expo.astype(BF)
            state[item] = (high, jnp.sum(total, 0, keepdims=True))

        def mix(item):
            block, half = items[item]
            extent = (block + 1) * TILE
            columns = slice(block * TILE, extent)
            high, total = state[item]
            mixed = dot(vt_ref[64 * half : 64 * half + 64, :extent], expo_ref[item % 2, :extent, :])
            row = pl.multiple_of(pair * 128 + half * 64, 64)
            ctxt_ref[pl.ds(row, 64), columns] = mixed * (1.0 / total)
            lse_ref[pl.ds(pair * 2 + half, 1), columns] = high + jnp.log(total)

        count = len(items)
        score(0)
        for item in range(count + 1):
            if item + 1 < count:
                score(item + 1)
            if item >= 1:
                mix(item - 1)
            if item < count:
                exponential(item)
        ctx_ref[:, lanes] = ctxt_ref[lanes, :].T.astype(BF)
        start_all(results(pair))


def forward_own_kernel(
    length_ref, qkv_ref, lse_ref, ctx_out, ctxt_out, qkv_out, ctx_ref, ctxt_ref, *rest
):
    scratch, sems = rest[:5], rest[5]
    saved = pltpu.make_async_copy(qkv_ref, qkv_out, sems.at[2, 0])
    saved.start()

    def results(pair):
        lanes = pair_lanes(pair)
        return [
            pltpu.make_async_copy(ctx_ref.at[:, lanes], ctx_out.at[:, lanes], sems.at[0, pair]),
            pltpu.make_async_copy(ctxt_ref.at[lanes, :], ctxt_out.at[lanes, :], sems.at[1, pair]),
        ]

    forward_pairs(length_ref[0], qkv_ref, ctx_ref, ctxt_ref, lse_ref, scratch, results)
    for pair in range(ctx_ref.shape[1] // 128):
        wait_all(results(pair))
    saved.wait()


def forward_other_kernel(
    bits_ref, length_ref, other_vec_ref, vec_ref, a_hbm, x_hbm, ctx0_hbm, proj0_hbm, *rest
):
    pieces, proj_pieces, rest = rest[:4], rest[4:6], rest[6:]
    lse_ref, c_ref, ct_ref, middle_out, ctxt_out, qkv_out, *rest = rest
    both_ref, ctxt_ref, *rest = rest
    scratch, rest = rest[:5], rest[5:]
    qkv_ref, a_ref, w_ref, x_ref, proj_ref, middle_ref, sum_ref, *rest = rest
    a_sems, w_sems, qkv_sems, sems, late_sems, proj_sems, middle_sems = rest
    slots, width = ctx0_hbm.shape
    own = pl.ds(pl.multiple_of(bits_ref[3] * width, 128), width)
    other = pl.ds(pl.multiple_of((1 - bits_ref[3]) * width, 128), width)
    ctx_ref = both_ref.at[:, other]
    w_in = fetch_rows(pieces, bits_ref[1], w_ref, w_sems)
    start_all(w_in)
    a_in = tiles(a_hbm, a_ref, a_sems)
    start_all(a_in)
    late = [
        pltpu.make_async_copy(source, target, late_sems.at[index])
        for index, (source, target) in enumerate(
            ((x_hbm, x_ref), (ctx0_hbm, both_ref.at[:, own]), (proj0_hbm, proj_ref.at[own, :]))
        )
    ]
    halves_in = [piece.at[: width // 2, :] for piece in proj_pieces]
    late += fetch_rows(halves_in, bits_ref[0], proj_ref.at[other, :], proj_sems)
    start_all(late)
    bias, scale = qkv_bias(other_vec_ref[0:1, :], width)
    qkv_tiles = tiles(qkv_ref, qkv_out, qkv_sems)
    wait_all(w_in + a_in)

    @pl.loop(0, len(a_in))
    def _(index):
        rows = tile_of(index)
        product = dot(a_ref[rows, :], w_ref[...])
        qkv_ref[rows, :] = ((product + bias) * scale).astype(BF)

    start_all(qkv_tiles)

    def results(pair):
        lanes = pair_lanes(pair)
        return [
            pltpu.make_async_copy(ctxt_ref.at[lanes, :], ctxt_out.at[lanes, :], sems.at[pair])
        ]

    forward_pairs(length_ref[0], qkv_ref, ctx_ref, ctxt_ref, lse_ref, scratch, results)
    wait_all(late)
    count = slots // TILE

    def branch(index):
        return dot(both_ref[tile_of(index), :], proj_ref[...])

    def normalize(index):
        rows = tile_of(index)
        total = sum_ref[...] + vec_ref[BIAS_P : BIAS_P + 1, :]
        middle = x_ref[rows, :].astype(F32) + BRANCH * total
        middle_ref[rows, :] = middle
        normed, _ = norm_parts(middle)
        low = (normed * vec_ref[GAIN2 : GAIN2 + 1, :] + vec_ref[SHIFT2 : SHIFT2 + 1, :]).astype(BF)
        c_ref[rows, :] = low
        ct_ref[:, rows] = low.T

    sum_ref[...] = branch(0)

    @pl.loop(0, count - 1)
    def _(index):
        normalize(index)
        sum_ref[...] = branch(index + 1)
        tile_copy(middle_ref, middle_out, middle_sems, index).start()

    normalize(count - 1)
    middle_tiles = tiles(middle_ref, middle_out, middle_sems)
    middle_tiles[-1].start()
    for pair in range(width // 128):
        wait_all(results(pair))
    wait_all(qkv_tiles + middle_tiles)


def forward_scratch(slots, width):
    return [
        pltpu.VMEM((slots, width), BF),
        pltpu.VMEM((width, slots), F32),
        pltpu.VMEM((2, slots, 128), BF),
        pltpu.VMEM((2, slots, 128), BF),
        pltpu.VMEM((128, slots), BF),
        pltpu.VMEM((2, slots, TILE), F32),
        pltpu.VMEM((2, slots, TILE), BF),
    ]


def attention_forward_own(length, qkv):
    slots = qkv.shape[0]
    width = qkv.shape[1] // 3
    heads = width // 64
    return call(
        forward_own_kernel,
        "attention_forward_own",
        1,
        [(length, SMEM), (qkv, KEPT)],
        [
            ((heads, slots), F32, whole((heads, slots))),
            ((slots, width), BF, HBM),
            ((width, slots), F32, HBM),
            ((slots, 3 * width), BF, HBM),
        ],
        [*forward_scratch(slots, width), pltpu.SemaphoreType.DMA((3, width // 128))],
        6 * slots * slots * width,
        6,
    )


def attention_forward_other(bits, length, other_vec, vec, a_low, x, ctx, proj, pieces, proj_pieces):
    slots, model = x.shape
    width = ctx.shape[1]
    heads = width // 64
    tokens = slots // TILE
    dma = pltpu.SemaphoreType.DMA
    ins = [(bits, SMEM), (length, SMEM)]
    ins += [(value, whole(value.shape)) for value in (other_vec, vec)]
    ins += [(value, HBM) for value in (a_low, x, ctx, proj)]
    ins += [(value, LOOSE) for value in (*pieces, *proj_pieces)]
    return call(
        forward_other_kernel,
        "attention_forward_other",
        1,
        ins,
        [
            ((heads, slots), F32, whole((heads, slots))),
            ((slots, model), BF, KEPT),
            ((model, slots), BF, KEPT),
            ((slots, model), F32, HBM),
            ((width, slots), F32, HBM),
            ((slots, 3 * width), BF, HBM),
        ],
        [
            pltpu.VMEM((slots, 2 * width), BF),
            *forward_scratch(slots, width)[1:],
            pltpu.VMEM((slots, 3 * width), BF),
            pltpu.VMEM((slots, model), BF),
            pltpu.VMEM((model, 3 * width), BF),
            pltpu.VMEM((slots, model), BF),
            pltpu.VMEM((2 * width, model), BF),
            pltpu.VMEM((slots, model), F32),
            pltpu.VMEM((TILE, model), F32),
            dma((tokens,)),
            dma((12,)),
            dma((tokens,)),
            dma((width // 128,)),
            dma((3,)),
            dma((2,)),
            dma((tokens,)),
        ],
        6 * slots * slots * width + 10 * slots * model * width,
        20,
    )


def mlp_step(hidden, g_ref, ow):
    square = hidden * hidden
    tanh = jnp.tanh(hidden * (GELU + GELU * CUBIC * square))
    share = 0.5 + 0.5 * tanh
    value = hidden * share
    slope = share + value * (1.0 - share) * (2.0 * GELU + 6.0 * GELU * CUBIC * square)
    return value.astype(BF), (dot_nt(g_ref[...], ow) * slope).astype(BF)


def unit_bias(vec_ref, base, bias_ref):
    model = vec_ref.shape[1]
    for row in range(bias_ref.shape[1] // model):
        columns = slice(row * model, (row + 1) * model)
        bias_ref[:, columns] = vec_ref[base + row : base + row + 1, :]


def mlp_own_kernel(
    steps,
    block,
    bits_ref,
    c_ref,
    g_ref,
    ct_ref,
    gt_ref,
    vec_ref,
    fc_ref,
    ow_ref,
    gc_out,
    act_ref,
    fc_kept_ref,
    out_kept_ref,
    fc_sent_ref,
    out_sent_ref,
    db_ref,
    c_out,
    g_out,
    gc_ref,
    gc_low_ref,
    bias_ref,
    gh_ref,
    dw_ref,
    sems,
):
    saved = [
        pltpu.make_async_copy(c_ref, c_out, sems.at[1]),
        pltpu.make_async_copy(g_ref, g_out, sems.at[2]),
    ]
    step = pl.program_id(0)

    @pl.when(step == 0)
    def _():
        start_all(saved)
        unit_bias(vec_ref, BIAS_FC, bias_ref)
        clear(gc_ref)

    lanes = pl.ds(pl.multiple_of(step * HIDDEN, HIDDEN), HIDDEN)
    hidden = dot(c_ref[...], fc_ref[...]) + bias_ref[:, lanes]
    act, gh = mlp_step(hidden, g_ref, ow_ref[...])
    act_ref[...] = act
    gh_ref[...] = gh
    db_ref[...] = jnp.sum(gh.astype(F32), 0, keepdims=True)
    gc_ref[...] += dot_nt(gh, fc_ref[...])
    results = [pltpu.make_async_copy(gc_low_ref, gc_out, sems.at[0])]

    @pl.when(step == steps - 1)
    def _():
        gc_low_ref[...] = gc_ref[...].astype(BF)
        start_all(results)

    dw_ref[0] = dot(ct_ref[...], gh_ref[...]).astype(BF)
    halves(dw_ref.at[0], bits_ref[2], block, fc_kept_ref, fc_sent_ref.at[:, lanes])
    dw_ref[1] = dot(gt_ref[...], act_ref[...]).astype(BF)
    halves(dw_ref.at[1], bits_ref[2], block, out_kept_ref, out_sent_ref.at[:, lanes])

    @pl.when(step == steps - 1)
    def _():
        wait_all(results + saved)


def feed_forward_own(bits, block, c_low, grad_mlp, c_turned, grad_turned, vec, fc, ow):
    slots, model = c_low.shape
    units = fc.shape[1]
    steps = units // HIDDEN
    half = column_tile(model // 2, HIDDEN)
    return call(
        functools.partial(mlp_own_kernel, steps, block),
        "feed_forward_own",
        steps,
        [(bits, SMEM)]
        + [(value, KEPT) for value in (c_low, grad_mlp, c_turned, grad_turned)]
        + [
            (vec, whole(vec.shape)),
            (fc, column_tile(model, HIDDEN)),
            (ow, pl.BlockSpec((HIDDEN, model), lambda i: (i, 0))),
        ],
        [((slots, model), BF, HBM), ((slots, units), BF, column_tile(slots, HIDDEN))]
        + [((model // 2, units), BF, half)] * 2
        + [((model // 2, units), BF, KEPT)] * 2
        + [((1, units), F32, column_tile(1, HIDDEN))]
        + [((slots, model), BF, HBM)] * 2,
        [
            pltpu.VMEM((slots, model), F32),
            pltpu.VMEM((slots, model), BF),
            pltpu.VMEM((1, units), F32),
            pltpu.VMEM((slots, HIDDEN), BF),
            pltpu.VMEM((2, model, HIDDEN), BF),
            pltpu.SemaphoreType.DMA((3,)),
        ],
        10 * slots * model * units,
        19,
    )


def mlp_other_kernel(
    steps,
    bits_ref,
    length_ref,
    c_hbm,
    g_hbm,
    other_vec_ref,
    vec_ref,
    gc0_hbm,
    middle_hbm,
    cot_hbm,
    proj0_hbm,
    fc_kept_hbm,
    out_kept_hbm,
    *rest,
):
    fc_pieces, out_pieces, proj_pieces, rest = rest[:4], rest[4:8], rest[8:10], rest[10:]
    do0_ref, fc_kept_ref, out_kept_ref, sums_ref, act_ref, gmid_out, ga_out, do1_out, *rest = rest
    gc_ref, bias_ref, fc_ref, ow_ref, c_ref, g_ref, *rest = rest
    late_refs, (gmid_ref, ga_ref, low_ref, do1_ref, proj1_ref, *rest) = rest[:4], rest[4:]
    sems, late_sems, proj_sems, out_sems = rest
    step = pl.program_id(0)
    slots, model = c_ref.shape
    first = fetch_rows(fc_pieces, bits_ref[1], fc_ref, sems.at[0])
    first += [pltpu.make_async_copy(c_hbm, c_ref, sems.at[2, 0])]
    second = fetch_rows(out_pieces, bits_ref[4], ow_ref, sems.at[1])
    second += [pltpu.make_async_copy(g_hbm, g_ref, sems.at[2, 1])]
    late = [
        pltpu.make_async_copy(source, target, late_sems.at[index])
        for index, (source, target) in enumerate(
            zip(
                (gc0_hbm, middle_hbm, cot_hbm, proj0_hbm, fc_kept_hbm, out_kept_hbm),
                (*late_refs, fc_kept_ref, out_kept_ref),
            )
        )
    ]
    half = proj1_ref.shape[0] // 2
    halves_in = [piece.at[:half, :] for piece in proj_pieces]
    late += fetch_rows(halves_in, bits_ref[0], proj1_ref, proj_sems)

    @pl.when(step == 0)
    def _():
        start_all(first + second)
        unit_bias(other_vec_ref, 1, bias_ref)
        clear(gc_ref)
        wait_all(first + second)
        start_all(late)

    lanes = pl.ds(pl.multiple_of(step * HIDDEN, HIDDEN), HIDDEN)
    hidden = dot(c_ref[...], fc_ref[:, lanes]) + bias_ref[:, lanes]
    act, gh = mlp_step(hidden, g_ref, ow_ref[lanes, :])
    act_ref[...] = act
    gc_ref[...] += dot_nt(gh, fc_ref[:, lanes])

    @pl.when(step == steps - 1)
    def _():
        wait_all(late)
        gc0_ref, middle_ref, cot_ref, proj0_ref = late_refs
        pairs = ((gmid_ref, gmid_out), (ga_ref, ga_out), (do1_ref, do1_out))
        outs = [(*pair, out_sems.at[index]) for index, pair in enumerate(pairs)]
        count = slots // TILE
        sums_ref[...] = jnp.zeros(sums_ref.shape, F32)

        def elementwise(index):
            rows = tile_of(index)
            grad_c = gc_ref[rows, :].astype(BF).astype(F32) + gc0_ref[rows, :].astype(F32)
            normed, inverse = norm_parts(middle_ref[rows, :])
            top = grad_top_of(cot_ref[rows, :], length_ref[0], index * TILE)
            grad_middle = top + norm_back(grad_c, normed, inverse, vec_ref[GAIN2 : GAIN2 + 1, :])
            sums_ref[0:1, :] += jnp.sum(grad_c * normed, 0, keepdims=True)
            sums_ref[1:2, :] += jnp.sum(grad_c, 0, keepdims=True)
            sums_ref[2:3, :] += BRANCH * jnp.sum(grad_middle, 0, keepdims=True)
            gmid_ref[rows, :] = grad_middle
            low = (BRANCH * grad_middle).astype(BF)
            ga_ref[rows, :] = low
            low_ref[...] = low

        def project_back(index):
            rows = tile_of(index)
            do0_ref[rows, :] = dot_nt(low_ref[...], proj0_ref[...]).astype(BF)
            do1_ref[rows, :] = dot_nt(low_ref[...], proj1_ref[...]).astype(BF)

        elementwise(0)

        @pl.loop(0, count - 1)
        def _(index):
            project_back(index)
            elementwise(index + 1)
            for group in outs:
                tile_copy(*group, index).start()

        project_back(count - 1)
        for group in outs:
            tile_copy(*group, count - 1).start()
        for group in outs:
            wait_all(tiles(*group))


def feed_forward_other(
    bits, length, c_low, grad_mlp, other_vec, vec, grad_c, middle, cot, proj, kept, fc, ow, proj_pieces
):
    slots, model = c_low.shape
    width = proj.shape[0]
    units = fc[0].shape[1]
    steps = units // HIDDEN
    tokens = slots // TILE
    dma = pltpu.SemaphoreType.DMA
    return call(
        functools.partial(mlp_other_kernel, steps),
        "feed_forward_other",
        steps,
        [(bits, SMEM), (length, SMEM), (c_low, HBM), (grad_mlp, HBM)]
        + [(value, whole(value.shape)) for value in (other_vec, vec)]
        + [(value, HBM) for value in (grad_c, middle, cot, proj, *kept, *fc, *ow, *proj_pieces)],
        [
            ((slots, width), BF, KEPT),
            *[(value.shape, BF, KEPT) for value in kept],
            ((3, model), F32, whole((3, model))),
            ((slots, units), BF, column_tile(slots, HIDDEN)),
            ((slots, model), F32, HBM),
            ((slots, model), BF, HBM),
            ((slots, width), BF, HBM),
        ],
        [
            pltpu.VMEM((slots, model), F32),
            pltpu.VMEM((1, units), F32),
            pltpu.VMEM((model, units), BF),
            pltpu.VMEM((units, model), BF),
            pltpu.VMEM((slots, model), BF),
            pltpu.VMEM((slots, model), BF),
            pltpu.VMEM((slots, model), BF),
            pltpu.VMEM((slots, model), F32),
            pltpu.VMEM((slots, model), BF),
            pltpu.VMEM((width, model), BF),
            pltpu.VMEM((slots, model), F32),
            pltpu.VMEM((slots, model), BF),
            pltpu.VMEM((TILE, model), BF),
            pltpu.VMEM((slots, width), BF),
            pltpu.VMEM((width, model), BF),
            dma((3, 4)),
            dma((6,)),
            dma((2,)),
            dma((3, tokens)),
        ],
        6 * slots * model * units + 4 * slots * model * width,
        34,
    )


def output_kernel(vec_ref, act_ref, ow_ref, middle_ref, y_ref):
    mlp = dot(act_ref[tile_of(pl.program_id(0)), :], ow_ref[...]) + vec_ref[BIAS_O : BIAS_O + 1, :]
    y_ref[...] = (middle_ref[...] + BRANCH * mlp).astype(BF)


def block_result(vec, act, ow, middle):
    slots, model = middle.shape
    return call(
        output_kernel,
        "output",
        slots // TILE,
        [(vec, whole(vec.shape)), (act, KEPT), (ow, KEPT), (middle, row_tile(model))],
        [((slots, model), BF, row_tile(model))],
        [],
        2 * slots * model * act.shape[1],
        5,
    )[0]


def backward_pairs(length, qkv_ref, do_ref, ctxt_ref, lse_ref, d_ref, scratch, sources):
    (
        ka_ref,
        qa_ref,
        do_mask_ref,
        kt_ref,
        qt_ref,
        dot_ref,
        delta_ref,
        dqt_ref,
        dkt_ref,
        dvt_ref,
        score_ref,
        grad_ref,
        prob_ref,
        slope_ref,
    ) = scratch
    slots, width = do_ref.shape
    causal = causal_fill()
    blocks = slots // TILE

    @pl.loop(0, width // 128)
    def _(pair):
        lanes = pair_lanes(pair)
        wait_all(sources(pair))
        keys_low = qkv_ref[:, pair_lanes(pair, width)]
        queries = qkv_ref[:, lanes]
        masked_pair(keys_low, queries, length, ka_ref, qa_ref)
        grads = do_ref[:, lanes]
        lane = lax.broadcasted_iota(jnp.int32, (slots, 128), 1)
        for half in (0, 1):
            do_mask_ref[half] = jnp.where(lane // 64 == half, grads.astype(F32), 0.0).astype(BF)
        kt_ref[...] = keys_low.T
        qt_ref[...] = queries.T
        turned = grads.T
        dot_ref[...] = turned
        product = turned.astype(F32) * ctxt_ref[lanes, :]
        for half in (0, 1):
            delta_ref[half : half + 1, :] = jnp.sum(
                product[64 * half : 64 * half + 64], 0, keepdims=True
            )
        items = block_order(blocks)

        def score(item):
            block, half = items[item]
            extent = (block + 1) * TILE
            columns = slice(block * TILE, extent)
            score_ref[item % 2, :extent, :] = dot_nt(
                ka_ref[half, :extent, :], qa_ref[half, columns, :]
            )
            grad_ref[item % 2, :extent, :] = dot_nt(
                qkv_ref[:extent, pair_lanes(pair, 2 * width)], do_mask_ref[half, columns, :]
            )

        def softmax(item):
            block, half = items[item]
            columns = slice(block * TILE, (block + 1) * TILE)
            lse = lse_ref[pl.ds(pair * 2 + half, 1), columns]
            delta = delta_ref[half : half + 1, columns]
            for inner in range(block + 1):
                keys = slice(inner * TILE, (inner + 1) * TILE)
                scores = score_ref[item % 2, keys, :]
                if inner == block:
                    scores = scores + causal
                prob = jnp.exp(scores - lse)
                slope_ref[item % 2, keys, :] = (
                    prob * (grad_ref[item % 2, keys, :] - delta)
                ).astype(BF)
                prob_ref[item % 2, keys, :] = prob.astype(BF)

        def gradients(item):
            block, half = items[item]
            extent = (block + 1) * TILE
            columns = slice(block * TILE, extent)
            rows = slice(64 * half, 64 * half + 64)
            dv_part = dot_nt(dot_ref[rows, columns], prob_ref[item % 2, :extent, :])
            dk_part = dot_nt(qt_ref[rows, columns], slope_ref[item % 2, :extent, :])
            fresh = block * TILE if half == 0 else (0 if block == blocks - 1 else extent)
            if fresh < extent:
                dvt_ref[rows, fresh:extent] = dv_part[:, fresh:]
                dkt_ref[rows, fresh:extent] = dk_part[:, fresh:]
            if fresh:
                dvt_ref[rows, :fresh] += dv_part[:, :fresh]
                dkt_ref[rows, :fresh] += dk_part[:, :fresh]
            dqt_ref[rows, columns] = dot(kt_ref[rows, :extent], slope_ref[item % 2, :extent, :])

        count_items = len(items)
        score(0)
        for item in range(count_items + 1):
            if item + 1 < count_items:
                score(item + 1)
            if item >= 1:
                gradients(item - 1)
            if item < count_items:
                softmax(item)
        d_ref[:, lanes] = (dqt_ref[...] * 0.125).astype(BF).T
        d_ref[:, pair_lanes(pair, width)] = dkt_ref[...].astype(BF).T
        d_ref[:, pair_lanes(pair, 2 * width)] = dvt_ref[...].astype(BF).T


def pair_sources(pair, width, qkv, ctxt, do, sems):
    lanes = pair_lanes(pair)
    moves = []
    for matrix in range(3):
        columns = pair_lanes(pair, matrix * width)
        moves.append((qkv[0].at[:, columns], qkv[1].at[:, columns]))
    moves.append((ctxt[0].at[lanes, :], ctxt[1].at[lanes, :]))
    if do is not None:
        moves.append((do[0].at[:, lanes], do[1].at[:, lanes]))
    return [
        pltpu.make_async_copy(source, target, sems.at[index, pair])
        for index, (source, target) in enumerate(moves)
    ]


def backward_other_kernel(
    bits_ref, length_ref, lse_ref, qkv_hbm, ctxt_hbm, do_hbm, d0_hbm, w_hbm, ow_hbm, act0_hbm, act1_hbm, *rest
):
    pieces, out_pieces, rest = rest[:4], rest[4:8], rest[8:]
    both_ref, weight_ref, ow_ref, act_ref, qkv_ref, ctxt_ref, do_ref, *rest = rest
    scratch, (sems, late_sem, w_sems, ow_sems, act_sems) = rest[:14], rest[14:]
    width = do_ref.shape[1]
    sources = lambda pair: pair_sources(
        pair, width, (qkv_hbm, qkv_ref), (ctxt_hbm, ctxt_ref), (do_hbm, do_ref), sems
    )
    for pair in range(width // 128):
        start_all(sources(pair))
    own = pl.ds(pl.multiple_of(bits_ref[3] * 3 * width, 128), 3 * width)
    other = pl.ds(pl.multiple_of((1 - bits_ref[3]) * 3 * width, 128), 3 * width)
    late = [pltpu.make_async_copy(d0_hbm, both_ref.at[:, own], late_sem)]
    late += fetch_rows([w_hbm], 0, weight_ref.at[:, own], w_sems.at[0])
    late += fetch_rows(pieces, bits_ref[1], weight_ref.at[:, other], w_sems.at[1])
    units = ow_hbm.shape[0]
    rows = pl.ds(pl.multiple_of(bits_ref[3] * units, 128), units)
    late += fetch_rows([ow_hbm], 0, ow_ref.at[rows, :], ow_sems.at[0])
    late += [pltpu.make_async_copy(act0_hbm, act_ref.at[:, rows], act_sems.at[0])]
    rows = pl.ds(pl.multiple_of((1 - bits_ref[3]) * units, 128), units)
    late += fetch_rows(out_pieces, bits_ref[4], ow_ref.at[rows, :], ow_sems.at[1])
    late += [pltpu.make_async_copy(act1_hbm, act_ref.at[:, rows], act_sems.at[1])]
    start_all(late)
    d_ref = both_ref.at[:, other]
    backward_pairs(length_ref[0], qkv_ref, do_ref, ctxt_ref, lse_ref, d_ref, scratch, sources)
    wait_all(late)


def lane_sums(value):
    total = value[:, :128]
    for start in range(128, value.shape[1], 128):
        total = total + value[:, start : start + 128]
    return jnp.sum(total.T, 0, keepdims=True)


def backward_own_kernel(
    block,
    bits_ref,
    length_ref,
    lse_ref,
    vec_ref,
    ob_ref,
    sums_ref,
    db_ref,
    do_ref,
    qkv_hbm,
    ctxt_hbm,
    at_hbm,
    gat_hbm,
    w_hbm,
    lead_ref,
    vectors_ref,
    kept_ref,
    sent_ref,
    d_out,
    qkv_ref,
    ctxt_ref,
    *rest,
):
    scratch, rest = rest[:14], rest[14:]
    d_ref, at_ref, gat_ref, w_ref, dw_ref, total_ref, sems, w_sems, late_sems, out_sem = rest
    width = do_ref.shape[1]
    model = at_ref.shape[0]
    sources = lambda pair: pair_sources(
        pair, width, (qkv_hbm, qkv_ref), (ctxt_hbm, ctxt_ref), None, sems
    )
    for pair in range(width // 128):
        start_all(sources(pair))
    late = fetch_rows([w_hbm], 0, w_ref, w_sems)
    late += [
        pltpu.make_async_copy(at_hbm, at_ref, late_sems.at[0]),
        pltpu.make_async_copy(gat_hbm, gat_ref, late_sems.at[1]),
    ]
    start_all(late)
    backward_pairs(length_ref[0], qkv_ref, do_ref, ctxt_ref, lse_ref, d_ref, scratch, sources)
    saved = pltpu.make_async_copy(d_ref, d_out, out_sem)
    saved.start()
    lead_ref[...] = jnp.zeros(lead_ref.shape, F32)
    wait_all(late)
    low = ctxt_ref[...].astype(BF)
    dw_ref[:, 3 * width :] = dot(low, gat_ref[...]).T.astype(BF)
    total_ref[...] = jnp.zeros(total_ref.shape, F32)

    @pl.loop(0, d_ref.shape[0] // TILE)
    def _(index):
        total_ref[...] += jnp.sum(d_ref[tile_of(index), :].astype(F32), 0, keepdims=True)

    sums = total_ref[...]

    @pl.loop(0, model // TILE)
    def _(index):
        rows = tile_of(index)
        part = dot(at_ref[rows, :], d_ref[...])
        dw_ref[rows, : 3 * width] = part.astype(BF)
        weight = w_ref[rows, :].astype(F32)
        lead_ref[0:1, rows] = lane_sums(part * weight)
        lead_ref[1:2, rows] = lane_sums(weight * sums)

    halves(dw_ref, bits_ref[2], block, kept_ref, sent_ref)
    scaled, shift = lead_ref[0:1, :], lead_ref[1:2, :]
    gain1, shift1 = vec_ref[GAIN1 : GAIN1 + 1, :], vec_ref[SHIFT1 : SHIFT1 + 1, :]
    vectors_ref[...] = jnp.zeros(vectors_ref.shape, F32)
    lead_ref[0:1, :] = (scaled - shift1 * shift) / gain1
    vectors_ref[2:3, :] = ob_ref[...]
    vectors_ref[3:6, :] = sums_ref[...]
    for index in range(2):
        vectors_ref[6 + index : 7 + index, :] = db_ref[:, index * model : (index + 1) * model]
    vectors_ref[8:9, :width] = sums[:, :width]
    vectors_ref[8:9, width:] = sums[:, 2 * width :]
    saved.wait()


def backward_scratch(slots):
    return [
        pltpu.VMEM((2, slots, 128), BF),
        pltpu.VMEM((2, slots, 128), BF),
        pltpu.VMEM((2, slots, 128), BF),
        pltpu.VMEM((128, slots), BF),
        pltpu.VMEM((128, slots), BF),
        pltpu.VMEM((128, slots), BF),
        pltpu.VMEM((2, slots), F32),
        pltpu.VMEM((128, slots), F32),
        pltpu.VMEM((128, slots), F32),
        pltpu.VMEM((128, slots), F32),
        pltpu.VMEM((2, slots, TILE), F32),
        pltpu.VMEM((2, slots, TILE), F32),
        pltpu.VMEM((2, slots, TILE), BF),
        pltpu.VMEM((2, slots, TILE), BF),
    ]


def attention_backward_other(
    bits, length, lse, qkv, ctxt, do, d0, weight, ow, act0, act1, pieces, out_pieces
):
    slots, width = do.shape
    model = weight.shape[1]
    dma = pltpu.SemaphoreType.DMA
    ins = [(bits, SMEM), (length, SMEM), (lse, whole(lse.shape))]
    ins += [(value, HBM) for value in (qkv, ctxt, do, d0, weight, ow, act0, act1)]
    ins += [(value, HBM) for value in (*pieces, *out_pieces)]
    return call(
        backward_other_kernel,
        "attention_backward_other",
        1,
        ins,
        [
            ((slots, 6 * width), BF, KEPT),
            ((model, 6 * width), BF, KEPT),
            ((2 * ow.shape[0], model), BF, KEPT),
            ((slots, 2 * ow.shape[0]), BF, KEPT),
        ],
        [
            pltpu.VMEM((slots, 3 * width), BF),
            pltpu.VMEM((width, slots), F32),
            pltpu.VMEM((slots, width), BF),
            *backward_scratch(slots),
            dma((5, width // 128)),
            dma,
            dma((2, 12)),
            dma((2, 4)),
            dma((2,)),
        ],
        9 * slots * slots * width,
        12,
    )


def attention_backward_own(bits, length, block, lse, vec, sums, do, qkv, ctxt, at, gat, weight):
    slots, width = do.shape
    model = at.shape[0]
    dma = pltpu.SemaphoreType.DMA
    ins = [(bits, SMEM), (length, SMEM)]
    ins += [(value, whole(value.shape)) for value in (lse, vec, *sums)]
    ins += [(do, KEPT)] + [(value, HBM) for value in (qkv, ctxt, at, gat, weight)]
    outs = [((rows, model), F32, KEPT) for rows in (8, 16)] + [((model // 2, 4 * width), BF, KEPT)] * 2
    outs += [((slots, 3 * width), BF, HBM)]
    return call(
        functools.partial(backward_own_kernel, block),
        "attention_backward_own",
        1,
        ins,
        outs,
        [
            pltpu.VMEM((slots, 3 * width), BF),
            pltpu.VMEM((width, slots), F32),
            *backward_scratch(slots),
            pltpu.VMEM((slots, 3 * width), BF),
            pltpu.VMEM((model, slots), BF),
            pltpu.VMEM((slots, model), BF),
            pltpu.VMEM((model, 3 * width), BF),
            pltpu.VMEM((model, 4 * width), BF),
            pltpu.VMEM((1, 3 * width), F32),
            dma((4, width // 128)),
            dma((3,)),
            dma((2,)),
            dma,
        ],
        9 * slots * slots * width + 8 * slots * model * width,
        21,
    )


def final_kernel(vec_ref, d_ref, w_ref, x_hbm, gmid_hbm, gin_out, *rest):
    x_ref, gmid_ref, gin_ref, product_ref, x_sems, gmid_sems, gin_sems = rest
    x_in = tiles(x_hbm, x_ref, x_sems)
    gmid_in = tiles(gmid_hbm, gmid_ref, gmid_sems)
    gin_tiles = tiles(gin_ref, gin_out, gin_sems)
    start_all(x_in + gmid_in)
    count = len(x_in)

    def product(index):
        return dot_nt(d_ref[tile_of(index), :], w_ref[...])

    def norm(index):
        rows = tile_of(index)
        normed, inverse = norm_parts(x_ref[rows, :].astype(F32))
        back = norm_back(product_ref[...], normed, inverse, vec_ref[GAIN1 : GAIN1 + 1, :])
        gin_ref[rows, :] = gmid_ref[rows, :] + back

    product_ref[...] = product(0)
    wait_all(x_in + gmid_in)

    @pl.loop(0, count - 1)
    def _(index):
        norm(index)
        product_ref[...] = product(index + 1)
        tile_copy(gin_ref, gin_out, gin_sems, index).start()

    norm(count - 1)
    gin_tiles[-1].start()
    wait_all(gin_tiles)


def gradient_of_input(vec, both, weight, x, gmid):
    slots, model = x.shape
    tokens = slots // TILE
    dma = pltpu.SemaphoreType.DMA
    return call(
        final_kernel,
        "final",
        1,
        [(vec, whole(vec.shape)), (both, KEPT), (weight, KEPT), (x, HBM), (gmid, HBM)],
        [((slots, model), F32, HBM)],
        [
            pltpu.VMEM((slots, model), BF),
            pltpu.VMEM((slots, model), F32),
            pltpu.VMEM((slots, model), F32),
            pltpu.VMEM((TILE, model), F32),
            dma((tokens,)),
            dma((tokens,)),
            dma((tokens,)),
        ],
        2 * slots * model * both.shape[1],
        13,
    )[0]


def across(value):
    return lax.ppermute(value, "tensor", [(0, 1), (1, 0)])


def swap(value, bit):
    count = lax.axis_size("dp")
    return lax.ppermute(value, "dp", [(i, i ^ bit) for i in range(count)])


def tie(*values):
    return lax.optimization_barrier(values)


def pick(value, index, axis):
    return lax.dynamic_index_in_dim(value, index, axis, keepdims=False)


def split_rows(value, count):
    shape = value.shape
    return value.reshape(*shape[:-2], count, shape[-2] // count, shape[-1])


class Reduction:
    def __init__(self, kept, first_bit, order):
        self.order = order
        self.bits = [bit for bit in reversed(range(len(order) + 1)) if bit != first_bit]
        rows = kept.shape[0] >> len(self.bits)
        self.kept = kept.reshape(*[2] * len(self.bits), rows, kept.shape[1])

    def advance(self, got):
        got = got.reshape(self.kept.shape)
        self.bit = self.order.pop(0)
        axis = self.bits.index(self.bit)
        self.bits.remove(self.bit)
        side = (lax.axis_index("dp") >> self.bit) & 1

        def part(index):
            total = pick(self.kept, index, axis).astype(F32) + pick(got, index, axis).astype(F32)
            return total.astype(BF)

        sent = part(1 - side)
        self.kept = part(side)
        return sent.reshape(-1, sent.shape[-1])

    def finish(self, got):
        return self.kept.astype(F32) + got.reshape(self.kept.shape).astype(F32)


def local(
    block_input,
    first_gain,
    first_shift,
    qkv_weight,
    qv_bias,
    proj_weight,
    proj_bias,
    second_gain,
    second_shift,
    fc_weight,
    fc_bias,
    out_weight,
    out_bias,
    cotangent,
    lengths,
):
    slots, model = block_input.shape
    width = qkv_weight.shape[2]
    units = fc_weight.shape[1]
    shards = lax.axis_size("dp")
    levels = shards.bit_length() - 1
    share = model // shards
    first_bit = next(bit for bit in range(levels) if (share << bit) % 16 == 0)
    block = share << first_bit
    later = [bit for bit in range(levels) if bit != first_bit]
    order_a = list(later)
    order_b = [later[1], later[0]] + later[2:]
    place = lax.axis_index("dp")
    quarter = jnp.bitwise_and(place, 3)
    one_bit = jnp.bitwise_and(place, 1)
    bits = jnp.stack(
        [
            one_bit,
            quarter,
            (place >> first_bit) & 1,
            lax.axis_index("tensor"),
            ((place >> 2) & 1) * 2 + one_bit,
        ]
    ).astype(jnp.int32)
    length = lengths.astype(jnp.int32)

    qkv_mine = across(pick(split_rows(qkv_weight, 4), quarter, 1))
    vectors = (first_gain, first_shift, proj_bias, second_gain, second_shift, out_bias)
    (
        vec,
        qkv0,
        grad_mlp,
        grad_mlp_turned,
        grad_out_bias,
        a_low,
        a_turned,
        proj_send,
        fc_send,
        out_send,
    ) = project(
        bits,
        length,
        block_input,
        cotangent,
        (*vectors, qv_bias, fc_bias),
        qkv_weight,
        proj_weight,
        fc_weight,
        out_weight,
    )

    fc_mine = across(fc_send)
    proj_got = across(proj_send)
    qkv_mine, qkv0 = tie(qkv_mine, qkv0)
    qkv_side = swap(qkv_mine, 2)
    qkv_core = swap(qkv_mine, 1)
    lse0, ctx0, ctxt0, qkv0 = attention_forward_own(length, qkv0)

    qkv_side, qkv_core, proj_got, ctx0, out_send = tie(
        qkv_side, qkv_core, proj_got, ctx0, out_send
    )
    half_rows = width // 2
    parts = proj_got[half_rows : half_rows + 24].astype(F32).reshape(3, 8, model)
    other_vec = (parts[0] + parts[1]) + parts[2]
    proj_other = [proj_got, swap(proj_got, 1)]
    qkv_other = [qkv_mine, qkv_core, qkv_side, swap(qkv_side, 1)]
    out_mine = across(out_send)
    lse1, c_low, c_turned, middle, ctxt1, qkv1 = attention_forward_other(
        bits,
        length,
        other_vec,
        vec,
        a_low,
        block_input,
        ctx0,
        proj_weight,
        qkv_other,
        proj_other,
    )

    c_low, fc_mine, out_mine = tie(c_low, fc_mine, out_mine)
    fc_side = swap(fc_mine, 2)
    fc_core = swap(fc_mine, 1)
    out_side = swap(out_mine, 4)
    out_core = swap(out_mine, 1)
    gc0, act0, fc_kept, out_kept, fc_sent, out_sent, grad_fc_bias, c_low, grad_mlp = feed_forward_own(
        bits, block, c_low, grad_mlp, c_turned, grad_mlp_turned, vec, fc_weight, out_weight
    )

    fc_sent, out_sent, fc_side, fc_core, out_side, out_core = tie(
        fc_sent, out_sent, fc_side, fc_core, out_side, out_core
    )
    fc_other = [fc_mine, fc_core, fc_side, swap(fc_side, 1)]
    out_other = [out_mine, out_core, out_side, swap(out_side, 1)]
    fc_got = swap(fc_sent, 1 << first_bit)
    out_got = swap(out_sent, 1 << first_bit)
    do0, fc_kept, out_kept, sums2, act1, grad_middle, grad_attn, do1 = feed_forward_other(
        bits,
        length,
        c_low,
        grad_mlp,
        other_vec,
        vec,
        gc0,
        middle,
        cotangent,
        proj_weight,
        (fc_kept, out_kept),
        fc_other,
        out_other,
        proj_other,
    )

    fc_sum = Reduction(fc_kept, first_bit, list(order_a))
    out_sum = Reduction(out_kept, first_bit, list(order_b))
    do0, fc_got, out_got = tie(do0, fc_got, out_got)
    fc_sent = fc_sum.advance(fc_got)
    out_sent = out_sum.advance(out_got)
    do0, fc_sent, out_sent = tie(do0, fc_sent, out_sent)
    fc_got = swap(fc_sent, 1 << fc_sum.bit)
    out_got = swap(out_sent, 1 << out_sum.bit)
    lead, vectors, kept, sent, d0 = attention_backward_own(
        bits,
        length,
        block,
        lse0,
        vec,
        (grad_out_bias, sums2, grad_fc_bias),
        do0,
        qkv0,
        ctxt0,
        a_turned,
        grad_attn,
        qkv_weight,
    )

    sent, lead, fc_got, out_got = tie(sent, lead, fc_got, out_got)
    attn_got = swap(sent, 1 << first_bit)
    lead_got = across(lead)
    fc_sent = fc_sum.advance(fc_got)
    out_sent = out_sum.advance(out_got)
    fc_got = swap(fc_sent, 1 << fc_sum.bit)
    out_got = swap(out_sent, 1 << out_sum.bit)

    def rounded(vectors):
        return lax.reduce_precision(vectors, 8, 7)

    def join(vectors, got):
        return rounded(vectors) + got.astype(F32)

    vectors = jnp.concatenate([(lead + lead_got)[:2], vectors[2:]], 0)
    lines = vectors.shape[0]
    vectors = join(vectors, swap(vectors.astype(BF), 1 << first_bit))
    first_sum = Reduction(kept[:, :model], first_bit, list(order_a))
    second_sum = Reduction(kept[:, model:], first_bit, list(order_b))
    first_sent = jnp.concatenate(
        [first_sum.advance(attn_got[:, :model]), vectors.astype(BF)], 0
    )
    second_sent = second_sum.advance(attn_got[:, model:])
    first_sent, second_sent, qkv1 = tie(first_sent, second_sent, qkv1)
    first_got = swap(first_sent, 1 << first_sum.bit)
    second_got = swap(second_sent, 1 << second_sum.bit)
    both, weights, ow, act = attention_backward_other(
        bits,
        length,
        lse1,
        qkv1,
        ctxt1,
        do1,
        d0,
        qkv_weight,
        out_weight,
        act0,
        act1,
        qkv_other,
        out_other,
    )

    both, fc_got, out_got, first_got, second_got = tie(both, fc_got, out_got, first_got, second_got)
    vectors = join(vectors, first_got[-lines:])
    first_sent = jnp.concatenate(
        [first_sum.advance(first_got[:-lines]), vectors.astype(BF)], 0
    )
    second_sent = second_sum.advance(second_got)
    rest_sent = jnp.concatenate([fc_sum.advance(fc_got), out_sum.advance(out_got)], 0)
    both, first_sent, second_sent, rest_sent = tie(both, first_sent, second_sent, rest_sent)
    first_got = swap(first_sent, 1 << first_sum.bit)
    second_got = swap(second_sent, 1 << second_sum.bit)
    rest_got = swap(rest_sent, 1 << fc_sum.bit)
    grad_input = gradient_of_input(vec, both, weights, block_input, grad_middle)

    grad_input, first_got, second_got, act = tie(grad_input, first_got, second_got, act)
    for level in range(3, levels):
        vectors = join(vectors, first_got[-lines:])
        sent = [first_sum.advance(first_got[:-lines]), second_sum.advance(second_got)]
        rows = sent[0].shape[0]
        sent = jnp.concatenate([*sent, vectors.astype(BF)], 0)
        sent, act = tie(sent, act)
        got = swap(sent, 1 << first_sum.bit)
        first_got = jnp.concatenate([got[:rows], got[2 * rows :]], 0)
        second_got = got[rows : 2 * rows]
        if fc_sum.order:
            rows = rest_got.shape[0] // 2
            rest_sent = [fc_sum.advance(rest_got[:rows]), out_sum.advance(rest_got[rows:])]
            rest_got = swap(jnp.concatenate(rest_sent, 0), 1 << fc_sum.bit)
    block_output = block_result(vec, act, ow, middle)
    vectors = join(vectors, first_got[-lines:])
    first = first_sum.finish(first_got[:-lines])
    second = second_sum.finish(second_got)
    rows = rest_got.shape[0] // 2
    grad_fc_weight = fc_sum.finish(rest_got[:rows])
    grad_out_weight = out_sum.finish(rest_got[rows:]).T
    grad_qkv_weight = jnp.stack([first[:, :width], first[:, width:], second[:, :width]])
    grad_proj_weight = second[:, width:].T
    return (
        block_output,
        grad_input,
        vectors[0],
        vectors[1],
        grad_qkv_weight,
        vectors[8].reshape(2, width),
        grad_proj_weight,
        vectors[5],
        vectors[3],
        vectors[4],
        grad_fc_weight,
        vectors[6:8].reshape(units),
        grad_out_weight,
        vectors[2],
    )


def solution(mesh):
    placed = (
        P("dp", None),
        P(),
        P(),
        P(None, None, "tensor"),
        P(None, "tensor"),
        P("tensor", None),
        P(),
        P(),
        P(),
        P(None, "tensor"),
        P("tensor"),
        P("tensor", None),
        P(),
        P("dp", None),
        P("dp"),
    )
    return jax.shard_map(
        local,
        mesh=mesh,
        in_specs=placed,
        out_specs=(
            P("dp", None),
            P("dp", None),
            P(),
            P(),
            P(None, "dp", "tensor"),
            P(None, "tensor"),
            P("tensor", "dp"),
            P(),
            P(),
            P(),
            P("dp", "tensor"),
            P("tensor"),
            P("tensor", "dp"),
            P(),
        ),
        check_vma=False,
    )
```

```python
import functools

import jax
import jax.numpy as jnp
from jax import lax
from jax.experimental import pallas as pl
from jax.experimental.pallas import tpu as pltpu
from jax.sharding import PartitionSpec as P

EPSILON = 1e-05
BRANCH = 48 ** (-0.5)
GELU = 0.7978845608028654
CUBIC = 0.044715
FILL = -1e30
BF = jnp.bfloat16
F32 = jnp.float32
MIB = 1024 * 1024
TILE = 256
HIDDEN = 512
GAIN1, SHIFT1, BIAS_P, GAIN2, SHIFT2, BIAS_O = range(6)
BIAS_QV, BIAS_FC = 8, 9


def dot(left, right):
    return lax.dot_general(left, right, (((1,), (0,)), ((), ())), preferred_element_type=F32)


def dot_nt(left, right):
    return lax.dot_general(left, right, (((1,), (1,)), ((), ())), preferred_element_type=F32)


def norm_parts(values):
    row_mean = jnp.mean(values, -1, keepdims=True)
    centered = values - row_mean
    inverse = lax.rsqrt(jnp.mean(centered * centered, -1, keepdims=True) + EPSILON)
    return centered * inverse, inverse


def norm_back(grad_out, normed, inverse, gain):
    scaled = grad_out * gain
    inner = (
        scaled
        - jnp.mean(scaled, -1, keepdims=True)
        - normed * jnp.mean(scaled * normed, -1, keepdims=True)
    )
    return inverse * inner


def whole(shape):
    return pl.BlockSpec(shape, lambda *_: (0,) * len(shape))


def row_tile(columns):
    return pl.BlockSpec((TILE, columns), lambda i: (i, 0))


def column_tile(rows, size=TILE):
    return pl.BlockSpec((rows, size), lambda i: (0, i))


SMEM = pl.BlockSpec(memory_space=pltpu.SMEM)
HBM = pl.BlockSpec(memory_space=pl.ANY)
LOOSE = pl.BlockSpec(memory_space=pl.ANY)
KEPT = pl.BlockSpec(memory_space=pltpu.VMEM)


def call(body, name, steps, ins, outs, scratch, flops, limit=12):
    args = []
    for array, spec in ins:
        if spec is KEPT:
            array = pltpu.with_memory_space_constraint(array, pltpu.VMEM)
        elif spec is not SMEM and spec is not LOOSE:
            array = pltpu.with_memory_space_constraint(array, pltpu.HBM)
        args.append(array)
    moved = sum(a.size * a.dtype.itemsize for a, spec in ins if spec is not KEPT)
    moved += sum(
        jax.ShapeDtypeStruct(shape, dtype).size * jnp.dtype(dtype).itemsize
        for shape, dtype, spec in outs
        if spec is not KEPT
    )
    return pl.pallas_call(
        body,
        name=name,
        grid=(steps,),
        out_shape=tuple(
            (pltpu.VMEM if spec is KEPT else pltpu.HBM)(shape, dtype) for shape, dtype, spec in outs
        ),
        in_specs=[spec for _, spec in ins],
        out_specs=tuple(spec for _, _, spec in outs),
        scratch_shapes=scratch,
        compiler_params=pltpu.CompilerParams(vmem_limit_bytes=limit * MIB),
        cost_estimate=pl.CostEstimate(flops=flops, bytes_accessed=moved, transcendentals=0),
    )(*args)


def tile_of(step):
    return pl.ds(pl.multiple_of(step * TILE, TILE), TILE)


def fetch_rows(pieces, turn, target, sems):
    copies = []
    for index, piece in enumerate(pieces):
        rows = piece.shape[-2]
        if len(pieces) > 1:
            place = jnp.bitwise_xor(jnp.int32(index), turn)
            where = pl.ds(pl.multiple_of(place * rows, 32), rows)
        else:
            where = slice(None)
        if len(piece.shape) == 2:
            copies.append(pltpu.make_async_copy(piece, target.at[where, :], sems.at[index]))
            continue
        width = piece.shape[2]
        for matrix in range(3):
            columns = slice(matrix * width, (matrix + 1) * width)
            copies.append(
                pltpu.make_async_copy(
                    piece.at[matrix], target.at[where, columns], sems.at[3 * index + matrix]
                )
            )
    return copies


def start_all(copies):
    for copy in copies:
        copy.start()


def wait_all(copies):
    for copy in copies:
        copy.wait()


def qkv_bias(biases, width):
    bias = jnp.concatenate(
        [biases[:, :width], jnp.zeros((1, width), F32), biases[:, width:]], axis=1
    )
    lane = lax.broadcasted_iota(jnp.int32, (1, 3 * width), 1)
    return bias, jnp.where(lane < width, 0.125, 1.0)


def tiles(source, target, sems, axis=0):
    copies = []
    for index in range(source.shape[axis] // TILE):
        part = slice(index * TILE, (index + 1) * TILE)
        view = (part, slice(None)) if axis == 0 else (slice(None), part)
        copies.append(pltpu.make_async_copy(source.at[view], target.at[view], sems.at[index]))
    return copies


def tile_copy(source, target, sems, index):
    rows = tile_of(index)
    return pltpu.make_async_copy(source.at[rows, :], target.at[rows, :], sems.at[index])


def clear(*refs):
    @pl.loop(0, refs[0].shape[0] // TILE)
    def _(index):
        for ref in refs:
            ref[tile_of(index), :] = jnp.zeros((TILE, ref.shape[1]), ref.dtype)


def halves(value_ref, side, block, kept_ref, sent_ref):
    for index in range(value_ref.shape[0] // (2 * block)):
        rows = slice(index * block, (index + 1) * block)
        first = 2 * block * index
        here = pl.ds(pl.multiple_of(first + block * side, 16), block)
        there = pl.ds(pl.multiple_of(first + block * (1 - side), 16), block)
        kept_ref[rows, :] = value_ref[here, :]
        sent_ref[rows, :] = value_ref[there, :]


def grad_top_of(cot, length, start):
    rows, model = cot.shape
    position = lax.broadcasted_iota(jnp.int32, (rows, 128), 0) + start
    valid = jnp.where(position < length, 1.0, 0.0)
    return cot.astype(F32) * jnp.concatenate([valid] * (model // 128), axis=1)


def project_kernel(
    bits_ref,
    x_hbm,
    gain1_ref,
    shift1_ref,
    bias_p_ref,
    gain2_ref,
    shift2_ref,
    bias_o_ref,
    qv_ref,
    fcb_ref,
    qkv_hbm,
    proj_hbm,
    fc_hbm,
    out_hbm,
    length_ref,
    cot_hbm,
    vec_ref,
    qkv_ref,
    gm_ref,
    gmt_ref,
    ob_ref,
    a_out,
    at_out,
    proj_out,
    fc_out,
    out_out,
    x_ref,
    w_ref,
    a_ref,
    at_ref,
    proj_ref,
    fc_ref,
    out_ref,
    cot_ref,
    low_ref,
    x_sems,
    w_sems,
    cot_sems,
    send_sems,
    a_sems,
    at_sems,
):
    x_in = tiles(x_hbm, x_ref, x_sems)
    x_in[0].start()
    w_in = fetch_rows([qkv_hbm], 0, w_ref, w_sems)
    start_all(w_in)
    start_all(x_in[1:])
    model = x_ref.shape[1]
    half, quarter, out_half = proj_hbm.shape[0] // 2, fc_hbm.shape[0] // 4, out_hbm.shape[0] // 2
    sends_in = []
    for index, (source, target, place, rows) in enumerate(
        (
            (proj_hbm, proj_ref.at[:half, :], bits_ref[0], half),
            (fc_hbm, fc_ref, bits_ref[1], quarter),
            (out_hbm, out_ref, bits_ref[0], out_half),
        )
    ):
        where = pl.ds(pl.multiple_of(place * rows, 32), rows)
        sends_in.append(pltpu.make_async_copy(source.at[where, :], target, send_sems.at[index]))
    start_all(sends_in)
    sends_out = [
        pltpu.make_async_copy(source, target, send_sems.at[3 + index])
        for index, (source, target) in enumerate(
            ((proj_ref, proj_out), (fc_ref, fc_out), (out_ref, out_out))
        )
    ]
    cot_in = tiles(cot_hbm, cot_ref, cot_sems)
    start_all(cot_in)
    vec_ref[...] = jnp.zeros(vec_ref.shape, F32)
    for index, ref in enumerate(
        (gain1_ref, shift1_ref, bias_p_ref, gain2_ref, shift2_ref, bias_o_ref)
    ):
        vec_ref[index : index + 1, :] = ref[...].reshape(1, model)
    width = qv_ref.shape[1]
    vec_ref[BIAS_QV : BIAS_QV + 1, :width] = qv_ref[0:1, :]
    vec_ref[BIAS_QV : BIAS_QV + 1, width:] = qv_ref[1:2, :]
    fcb = fcb_ref[...].reshape(1, fcb_ref.shape[0])
    for index in range(2):
        vec_ref[BIAS_FC + index : BIAS_FC + index + 1, :] = fcb[:, index * model : (index + 1) * model]
    value = vec_ref[8 * (BIAS_QV // 8) :, :]
    high = value.astype(BF)
    rest = value - high.astype(F32)
    mid = rest.astype(BF)
    low = (rest - mid.astype(F32)).astype(BF)
    lines = value.shape[0]
    for index, part in enumerate((high, mid, low)):
        proj_ref[half + index * lines : half + (index + 1) * lines, :] = part

    def normalize(index):
        rows = tile_of(index)
        normed, _ = norm_parts(x_ref[rows, :].astype(F32))
        low = normed * vec_ref[GAIN1 : GAIN1 + 1, :] + vec_ref[SHIFT1 : SHIFT1 + 1, :]
        low = low.astype(BF)
        low_ref[...] = low
        a_ref[rows, :] = low
        at_ref[:, rows] = low.T

    def gradient(index):
        rows = tile_of(index)
        top = grad_top_of(cot_ref[rows, :], length_ref[0], index * TILE)
        ob_ref[...] += BRANCH * jnp.sum(top, 0, keepdims=True)
        low = (BRANCH * top).astype(BF)
        gm_ref[rows, :] = low
        gmt_ref[:, rows] = low.T

    def multiply(index):
        qkv_ref[tile_of(index), :] = ((dot(low_ref[...], w_ref[...]) + bias) * scale).astype(BF)

    count = len(x_in)
    bias, scale = qkv_bias(vec_ref[BIAS_QV : BIAS_QV + 1, :], width)
    a_tiles = tiles(a_ref, a_out, a_sems)
    at_tiles = tiles(at_ref, at_out, at_sems, 1)
    ob_ref[...] = jnp.zeros(ob_ref.shape, F32)
    x_in[0].wait()
    normalize(0)
    wait_all(w_in + x_in[1:])

    @pl.loop(0, count - 1)
    def _(index):
        multiply(index)
        normalize(index + 1)

    start_all(a_tiles + at_tiles)
    wait_all(sends_in + cot_in)
    start_all(sends_out)
    multiply(count - 1)

    @pl.loop(0, count)
    def _(index):
        gradient(index)

    wait_all(sends_out + a_tiles + at_tiles)


def project(bits, length, x, cot, vectors, qkv, proj, fc, ow):
    slots, model = x.shape
    width = qkv.shape[2]
    units = fc.shape[1]
    tokens = slots // TILE
    sends = [
        (width // 2 + 32, model),
        (model // 4, units),
        (units // 2, model),
    ]
    shapes = [(slots, model), (model, slots)]
    dma = pltpu.SemaphoreType.DMA
    return call(
        project_kernel,
        "project_own",
        1,
        [(bits, SMEM), (x, HBM)]
        + [(vector, whole(vector.shape)) for vector in vectors]
        + [(weight, HBM) for weight in (qkv, proj, fc, ow)]
        + [(length, SMEM), (cot, HBM)],
        [
            ((16, model), F32, whole((16, model))),
            ((slots, 3 * width), BF, KEPT),
            ((slots, model), BF, KEPT),
            ((model, slots), BF, KEPT),
            ((1, model), F32, whole((1, model))),
        ]
        + [(shape, BF, HBM) for shape in shapes + sends],
        [pltpu.VMEM((slots, model), BF), pltpu.VMEM((model, 3 * width), BF)]
        + [pltpu.VMEM(shape, BF) for shape in shapes + sends]
        + [pltpu.VMEM((slots, model), BF), pltpu.VMEM((TILE, model), BF)]
        + [dma((tokens,)), dma((3,)), dma((tokens,)), dma((6,)), dma((tokens,)), dma((tokens,))],
        6 * slots * model * width,
        13,
    )


def causal_fill():
    keys = lax.broadcasted_iota(jnp.int32, (TILE, TILE), 0)
    queries = lax.broadcasted_iota(jnp.int32, (TILE, TILE), 1)
    return jnp.where(keys <= queries, 0.0, FILL)


def masked_pair(pair_keys, pair_queries, length, keys_ref, queries_ref):
    slots = pair_keys.shape[0]
    lane = lax.broadcasted_iota(jnp.int32, (slots, 128), 1)
    position = lax.broadcasted_iota(jnp.int32, (slots, 128), 0)
    fill = jnp.where(position < length, 0.0, FILL)
    pair_keys = pair_keys.astype(F32)
    pair_queries = pair_queries.astype(F32)
    for half in (0, 1):
        spare = 64 * (1 - half)
        keys_ref[half] = jnp.where(lane == spare, fill, pair_keys).astype(BF)
        queries_ref[half] = jnp.where(
            lane // 64 == half, pair_queries, jnp.where(lane == spare, 1.0, 0.0)
        ).astype(BF)


def block_order(blocks):
    return [(block, 0) for block in range(blocks)] + [(block, 1) for block in reversed(range(blocks))]


def pair_lanes(pair, offset=0):
    return pl.ds(pl.multiple_of(offset + pair * 128, 128), 128)


def forward_pairs(length, qkv_ref, ctx_ref, ctxt_ref, lse_ref, scratch, results):
    ka_ref, qa_ref, vt_ref, score_ref, expo_ref = scratch
    width, slots = ctxt_ref.shape
    causal = causal_fill()

    @pl.loop(0, width // 128)
    def _(pair):
        lanes = pair_lanes(pair)
        masked_pair(
            qkv_ref[:, pair_lanes(pair, width)], qkv_ref[:, lanes], length, ka_ref, qa_ref
        )
        vt_ref[...] = qkv_ref[:, pair_lanes(pair, 2 * width)].T
        items = block_order(slots // TILE)
        state = {}

        def score(item):
            block, half = items[item]
            extent = (block + 1) * TILE
            columns = slice(block * TILE, extent)
            scores = dot_nt(ka_ref[half, :extent, :], qa_ref[half, columns, :])
            high = None
            for inner in range(block + 1):
                keys = slice(inner * TILE, (inner + 1) * TILE)
                part = scores[keys]
                if inner == block:
                    part = part + causal
                score_ref[item % 2, keys, :] = part
                most = jnp.max(part.reshape(TILE // 8, 8, TILE), 0)
                high = most if high is None else jnp.maximum(high, most)
            state[item] = jnp.max(high, 0, keepdims=True)

        def exponential(item):
            block, half = items[item]
            high = state[item]
            total = None
            for inner in range(block + 1):
                keys = slice(inner * TILE, (inner + 1) * TILE)
                expo = jnp.exp(score_ref[item % 2, keys, :] - high)
                part = jnp.sum(expo.reshape(TILE // 8, 8, TILE), 0)
                total = part if total is None else total + part
                expo_ref[item % 2, keys, :] = expo.astype(BF)
            state[item] = (high, jnp.sum(total, 0, keepdims=True))

        def mix(item):
            block, half = items[item]
            extent = (block + 1) * TILE
            columns = slice(block * TILE, extent)
            high, total = state[item]
            mixed = dot(vt_ref[64 * half : 64 * half + 64, :extent], expo_ref[item % 2, :extent, :])
            row = pl.multiple_of(pair * 128 + half * 64, 64)
            ctxt_ref[pl.ds(row, 64), columns] = mixed * (1.0 / total)
            lse_ref[pl.ds(pair * 2 + half, 1), columns] = high + jnp.log(total)

        count = len(items)
        score(0)
        for item in range(count + 1):
            if item + 1 < count:
                score(item + 1)
            if item >= 1:
                mix(item - 1)
            if item < count:
                exponential(item)
        ctx_ref[:, lanes] = ctxt_ref[lanes, :].T.astype(BF)
        start_all(results(pair))


def forward_own_kernel(
    length_ref, qkv_ref, lse_ref, ctx_out, ctxt_out, qkv_out, ctx_ref, ctxt_ref, *rest
):
    scratch, sems = rest[:5], rest[5]
    saved = pltpu.make_async_copy(qkv_ref, qkv_out, sems.at[2, 0])
    saved.start()

    def results(pair):
        lanes = pair_lanes(pair)
        return [
            pltpu.make_async_copy(ctx_ref.at[:, lanes], ctx_out.at[:, lanes], sems.at[0, pair]),
            pltpu.make_async_copy(ctxt_ref.at[lanes, :], ctxt_out.at[lanes, :], sems.at[1, pair]),
        ]

    forward_pairs(length_ref[0], qkv_ref, ctx_ref, ctxt_ref, lse_ref, scratch, results)
    for pair in range(ctx_ref.shape[1] // 128):
        wait_all(results(pair))
    saved.wait()


def forward_other_kernel(
    bits_ref, length_ref, other_vec_ref, vec_ref, a_hbm, x_hbm, ctx0_hbm, proj0_hbm, *rest
):
    pieces, proj_pieces, rest = rest[:4], rest[4:6], rest[6:]
    lse_ref, c_ref, ct_ref, middle_out, ctxt_out, qkv_out, *rest = rest
    both_ref, ctxt_ref, *rest = rest
    scratch, rest = rest[:5], rest[5:]
    qkv_ref, a_ref, w_ref, x_ref, proj_ref, middle_ref, sum_ref, *rest = rest
    a_sems, w_sems, qkv_sems, sems, late_sems, proj_sems, middle_sems = rest
    slots, width = ctx0_hbm.shape
    own = pl.ds(pl.multiple_of(bits_ref[3] * width, 128), width)
    other = pl.ds(pl.multiple_of((1 - bits_ref[3]) * width, 128), width)
    ctx_ref = both_ref.at[:, other]
    w_in = fetch_rows(pieces, bits_ref[1], w_ref, w_sems)
    start_all(w_in)
    a_in = tiles(a_hbm, a_ref, a_sems)
    start_all(a_in)
    late = [
        pltpu.make_async_copy(source, target, late_sems.at[index])
        for index, (source, target) in enumerate(
            ((x_hbm, x_ref), (ctx0_hbm, both_ref.at[:, own]), (proj0_hbm, proj_ref.at[own, :]))
        )
    ]
    halves_in = [piece.at[: width // 2, :] for piece in proj_pieces]
    late += fetch_rows(halves_in, bits_ref[0], proj_ref.at[other, :], proj_sems)
    start_all(late)
    bias, scale = qkv_bias(other_vec_ref[0:1, :], width)
    qkv_tiles = tiles(qkv_ref, qkv_out, qkv_sems)
    wait_all(w_in + a_in)

    @pl.loop(0, len(a_in))
    def _(index):
        rows = tile_of(index)
        product = dot(a_ref[rows, :], w_ref[...])
        qkv_ref[rows, :] = ((product + bias) * scale).astype(BF)

    start_all(qkv_tiles)

    def results(pair):
        lanes = pair_lanes(pair)
        return [
            pltpu.make_async_copy(ctxt_ref.at[lanes, :], ctxt_out.at[lanes, :], sems.at[pair])
        ]

    forward_pairs(length_ref[0], qkv_ref, ctx_ref, ctxt_ref, lse_ref, scratch, results)
    wait_all(late)
    count = slots // TILE

    def branch(index):
        return dot(both_ref[tile_of(index), :], proj_ref[...])

    def normalize(index):
        rows = tile_of(index)
        total = sum_ref[...] + vec_ref[BIAS_P : BIAS_P + 1, :]
        middle = x_ref[rows, :].astype(F32) + BRANCH * total
        middle_ref[rows, :] = middle
        normed, _ = norm_parts(middle)
        low = (normed * vec_ref[GAIN2 : GAIN2 + 1, :] + vec_ref[SHIFT2 : SHIFT2 + 1, :]).astype(BF)
        c_ref[rows, :] = low
        ct_ref[:, rows] = low.T

    sum_ref[...] = branch(0)

    @pl.loop(0, count - 1)
    def _(index):
        normalize(index)
        sum_ref[...] = branch(index + 1)
        tile_copy(middle_ref, middle_out, middle_sems, index).start()

    normalize(count - 1)
    middle_tiles = tiles(middle_ref, middle_out, middle_sems)
    middle_tiles[-1].start()
    for pair in range(width // 128):
        wait_all(results(pair))
    wait_all(qkv_tiles + middle_tiles)


def forward_scratch(slots, width):
    return [
        pltpu.VMEM((slots, width), BF),
        pltpu.VMEM((width, slots), F32),
        pltpu.VMEM((2, slots, 128), BF),
        pltpu.VMEM((2, slots, 128), BF),
        pltpu.VMEM((128, slots), BF),
        pltpu.VMEM((2, slots, TILE), F32),
        pltpu.VMEM((2, slots, TILE), BF),
    ]


def attention_forward_own(length, qkv):
    slots = qkv.shape[0]
    width = qkv.shape[1] // 3
    heads = width // 64
    return call(
        forward_own_kernel,
        "attention_forward_own",
        1,
        [(length, SMEM), (qkv, KEPT)],
        [
            ((heads, slots), F32, whole((heads, slots))),
            ((slots, width), BF, HBM),
            ((width, slots), F32, HBM),
            ((slots, 3 * width), BF, HBM),
        ],
        [*forward_scratch(slots, width), pltpu.SemaphoreType.DMA((3, width // 128))],
        6 * slots * slots * width,
        6,
    )


def attention_forward_other(bits, length, other_vec, vec, a_low, x, ctx, proj, pieces, proj_pieces):
    slots, model = x.shape
    width = ctx.shape[1]
    heads = width // 64
    tokens = slots // TILE
    dma = pltpu.SemaphoreType.DMA
    ins = [(bits, SMEM), (length, SMEM)]
    ins += [(value, whole(value.shape)) for value in (other_vec, vec)]
    ins += [(value, HBM) for value in (a_low, x, ctx, proj)]
    ins += [(value, LOOSE) for value in (*pieces, *proj_pieces)]
    return call(
        forward_other_kernel,
        "attention_forward_other",
        1,
        ins,
        [
            ((heads, slots), F32, whole((heads, slots))),
            ((slots, model), BF, KEPT),
            ((model, slots), BF, KEPT),
            ((slots, model), F32, HBM),
            ((width, slots), F32, HBM),
            ((slots, 3 * width), BF, HBM),
        ],
        [
            pltpu.VMEM((slots, 2 * width), BF),
            *forward_scratch(slots, width)[1:],
            pltpu.VMEM((slots, 3 * width), BF),
            pltpu.VMEM((slots, model), BF),
            pltpu.VMEM((model, 3 * width), BF),
            pltpu.VMEM((slots, model), BF),
            pltpu.VMEM((2 * width, model), BF),
            pltpu.VMEM((slots, model), F32),
            pltpu.VMEM((TILE, model), F32),
            dma((tokens,)),
            dma((12,)),
            dma((tokens,)),
            dma((width // 128,)),
            dma((3,)),
            dma((2,)),
            dma((tokens,)),
        ],
        6 * slots * slots * width + 10 * slots * model * width,
        20,
    )


def mlp_step(hidden, g_ref, ow):
    square = hidden * hidden
    tanh = jnp.tanh(hidden * (GELU + GELU * CUBIC * square))
    share = 0.5 + 0.5 * tanh
    value = hidden * share
    slope = share + value * (1.0 - share) * (2.0 * GELU + 6.0 * GELU * CUBIC * square)
    return value.astype(BF), (dot_nt(g_ref[...], ow) * slope).astype(BF)


def unit_bias(vec_ref, base, bias_ref):
    model = vec_ref.shape[1]
    for row in range(bias_ref.shape[1] // model):
        columns = slice(row * model, (row + 1) * model)
        bias_ref[:, columns] = vec_ref[base + row : base + row + 1, :]


def mlp_own_kernel(
    steps,
    block,
    bits_ref,
    c_ref,
    g_ref,
    ct_ref,
    gt_ref,
    vec_ref,
    fc_ref,
    ow_ref,
    gc_out,
    act_ref,
    fc_kept_ref,
    out_kept_ref,
    fc_sent_ref,
    out_sent_ref,
    db_ref,
    c_out,
    g_out,
    gc_ref,
    gc_low_ref,
    bias_ref,
    gh_ref,
    dw_ref,
    sems,
):
    saved = [
        pltpu.make_async_copy(c_ref, c_out, sems.at[1]),
        pltpu.make_async_copy(g_ref, g_out, sems.at[2]),
    ]
    step = pl.program_id(0)

    @pl.when(step == 0)
    def _():
        start_all(saved)
        unit_bias(vec_ref, BIAS_FC, bias_ref)
        clear(gc_ref)

    lanes = pl.ds(pl.multiple_of(step * HIDDEN, HIDDEN), HIDDEN)
    hidden = dot(c_ref[...], fc_ref[...]) + bias_ref[:, lanes]
    act, gh = mlp_step(hidden, g_ref, ow_ref[...])
    act_ref[...] = act
    gh_ref[...] = gh
    db_ref[...] = jnp.sum(gh.astype(F32), 0, keepdims=True)
    gc_ref[...] += dot_nt(gh, fc_ref[...])
    results = [pltpu.make_async_copy(gc_low_ref, gc_out, sems.at[0])]

    @pl.when(step == steps - 1)
    def _():
        gc_low_ref[...] = gc_ref[...].astype(BF)
        start_all(results)

    dw_ref[0] = dot(ct_ref[...], gh_ref[...]).astype(BF)
    halves(dw_ref.at[0], bits_ref[2], block, fc_kept_ref, fc_sent_ref.at[:, lanes])
    dw_ref[1] = dot(gt_ref[...], act_ref[...]).astype(BF)
    halves(dw_ref.at[1], bits_ref[2], block, out_kept_ref, out_sent_ref.at[:, lanes])

    @pl.when(step == steps - 1)
    def _():
        wait_all(results + saved)


def feed_forward_own(bits, block, c_low, grad_mlp, c_turned, grad_turned, vec, fc, ow):
    slots, model = c_low.shape
    units = fc.shape[1]
    steps = units // HIDDEN
    half = column_tile(model // 2, HIDDEN)
    return call(
        functools.partial(mlp_own_kernel, steps, block),
        "feed_forward_own",
        steps,
        [(bits, SMEM)]
        + [(value, KEPT) for value in (c_low, grad_mlp, c_turned, grad_turned)]
        + [
            (vec, whole(vec.shape)),
            (fc, column_tile(model, HIDDEN)),
            (ow, pl.BlockSpec((HIDDEN, model), lambda i: (i, 0))),
        ],
        [((slots, model), BF, HBM), ((slots, units), BF, column_tile(slots, HIDDEN))]
        + [((model // 2, units), BF, half)] * 2
        + [((model // 2, units), BF, KEPT)] * 2
        + [((1, units), F32, column_tile(1, HIDDEN))]
        + [((slots, model), BF, HBM)] * 2,
        [
            pltpu.VMEM((slots, model), F32),
            pltpu.VMEM((slots, model), BF),
            pltpu.VMEM((1, units), F32),
            pltpu.VMEM((slots, HIDDEN), BF),
            pltpu.VMEM((2, model, HIDDEN), BF),
            pltpu.SemaphoreType.DMA((3,)),
        ],
        10 * slots * model * units,
        19,
    )


def mlp_other_kernel(
    steps,
    bits_ref,
    length_ref,
    c_hbm,
    g_hbm,
    other_vec_ref,
    vec_ref,
    gc0_hbm,
    middle_hbm,
    cot_hbm,
    proj0_hbm,
    fc_kept_hbm,
    out_kept_hbm,
    *rest,
):
    fc_pieces, out_pieces, proj_pieces, rest = rest[:4], rest[4:6], rest[6:8], rest[8:]
    do0_ref, fc_kept_ref, out_kept_ref, sums_ref, act_ref, gmid_out, ga_out, do1_out, *rest = rest
    gc_ref, bias_ref, fc_ref, ow_ref, c_ref, g_ref, *rest = rest
    late_refs, (gmid_ref, ga_ref, low_ref, do1_ref, proj1_ref, *rest) = rest[:4], rest[4:]
    sems, late_sems, proj_sems, out_sems = rest
    step = pl.program_id(0)
    slots, model = c_ref.shape
    first = fetch_rows(fc_pieces, bits_ref[1], fc_ref, sems.at[0])
    first += [pltpu.make_async_copy(c_hbm, c_ref, sems.at[2, 0])]
    second = fetch_rows(out_pieces, bits_ref[0], ow_ref, sems.at[1])
    second += [pltpu.make_async_copy(g_hbm, g_ref, sems.at[2, 1])]
    late = [
        pltpu.make_async_copy(source, target, late_sems.at[index])
        for index, (source, target) in enumerate(
            zip(
                (gc0_hbm, middle_hbm, cot_hbm, proj0_hbm, fc_kept_hbm, out_kept_hbm),
                (*late_refs, fc_kept_ref, out_kept_ref),
            )
        )
    ]
    half = proj1_ref.shape[0] // 2
    halves_in = [piece.at[:half, :] for piece in proj_pieces]
    late += fetch_rows(halves_in, bits_ref[0], proj1_ref, proj_sems)

    @pl.when(step == 0)
    def _():
        start_all(first + second)
        unit_bias(other_vec_ref, 1, bias_ref)
        clear(gc_ref)
        wait_all(first + second)
        start_all(late)

    lanes = pl.ds(pl.multiple_of(step * HIDDEN, HIDDEN), HIDDEN)
    hidden = dot(c_ref[...], fc_ref[:, lanes]) + bias_ref[:, lanes]
    act, gh = mlp_step(hidden, g_ref, ow_ref[lanes, :])
    act_ref[...] = act
    gc_ref[...] += dot_nt(gh, fc_ref[:, lanes])

    @pl.when(step == steps - 1)
    def _():
        wait_all(late)
        gc0_ref, middle_ref, cot_ref, proj0_ref = late_refs
        pairs = ((gmid_ref, gmid_out), (ga_ref, ga_out), (do1_ref, do1_out))
        outs = [(*pair, out_sems.at[index]) for index, pair in enumerate(pairs)]
        count = slots // TILE
        sums_ref[...] = jnp.zeros(sums_ref.shape, F32)

        def elementwise(index):
            rows = tile_of(index)
            grad_c = gc_ref[rows, :].astype(BF).astype(F32) + gc0_ref[rows, :].astype(F32)
            normed, inverse = norm_parts(middle_ref[rows, :])
            top = grad_top_of(cot_ref[rows, :], length_ref[0], index * TILE)
            grad_middle = top + norm_back(grad_c, normed, inverse, vec_ref[GAIN2 : GAIN2 + 1, :])
            sums_ref[0:1, :] += jnp.sum(grad_c * normed, 0, keepdims=True)
            sums_ref[1:2, :] += jnp.sum(grad_c, 0, keepdims=True)
            sums_ref[2:3, :] += BRANCH * jnp.sum(grad_middle, 0, keepdims=True)
            gmid_ref[rows, :] = grad_middle
            low = (BRANCH * grad_middle).astype(BF)
            ga_ref[rows, :] = low
            low_ref[...] = low

        def project_back(index):
            rows = tile_of(index)
            do0_ref[rows, :] = dot_nt(low_ref[...], proj0_ref[...]).astype(BF)
            do1_ref[rows, :] = dot_nt(low_ref[...], proj1_ref[...]).astype(BF)

        elementwise(0)

        @pl.loop(0, count - 1)
        def _(index):
            project_back(index)
            elementwise(index + 1)
            for group in outs:
                tile_copy(*group, index).start()

        project_back(count - 1)
        for group in outs:
            tile_copy(*group, count - 1).start()
        for group in outs:
            wait_all(tiles(*group))


def feed_forward_other(
    bits, length, c_low, grad_mlp, other_vec, vec, grad_c, middle, cot, proj, kept, fc, ow, proj_pieces
):
    slots, model = c_low.shape
    width = proj.shape[0]
    units = fc[0].shape[1]
    steps = units // HIDDEN
    tokens = slots // TILE
    dma = pltpu.SemaphoreType.DMA
    return call(
        functools.partial(mlp_other_kernel, steps),
        "feed_forward_other",
        steps,
        [(bits, SMEM), (length, SMEM), (c_low, HBM), (grad_mlp, HBM)]
        + [(value, whole(value.shape)) for value in (other_vec, vec)]
        + [(value, HBM) for value in (grad_c, middle, cot, proj, *kept, *fc, *ow, *proj_pieces)],
        [
            ((slots, width), BF, KEPT),
            *[(value.shape, BF, KEPT) for value in kept],
            ((3, model), F32, whole((3, model))),
            ((slots, units), BF, column_tile(slots, HIDDEN)),
            ((slots, model), F32, HBM),
            ((slots, model), BF, HBM),
            ((slots, width), BF, HBM),
        ],
        [
            pltpu.VMEM((slots, model), F32),
            pltpu.VMEM((1, units), F32),
            pltpu.VMEM((model, units), BF),
            pltpu.VMEM((units, model), BF),
            pltpu.VMEM((slots, model), BF),
            pltpu.VMEM((slots, model), BF),
            pltpu.VMEM((slots, model), BF),
            pltpu.VMEM((slots, model), F32),
            pltpu.VMEM((slots, model), BF),
            pltpu.VMEM((width, model), BF),
            pltpu.VMEM((slots, model), F32),
            pltpu.VMEM((slots, model), BF),
            pltpu.VMEM((TILE, model), BF),
            pltpu.VMEM((slots, width), BF),
            pltpu.VMEM((width, model), BF),
            dma((3, 4)),
            dma((6,)),
            dma((2,)),
            dma((3, tokens)),
        ],
        6 * slots * model * units + 4 * slots * model * width,
        34,
    )


def output_kernel(vec_ref, act_ref, ow_ref, middle_ref, y_ref):
    mlp = dot(act_ref[tile_of(pl.program_id(0)), :], ow_ref[...]) + vec_ref[BIAS_O : BIAS_O + 1, :]
    y_ref[...] = (middle_ref[...] + BRANCH * mlp).astype(BF)


def block_result(vec, act, ow, middle):
    slots, model = middle.shape
    return call(
        output_kernel,
        "output",
        slots // TILE,
        [(vec, whole(vec.shape)), (act, KEPT), (ow, KEPT), (middle, row_tile(model))],
        [((slots, model), BF, row_tile(model))],
        [],
        2 * slots * model * act.shape[1],
        5,
    )[0]


def backward_pairs(length, qkv_ref, do_ref, ctxt_ref, lse_ref, d_ref, scratch, sources):
    (
        ka_ref,
        qa_ref,
        do_mask_ref,
        kt_ref,
        qt_ref,
        dot_ref,
        delta_ref,
        dqt_ref,
        dkt_ref,
        dvt_ref,
        score_ref,
        grad_ref,
        prob_ref,
        slope_ref,
    ) = scratch
    slots, width = do_ref.shape
    causal = causal_fill()
    blocks = slots // TILE

    @pl.loop(0, width // 128)
    def _(pair):
        lanes = pair_lanes(pair)
        wait_all(sources(pair))
        keys_low = qkv_ref[:, pair_lanes(pair, width)]
        queries = qkv_ref[:, lanes]
        masked_pair(keys_low, queries, length, ka_ref, qa_ref)
        grads = do_ref[:, lanes]
        lane = lax.broadcasted_iota(jnp.int32, (slots, 128), 1)
        for half in (0, 1):
            do_mask_ref[half] = jnp.where(lane // 64 == half, grads.astype(F32), 0.0).astype(BF)
        kt_ref[...] = keys_low.T
        qt_ref[...] = queries.T
        turned = grads.T
        dot_ref[...] = turned
        product = turned.astype(F32) * ctxt_ref[lanes, :]
        for half in (0, 1):
            delta_ref[half : half + 1, :] = jnp.sum(
                product[64 * half : 64 * half + 64], 0, keepdims=True
            )
        items = block_order(blocks)

        def score(item):
            block, half = items[item]
            extent = (block + 1) * TILE
            columns = slice(block * TILE, extent)
            score_ref[item % 2, :extent, :] = dot_nt(
                ka_ref[half, :extent, :], qa_ref[half, columns, :]
            )
            grad_ref[item % 2, :extent, :] = dot_nt(
                qkv_ref[:extent, pair_lanes(pair, 2 * width)], do_mask_ref[half, columns, :]
            )

        def softmax(item):
            block, half = items[item]
            columns = slice(block * TILE, (block + 1) * TILE)
            lse = lse_ref[pl.ds(pair * 2 + half, 1), columns]
            delta = delta_ref[half : half + 1, columns]
            for inner in range(block + 1):
                keys = slice(inner * TILE, (inner + 1) * TILE)
                scores = score_ref[item % 2, keys, :]
                if inner == block:
                    scores = scores + causal
                prob = jnp.exp(scores - lse)
                slope_ref[item % 2, keys, :] = (
                    prob * (grad_ref[item % 2, keys, :] - delta)
                ).astype(BF)
                prob_ref[item % 2, keys, :] = prob.astype(BF)

        def gradients(item):
            block, half = items[item]
            extent = (block + 1) * TILE
            columns = slice(block * TILE, extent)
            rows = slice(64 * half, 64 * half + 64)
            dv_part = dot_nt(dot_ref[rows, columns], prob_ref[item % 2, :extent, :])
            dk_part = dot_nt(qt_ref[rows, columns], slope_ref[item % 2, :extent, :])
            fresh = block * TILE if half == 0 else (0 if block == blocks - 1 else extent)
            if fresh < extent:
                dvt_ref[rows, fresh:extent] = dv_part[:, fresh:]
                dkt_ref[rows, fresh:extent] = dk_part[:, fresh:]
            if fresh:
                dvt_ref[rows, :fresh] += dv_part[:, :fresh]
                dkt_ref[rows, :fresh] += dk_part[:, :fresh]
            dqt_ref[rows, columns] = dot(kt_ref[rows, :extent], slope_ref[item % 2, :extent, :])

        count_items = len(items)
        score(0)
        for item in range(count_items + 1):
            if item + 1 < count_items:
                score(item + 1)
            if item >= 1:
                gradients(item - 1)
            if item < count_items:
                softmax(item)
        d_ref[:, lanes] = (dqt_ref[...] * 0.125).astype(BF).T
        d_ref[:, pair_lanes(pair, width)] = dkt_ref[...].astype(BF).T
        d_ref[:, pair_lanes(pair, 2 * width)] = dvt_ref[...].astype(BF).T


def pair_sources(pair, width, qkv, ctxt, do, sems):
    lanes = pair_lanes(pair)
    moves = []
    for matrix in range(3):
        columns = pair_lanes(pair, matrix * width)
        moves.append((qkv[0].at[:, columns], qkv[1].at[:, columns]))
    moves.append((ctxt[0].at[lanes, :], ctxt[1].at[lanes, :]))
    if do is not None:
        moves.append((do[0].at[:, lanes], do[1].at[:, lanes]))
    return [
        pltpu.make_async_copy(source, target, sems.at[index, pair])
        for index, (source, target) in enumerate(moves)
    ]


def backward_other_kernel(
    bits_ref, length_ref, lse_ref, qkv_hbm, ctxt_hbm, do_hbm, d0_hbm, w_hbm, ow_hbm, act0_hbm, act1_hbm, *rest
):
    pieces, out_pieces, rest = rest[:4], rest[4:6], rest[6:]
    both_ref, weight_ref, ow_ref, act_ref, qkv_ref, ctxt_ref, do_ref, *rest = rest
    scratch, (sems, late_sem, w_sems, ow_sems, act_sems) = rest[:14], rest[14:]
    width = do_ref.shape[1]
    sources = lambda pair: pair_sources(
        pair, width, (qkv_hbm, qkv_ref), (ctxt_hbm, ctxt_ref), (do_hbm, do_ref), sems
    )
    for pair in range(width // 128):
        start_all(sources(pair))
    own = pl.ds(pl.multiple_of(bits_ref[3] * 3 * width, 128), 3 * width)
    other = pl.ds(pl.multiple_of((1 - bits_ref[3]) * 3 * width, 128), 3 * width)
    late = [pltpu.make_async_copy(d0_hbm, both_ref.at[:, own], late_sem)]
    late += fetch_rows([w_hbm], 0, weight_ref.at[:, own], w_sems.at[0])
    late += fetch_rows(pieces, bits_ref[1], weight_ref.at[:, other], w_sems.at[1])
    units = ow_hbm.shape[0]
    rows = pl.ds(pl.multiple_of(bits_ref[3] * units, 128), units)
    late += fetch_rows([ow_hbm], 0, ow_ref.at[rows, :], ow_sems.at[0])
    late += [pltpu.make_async_copy(act0_hbm, act_ref.at[:, rows], act_sems.at[0])]
    rows = pl.ds(pl.multiple_of((1 - bits_ref[3]) * units, 128), units)
    late += fetch_rows(out_pieces, bits_ref[0], ow_ref.at[rows, :], ow_sems.at[1])
    late += [pltpu.make_async_copy(act1_hbm, act_ref.at[:, rows], act_sems.at[1])]
    start_all(late)
    d_ref = both_ref.at[:, other]
    backward_pairs(length_ref[0], qkv_ref, do_ref, ctxt_ref, lse_ref, d_ref, scratch, sources)
    wait_all(late)


def lane_sums(value):
    total = value[:, :128]
    for start in range(128, value.shape[1], 128):
        total = total + value[:, start : start + 128]
    return jnp.sum(total.T, 0, keepdims=True)


def backward_own_kernel(
    block,
    bits_ref,
    length_ref,
    lse_ref,
    vec_ref,
    ob_ref,
    sums_ref,
    db_ref,
    do_ref,
    qkv_hbm,
    ctxt_hbm,
    at_hbm,
    gat_hbm,
    w_hbm,
    lead_ref,
    vectors_ref,
    kept_ref,
    sent_ref,
    d_out,
    qkv_ref,
    ctxt_ref,
    *rest,
):
    scratch, rest = rest[:14], rest[14:]
    d_ref, at_ref, gat_ref, w_ref, dw_ref, total_ref, sems, w_sems, late_sems, out_sem = rest
    width = do_ref.shape[1]
    model = at_ref.shape[0]
    sources = lambda pair: pair_sources(
        pair, width, (qkv_hbm, qkv_ref), (ctxt_hbm, ctxt_ref), None, sems
    )
    for pair in range(width // 128):
        start_all(sources(pair))
    late = fetch_rows([w_hbm], 0, w_ref, w_sems)
    late += [
        pltpu.make_async_copy(at_hbm, at_ref, late_sems.at[0]),
        pltpu.make_async_copy(gat_hbm, gat_ref, late_sems.at[1]),
    ]
    start_all(late)
    backward_pairs(length_ref[0], qkv_ref, do_ref, ctxt_ref, lse_ref, d_ref, scratch, sources)
    saved = pltpu.make_async_copy(d_ref, d_out, out_sem)
    saved.start()
    lead_ref[...] = jnp.zeros(lead_ref.shape, F32)
    wait_all(late)
    low = ctxt_ref[...].astype(BF)
    dw_ref[:, 3 * width :] = dot(low, gat_ref[...]).T.astype(BF)
    total_ref[...] = jnp.zeros(total_ref.shape, F32)

    @pl.loop(0, d_ref.shape[0] // TILE)
    def _(index):
        total_ref[...] += jnp.sum(d_ref[tile_of(index), :].astype(F32), 0, keepdims=True)

    sums = total_ref[...]

    @pl.loop(0, model // TILE)
    def _(index):
        rows = tile_of(index)
        part = dot(at_ref[rows, :], d_ref[...])
        dw_ref[rows, : 3 * width] = part.astype(BF)
        weight = w_ref[rows, :].astype(F32)
        lead_ref[0:1, rows] = lane_sums(part * weight)
        lead_ref[1:2, rows] = lane_sums(weight * sums)

    halves(dw_ref, bits_ref[2], block, kept_ref, sent_ref)
    scaled, shift = lead_ref[0:1, :], lead_ref[1:2, :]
    gain1, shift1 = vec_ref[GAIN1 : GAIN1 + 1, :], vec_ref[SHIFT1 : SHIFT1 + 1, :]
    vectors_ref[...] = jnp.zeros(vectors_ref.shape, F32)
    lead_ref[0:1, :] = (scaled - shift1 * shift) / gain1
    vectors_ref[2:3, :] = ob_ref[...]
    vectors_ref[3:6, :] = sums_ref[...]
    for index in range(2):
        vectors_ref[6 + index : 7 + index, :] = db_ref[:, index * model : (index + 1) * model]
    vectors_ref[8:9, :width] = sums[:, :width]
    vectors_ref[8:9, width:] = sums[:, 2 * width :]
    saved.wait()


def backward_scratch(slots):
    return [
        pltpu.VMEM((2, slots, 128), BF),
        pltpu.VMEM((2, slots, 128), BF),
        pltpu.VMEM((2, slots, 128), BF),
        pltpu.VMEM((128, slots), BF),
        pltpu.VMEM((128, slots), BF),
        pltpu.VMEM((128, slots), BF),
        pltpu.VMEM((2, slots), F32),
        pltpu.VMEM((128, slots), F32),
        pltpu.VMEM((128, slots), F32),
        pltpu.VMEM((128, slots), F32),
        pltpu.VMEM((2, slots, TILE), F32),
        pltpu.VMEM((2, slots, TILE), F32),
        pltpu.VMEM((2, slots, TILE), BF),
        pltpu.VMEM((2, slots, TILE), BF),
    ]


def attention_backward_other(
    bits, length, lse, qkv, ctxt, do, d0, weight, ow, act0, act1, pieces, out_pieces
):
    slots, width = do.shape
    model = weight.shape[1]
    dma = pltpu.SemaphoreType.DMA
    ins = [(bits, SMEM), (length, SMEM), (lse, whole(lse.shape))]
    ins += [(value, HBM) for value in (qkv, ctxt, do, d0, weight, ow, act0, act1)]
    ins += [(value, HBM) for value in (*pieces, *out_pieces)]
    return call(
        backward_other_kernel,
        "attention_backward_other",
        1,
        ins,
        [
            ((slots, 6 * width), BF, KEPT),
            ((model, 6 * width), BF, KEPT),
            ((2 * ow.shape[0], model), BF, KEPT),
            ((slots, 2 * ow.shape[0]), BF, KEPT),
        ],
        [
            pltpu.VMEM((slots, 3 * width), BF),
            pltpu.VMEM((width, slots), F32),
            pltpu.VMEM((slots, width), BF),
            *backward_scratch(slots),
            dma((5, width // 128)),
            dma,
            dma((2, 12)),
            dma((2, 4)),
            dma((2,)),
        ],
        9 * slots * slots * width,
        12,
    )


def attention_backward_own(bits, length, block, lse, vec, sums, do, qkv, ctxt, at, gat, weight):
    slots, width = do.shape
    model = at.shape[0]
    dma = pltpu.SemaphoreType.DMA
    ins = [(bits, SMEM), (length, SMEM)]
    ins += [(value, whole(value.shape)) for value in (lse, vec, *sums)]
    ins += [(do, KEPT)] + [(value, HBM) for value in (qkv, ctxt, at, gat, weight)]
    outs = [((rows, model), F32, KEPT) for rows in (8, 16)] + [((model // 2, 4 * width), BF, KEPT)] * 2
    outs += [((slots, 3 * width), BF, HBM)]
    return call(
        functools.partial(backward_own_kernel, block),
        "attention_backward_own",
        1,
        ins,
        outs,
        [
            pltpu.VMEM((slots, 3 * width), BF),
            pltpu.VMEM((width, slots), F32),
            *backward_scratch(slots),
            pltpu.VMEM((slots, 3 * width), BF),
            pltpu.VMEM((model, slots), BF),
            pltpu.VMEM((slots, model), BF),
            pltpu.VMEM((model, 3 * width), BF),
            pltpu.VMEM((model, 4 * width), BF),
            pltpu.VMEM((1, 3 * width), F32),
            dma((4, width // 128)),
            dma((3,)),
            dma((2,)),
            dma,
        ],
        9 * slots * slots * width + 8 * slots * model * width,
        21,
    )


def final_kernel(vec_ref, d_ref, w_ref, x_hbm, gmid_hbm, gin_out, *rest):
    x_ref, gmid_ref, gin_ref, product_ref, x_sems, gmid_sems, gin_sems = rest
    x_in = tiles(x_hbm, x_ref, x_sems)
    gmid_in = tiles(gmid_hbm, gmid_ref, gmid_sems)
    gin_tiles = tiles(gin_ref, gin_out, gin_sems)
    start_all(x_in + gmid_in)
    count = len(x_in)

    def product(index):
        return dot_nt(d_ref[tile_of(index), :], w_ref[...])

    def norm(index):
        rows = tile_of(index)
        normed, inverse = norm_parts(x_ref[rows, :].astype(F32))
        back = norm_back(product_ref[...], normed, inverse, vec_ref[GAIN1 : GAIN1 + 1, :])
        gin_ref[rows, :] = gmid_ref[rows, :] + back

    product_ref[...] = product(0)
    wait_all(x_in + gmid_in)

    @pl.loop(0, count - 1)
    def _(index):
        norm(index)
        product_ref[...] = product(index + 1)
        tile_copy(gin_ref, gin_out, gin_sems, index).start()

    norm(count - 1)
    gin_tiles[-1].start()
    wait_all(gin_tiles)


def gradient_of_input(vec, both, weight, x, gmid):
    slots, model = x.shape
    tokens = slots // TILE
    dma = pltpu.SemaphoreType.DMA
    return call(
        final_kernel,
        "final",
        1,
        [(vec, whole(vec.shape)), (both, KEPT), (weight, KEPT), (x, HBM), (gmid, HBM)],
        [((slots, model), F32, HBM)],
        [
            pltpu.VMEM((slots, model), BF),
            pltpu.VMEM((slots, model), F32),
            pltpu.VMEM((slots, model), F32),
            pltpu.VMEM((TILE, model), F32),
            dma((tokens,)),
            dma((tokens,)),
            dma((tokens,)),
        ],
        2 * slots * model * both.shape[1],
        13,
    )[0]


def across(value):
    return lax.ppermute(value, "tensor", [(0, 1), (1, 0)])


def swap(value, bit):
    count = lax.axis_size("dp")
    return lax.ppermute(value, "dp", [(i, i ^ bit) for i in range(count)])


def tie(*values):
    return lax.optimization_barrier(values)


def pick(value, index, axis):
    return lax.dynamic_index_in_dim(value, index, axis, keepdims=False)


def split_rows(value, count):
    shape = value.shape
    return value.reshape(*shape[:-2], count, shape[-2] // count, shape[-1])


class Reduction:
    def __init__(self, kept, first_bit, order):
        self.order = order
        self.bits = [bit for bit in reversed(range(len(order) + 1)) if bit != first_bit]
        rows = kept.shape[0] >> len(self.bits)
        self.kept = kept.reshape(*[2] * len(self.bits), rows, kept.shape[1])

    def advance(self, got):
        got = got.reshape(self.kept.shape)
        self.bit = self.order.pop(0)
        axis = self.bits.index(self.bit)
        self.bits.remove(self.bit)
        side = (lax.axis_index("dp") >> self.bit) & 1

        def part(index):
            total = pick(self.kept, index, axis).astype(F32) + pick(got, index, axis).astype(F32)
            return total.astype(BF)

        sent = part(1 - side)
        self.kept = part(side)
        return sent.reshape(-1, sent.shape[-1])

    def finish(self, got):
        return self.kept.astype(F32) + got.reshape(self.kept.shape).astype(F32)


def local(
    block_input,
    first_gain,
    first_shift,
    qkv_weight,
    qv_bias,
    proj_weight,
    proj_bias,
    second_gain,
    second_shift,
    fc_weight,
    fc_bias,
    out_weight,
    out_bias,
    cotangent,
    lengths,
):
    slots, model = block_input.shape
    width = qkv_weight.shape[2]
    units = fc_weight.shape[1]
    shards = lax.axis_size("dp")
    levels = shards.bit_length() - 1
    share = model // shards
    first_bit = next(bit for bit in range(levels) if (share << bit) % 16 == 0)
    block = share << first_bit
    later = [bit for bit in range(levels) if bit != first_bit]
    order_a = list(later)
    order_b = [later[1], later[0]] + later[2:]
    place = lax.axis_index("dp")
    quarter = jnp.bitwise_and(place, 3)
    one_bit = jnp.bitwise_and(place, 1)
    bits = jnp.stack(
        [
            one_bit,
            quarter,
            (place >> first_bit) & 1,
            lax.axis_index("tensor"),
        ]
    ).astype(jnp.int32)
    length = lengths.astype(jnp.int32)

    qkv_mine = across(pick(split_rows(qkv_weight, 4), quarter, 1))
    vectors = (first_gain, first_shift, proj_bias, second_gain, second_shift, out_bias)
    (
        vec,
        qkv0,
        grad_mlp,
        grad_mlp_turned,
        grad_out_bias,
        a_low,
        a_turned,
        proj_send,
        fc_send,
        out_send,
    ) = project(
        bits,
        length,
        block_input,
        cotangent,
        (*vectors, qv_bias, fc_bias),
        qkv_weight,
        proj_weight,
        fc_weight,
        out_weight,
    )

    fc_mine = across(fc_send)
    proj_got = across(proj_send)
    qkv_mine, qkv0 = tie(qkv_mine, qkv0)
    qkv_side = swap(qkv_mine, 2)
    qkv_core = swap(qkv_mine, 1)
    lse0, ctx0, ctxt0, qkv0 = attention_forward_own(length, qkv0)

    qkv_side, qkv_core, proj_got, ctx0, out_send = tie(
        qkv_side, qkv_core, proj_got, ctx0, out_send
    )
    half_rows = width // 2
    parts = proj_got[half_rows : half_rows + 24].astype(F32).reshape(3, 8, model)
    other_vec = (parts[0] + parts[1]) + parts[2]
    proj_other = [proj_got, swap(proj_got, 1)]
    qkv_other = [qkv_mine, qkv_core, qkv_side, swap(qkv_side, 1)]
    out_mine = across(out_send)
    lse1, c_low, c_turned, middle, ctxt1, qkv1 = attention_forward_other(
        bits,
        length,
        other_vec,
        vec,
        a_low,
        block_input,
        ctx0,
        proj_weight,
        qkv_other,
        proj_other,
    )

    c_low, fc_mine = tie(c_low, fc_mine)
    fc_side = swap(fc_mine, 2)
    fc_core = swap(fc_mine, 1)
    gc0, act0, fc_kept, out_kept, fc_sent, out_sent, grad_fc_bias, c_low, grad_mlp = feed_forward_own(
        bits, block, c_low, grad_mlp, c_turned, grad_mlp_turned, vec, fc_weight, out_weight
    )

    fc_sent, out_sent, fc_side, fc_core, out_mine = tie(
        fc_sent, out_sent, fc_side, fc_core, out_mine
    )
    fc_other = [fc_mine, fc_core, fc_side, swap(fc_side, 1)]
    out_other = [out_mine, swap(out_mine, 1)]
    fc_sent, out_sent, fc_other[3], out_other[1] = tie(
        fc_sent, out_sent, fc_other[3], out_other[1]
    )
    fc_got = swap(fc_sent, 1 << first_bit)
    out_got = swap(out_sent, 1 << first_bit)
    do0, fc_kept, out_kept, sums2, act1, grad_middle, grad_attn, do1 = feed_forward_other(
        bits,
        length,
        c_low,
        grad_mlp,
        other_vec,
        vec,
        gc0,
        middle,
        cotangent,
        proj_weight,
        (fc_kept, out_kept),
        fc_other,
        out_other,
        proj_other,
    )

    fc_sum = Reduction(fc_kept, first_bit, list(order_a))
    out_sum = Reduction(out_kept, first_bit, list(order_b))
    do0, fc_got, out_got = tie(do0, fc_got, out_got)
    fc_sent = fc_sum.advance(fc_got)
    out_sent = out_sum.advance(out_got)
    do0, fc_sent, out_sent = tie(do0, fc_sent, out_sent)
    fc_got = swap(fc_sent, 1 << fc_sum.bit)
    out_got = swap(out_sent, 1 << out_sum.bit)
    lead, vectors, kept, sent, d0 = attention_backward_own(
        bits,
        length,
        block,
        lse0,
        vec,
        (grad_out_bias, sums2, grad_fc_bias),
        do0,
        qkv0,
        ctxt0,
        a_turned,
        grad_attn,
        qkv_weight,
    )

    sent, lead, fc_got, out_got = tie(sent, lead, fc_got, out_got)
    attn_got = swap(sent, 1 << first_bit)
    lead_got = across(lead)
    fc_sent = fc_sum.advance(fc_got)
    out_sent = out_sum.advance(out_got)
    fc_got = swap(fc_sent, 1 << fc_sum.bit)
    out_got = swap(out_sent, 1 << out_sum.bit)

    def rounded(vectors):
        return lax.reduce_precision(vectors, 8, 7)

    def join(vectors, got):
        return rounded(vectors) + got.astype(F32)

    vectors = jnp.concatenate([(lead + lead_got)[:2], vectors[2:]], 0)
    lines = vectors.shape[0]
    vectors = join(vectors, swap(vectors.astype(BF), 1 << first_bit))
    first_sum = Reduction(kept[:, :model], first_bit, list(order_a))
    second_sum = Reduction(kept[:, model:], first_bit, list(order_b))
    first_sent = jnp.concatenate(
        [first_sum.advance(attn_got[:, :model]), vectors.astype(BF)], 0
    )
    second_sent = second_sum.advance(attn_got[:, model:])
    first_sent, second_sent, qkv1 = tie(first_sent, second_sent, qkv1)
    first_got = swap(first_sent, 1 << first_sum.bit)
    second_got = swap(second_sent, 1 << second_sum.bit)
    both, weights, ow, act = attention_backward_other(
        bits,
        length,
        lse1,
        qkv1,
        ctxt1,
        do1,
        d0,
        qkv_weight,
        out_weight,
        act0,
        act1,
        qkv_other,
        out_other,
    )

    both, fc_got, out_got, first_got, second_got = tie(both, fc_got, out_got, first_got, second_got)
    vectors = join(vectors, first_got[-lines:])
    first_sent = jnp.concatenate(
        [first_sum.advance(first_got[:-lines]), vectors.astype(BF)], 0
    )
    second_sent = second_sum.advance(second_got)
    rest_sent = jnp.concatenate([fc_sum.advance(fc_got), out_sum.advance(out_got)], 0)
    both, first_sent, second_sent, rest_sent = tie(both, first_sent, second_sent, rest_sent)
    first_got = swap(first_sent, 1 << first_sum.bit)
    second_got = swap(second_sent, 1 << second_sum.bit)
    rest_got = swap(rest_sent, 1 << fc_sum.bit)
    grad_input = gradient_of_input(vec, both, weights, block_input, grad_middle)

    grad_input, first_got, second_got, act = tie(grad_input, first_got, second_got, act)
    for level in range(3, levels):
        vectors = join(vectors, first_got[-lines:])
        sent = [first_sum.advance(first_got[:-lines]), second_sum.advance(second_got)]
        rows = sent[0].shape[0]
        sent = jnp.concatenate([*sent, vectors.astype(BF)], 0)
        sent, act = tie(sent, act)
        got = swap(sent, 1 << first_sum.bit)
        first_got = jnp.concatenate([got[:rows], got[2 * rows :]], 0)
        second_got = got[rows : 2 * rows]
        if fc_sum.order:
            rows = rest_got.shape[0] // 2
            rest_sent = [fc_sum.advance(rest_got[:rows]), out_sum.advance(rest_got[rows:])]
            rest_got = swap(jnp.concatenate(rest_sent, 0), 1 << fc_sum.bit)
    block_output = block_result(vec, act, ow, middle)
    vectors = join(vectors, first_got[-lines:])
    first = first_sum.finish(first_got[:-lines])
    second = second_sum.finish(second_got)
    rows = rest_got.shape[0] // 2
    grad_fc_weight = fc_sum.finish(rest_got[:rows])
    grad_out_weight = out_sum.finish(rest_got[rows:]).T
    grad_qkv_weight = jnp.stack([first[:, :width], first[:, width:], second[:, :width]])
    grad_proj_weight = second[:, width:].T
    return (
        block_output,
        grad_input,
        vectors[0],
        vectors[1],
        grad_qkv_weight,
        vectors[8].reshape(2, width),
        grad_proj_weight,
        vectors[5],
        vectors[3],
        vectors[4],
        grad_fc_weight,
        vectors[6:8].reshape(units),
        grad_out_weight,
        vectors[2],
    )


def solution(mesh):
    placed = (
        P("dp", None),
        P(),
        P(),
        P(None, None, "tensor"),
        P(None, "tensor"),
        P("tensor", None),
        P(),
        P(),
        P(),
        P(None, "tensor"),
        P("tensor"),
        P("tensor", None),
        P(),
        P("dp", None),
        P("dp"),
    )
    return jax.shard_map(
        local,
        mesh=mesh,
        in_specs=placed,
        out_specs=(
            P("dp", None),
            P("dp", None),
            P(),
            P(),
            P(None, "dp", "tensor"),
            P(None, "tensor"),
            P("tensor", "dp"),
            P(),
            P(),
            P(),
            P("dp", "tensor"),
            P("tensor"),
            P("tensor", "dp"),
            P(),
        ),
        check_vma=False,
    )
```

```python
import functools

import jax
import jax.numpy as jnp
from jax import lax
from jax.experimental import pallas as pl
from jax.experimental.pallas import tpu as pltpu
from jax.sharding import PartitionSpec as P

EPSILON = 1e-05
BRANCH = 48 ** (-0.5)
GELU = 0.7978845608028654
CUBIC = 0.044715
FILL = -1e30
BF = jnp.bfloat16
F32 = jnp.float32
MIB = 1024 * 1024
TILE = 256
HIDDEN = 512
GAIN1, SHIFT1, BIAS_P, GAIN2, SHIFT2, BIAS_O = range(6)
BIAS_QV, BIAS_FC = 8, 9


def dot(left, right):
    return lax.dot_general(left, right, (((1,), (0,)), ((), ())), preferred_element_type=F32)


def dot_nt(left, right):
    return lax.dot_general(left, right, (((1,), (1,)), ((), ())), preferred_element_type=F32)


def norm_parts(values):
    row_mean = jnp.mean(values, -1, keepdims=True)
    centered = values - row_mean
    inverse = lax.rsqrt(jnp.mean(centered * centered, -1, keepdims=True) + EPSILON)
    return centered * inverse, inverse


def norm_back(grad_out, normed, inverse, gain):
    scaled = grad_out * gain
    inner = (
        scaled
        - jnp.mean(scaled, -1, keepdims=True)
        - normed * jnp.mean(scaled * normed, -1, keepdims=True)
    )
    return inverse * inner


def whole(shape):
    return pl.BlockSpec(shape, lambda *_: (0,) * len(shape))


def row_tile(columns):
    return pl.BlockSpec((TILE, columns), lambda i: (i, 0))


def column_tile(rows, size=TILE):
    return pl.BlockSpec((rows, size), lambda i: (0, i))


SMEM = pl.BlockSpec(memory_space=pltpu.SMEM)
HBM = pl.BlockSpec(memory_space=pl.ANY)
LOOSE = pl.BlockSpec(memory_space=pl.ANY)
KEPT = pl.BlockSpec(memory_space=pltpu.VMEM)


def call(body, name, steps, ins, outs, scratch, flops, limit=12):
    args = []
    for array, spec in ins:
        if spec is KEPT:
            array = pltpu.with_memory_space_constraint(array, pltpu.VMEM)
        elif spec is not SMEM and spec is not LOOSE:
            array = pltpu.with_memory_space_constraint(array, pltpu.HBM)
        args.append(array)
    moved = sum(a.size * a.dtype.itemsize for a, spec in ins if spec is not KEPT)
    moved += sum(
        jax.ShapeDtypeStruct(shape, dtype).size * jnp.dtype(dtype).itemsize
        for shape, dtype, spec in outs
        if spec is not KEPT
    )
    return pl.pallas_call(
        body,
        name=name,
        grid=(steps,),
        out_shape=tuple(
            (pltpu.VMEM if spec is KEPT else pltpu.HBM)(shape, dtype) for shape, dtype, spec in outs
        ),
        in_specs=[spec for _, spec in ins],
        out_specs=tuple(spec for _, _, spec in outs),
        scratch_shapes=scratch,
        compiler_params=pltpu.CompilerParams(vmem_limit_bytes=limit * MIB),
        cost_estimate=pl.CostEstimate(flops=flops, bytes_accessed=moved, transcendentals=0),
    )(*args)


def tile_of(step):
    return pl.ds(pl.multiple_of(step * TILE, TILE), TILE)


def fetch_rows(pieces, turn, target, sems):
    copies = []
    for index, piece in enumerate(pieces):
        rows = piece.shape[-2]
        if len(pieces) > 1:
            place = jnp.bitwise_xor(jnp.int32(index), turn)
            where = pl.ds(pl.multiple_of(place * rows, 32), rows)
        else:
            where = slice(None)
        if len(piece.shape) == 2:
            copies.append(pltpu.make_async_copy(piece, target.at[where, :], sems.at[index]))
            continue
        width = piece.shape[2]
        for matrix in range(3):
            columns = slice(matrix * width, (matrix + 1) * width)
            copies.append(
                pltpu.make_async_copy(
                    piece.at[matrix], target.at[where, columns], sems.at[3 * index + matrix]
                )
            )
    return copies


def start_all(copies):
    for copy in copies:
        copy.start()


def wait_all(copies):
    for copy in copies:
        copy.wait()


def qkv_bias(biases, width):
    bias = jnp.concatenate(
        [biases[:, :width], jnp.zeros((1, width), F32), biases[:, width:]], axis=1
    )
    lane = lax.broadcasted_iota(jnp.int32, (1, 3 * width), 1)
    return bias, jnp.where(lane < width, 0.125, 1.0)


def tiles(source, target, sems, axis=0):
    copies = []
    for index in range(source.shape[axis] // TILE):
        part = slice(index * TILE, (index + 1) * TILE)
        view = (part, slice(None)) if axis == 0 else (slice(None), part)
        copies.append(pltpu.make_async_copy(source.at[view], target.at[view], sems.at[index]))
    return copies


def tile_copy(source, target, sems, index):
    rows = tile_of(index)
    return pltpu.make_async_copy(source.at[rows, :], target.at[rows, :], sems.at[index])


def clear(*refs):
    @pl.loop(0, refs[0].shape[0] // TILE)
    def _(index):
        for ref in refs:
            ref[tile_of(index), :] = jnp.zeros((TILE, ref.shape[1]), ref.dtype)


def halves(value_ref, side, block, kept_ref, sent_ref):
    for index in range(value_ref.shape[0] // (2 * block)):
        rows = slice(index * block, (index + 1) * block)
        first = 2 * block * index
        here = pl.ds(pl.multiple_of(first + block * side, 16), block)
        there = pl.ds(pl.multiple_of(first + block * (1 - side), 16), block)
        kept_ref[rows, :] = value_ref[here, :]
        sent_ref[rows, :] = value_ref[there, :]


def grad_top_of(cot, length, start):
    rows, model = cot.shape
    position = lax.broadcasted_iota(jnp.int32, (rows, 128), 0) + start
    valid = jnp.where(position < length, 1.0, 0.0)
    return cot.astype(F32) * jnp.concatenate([valid] * (model // 128), axis=1)


def project_kernel(
    bits_ref,
    x_hbm,
    gain1_ref,
    shift1_ref,
    bias_p_ref,
    gain2_ref,
    shift2_ref,
    bias_o_ref,
    qv_ref,
    fcb_ref,
    qkv_hbm,
    proj_hbm,
    fc_hbm,
    out_hbm,
    length_ref,
    cot_hbm,
    vec_ref,
    qkv_ref,
    gm_ref,
    gmt_ref,
    ob_ref,
    a_out,
    at_out,
    proj_out,
    fc_out,
    out_out,
    x_ref,
    w_ref,
    a_ref,
    at_ref,
    proj_ref,
    fc_ref,
    out_ref,
    cot_ref,
    low_ref,
    x_sems,
    w_sems,
    cot_sems,
    send_sems,
    a_sems,
    at_sems,
):
    x_in = tiles(x_hbm, x_ref, x_sems)
    x_in[0].start()
    w_in = fetch_rows([qkv_hbm], 0, w_ref, w_sems)
    start_all(w_in)
    start_all(x_in[1:])
    model = x_ref.shape[1]
    half, quarter, out_half = proj_hbm.shape[0] // 2, fc_hbm.shape[0] // 4, out_hbm.shape[0] // 2
    sends_in = []
    for index, (source, target, place, rows) in enumerate(
        (
            (proj_hbm, proj_ref.at[:half, :], bits_ref[0], half),
            (fc_hbm, fc_ref, bits_ref[1], quarter),
            (out_hbm, out_ref, bits_ref[0], out_half),
        )
    ):
        where = pl.ds(pl.multiple_of(place * rows, 32), rows)
        sends_in.append(pltpu.make_async_copy(source.at[where, :], target, send_sems.at[index]))
    start_all(sends_in)
    sends_out = [
        pltpu.make_async_copy(source, target, send_sems.at[3 + index])
        for index, (source, target) in enumerate(
            ((proj_ref, proj_out), (fc_ref, fc_out), (out_ref, out_out))
        )
    ]
    cot_in = tiles(cot_hbm, cot_ref, cot_sems)
    start_all(cot_in)
    vec_ref[...] = jnp.zeros(vec_ref.shape, F32)
    for index, ref in enumerate(
        (gain1_ref, shift1_ref, bias_p_ref, gain2_ref, shift2_ref, bias_o_ref)
    ):
        vec_ref[index : index + 1, :] = ref[...].reshape(1, model)
    width = qv_ref.shape[1]
    vec_ref[BIAS_QV : BIAS_QV + 1, :width] = qv_ref[0:1, :]
    vec_ref[BIAS_QV : BIAS_QV + 1, width:] = qv_ref[1:2, :]
    fcb = fcb_ref[...].reshape(1, fcb_ref.shape[0])
    for index in range(2):
        vec_ref[BIAS_FC + index : BIAS_FC + index + 1, :] = fcb[:, index * model : (index + 1) * model]
    value = vec_ref[8 * (BIAS_QV // 8) :, :]
    high = value.astype(BF)
    rest = value - high.astype(F32)
    mid = rest.astype(BF)
    low = (rest - mid.astype(F32)).astype(BF)
    lines = value.shape[0]
    for index, part in enumerate((high, mid, low)):
        proj_ref[half + index * lines : half + (index + 1) * lines, :] = part

    def normalize(index):
        rows = tile_of(index)
        normed, _ = norm_parts(x_ref[rows, :].astype(F32))
        low = normed * vec_ref[GAIN1 : GAIN1 + 1, :] + vec_ref[SHIFT1 : SHIFT1 + 1, :]
        low = low.astype(BF)
        low_ref[...] = low
        a_ref[rows, :] = low
        at_ref[:, rows] = low.T

    def gradient(index):
        rows = tile_of(index)
        top = grad_top_of(cot_ref[rows, :], length_ref[0], index * TILE)
        ob_ref[...] += BRANCH * jnp.sum(top, 0, keepdims=True)
        low = (BRANCH * top).astype(BF)
        gm_ref[rows, :] = low
        gmt_ref[:, rows] = low.T

    def multiply(index):
        qkv_ref[tile_of(index), :] = ((dot(low_ref[...], w_ref[...]) + bias) * scale).astype(BF)

    count = len(x_in)
    bias, scale = qkv_bias(vec_ref[BIAS_QV : BIAS_QV + 1, :], width)
    a_tiles = tiles(a_ref, a_out, a_sems)
    at_tiles = tiles(at_ref, at_out, at_sems, 1)
    ob_ref[...] = jnp.zeros(ob_ref.shape, F32)
    x_in[0].wait()
    normalize(0)
    wait_all(w_in + x_in[1:])

    @pl.loop(0, count - 1)
    def _(index):
        multiply(index)
        normalize(index + 1)

    start_all(a_tiles + at_tiles)
    wait_all(sends_in + cot_in)
    start_all(sends_out)
    multiply(count - 1)

    @pl.loop(0, count)
    def _(index):
        gradient(index)

    wait_all(sends_out + a_tiles + at_tiles)


def project(bits, length, x, cot, vectors, qkv, proj, fc, ow):
    slots, model = x.shape
    width = qkv.shape[2]
    units = fc.shape[1]
    tokens = slots // TILE
    sends = [
        (width // 2 + 32, model),
        (model // 4, units),
        (units // 2, model),
    ]
    shapes = [(slots, model), (model, slots)]
    dma = pltpu.SemaphoreType.DMA
    return call(
        project_kernel,
        "project_own",
        1,
        [(bits, SMEM), (x, HBM)]
        + [(vector, whole(vector.shape)) for vector in vectors]
        + [(weight, HBM) for weight in (qkv, proj, fc, ow)]
        + [(length, SMEM), (cot, HBM)],
        [
            ((16, model), F32, whole((16, model))),
            ((slots, 3 * width), BF, KEPT),
            ((slots, model), BF, KEPT),
            ((model, slots), BF, KEPT),
            ((1, model), F32, whole((1, model))),
        ]
        + [(shape, BF, HBM) for shape in shapes + sends],
        [pltpu.VMEM((slots, model), BF), pltpu.VMEM((model, 3 * width), BF)]
        + [pltpu.VMEM(shape, BF) for shape in shapes + sends]
        + [pltpu.VMEM((slots, model), BF), pltpu.VMEM((TILE, model), BF)]
        + [dma((tokens,)), dma((3,)), dma((tokens,)), dma((6,)), dma((tokens,)), dma((tokens,))],
        6 * slots * model * width,
        13,
    )


def causal_fill():
    keys = lax.broadcasted_iota(jnp.int32, (TILE, TILE), 0)
    queries = lax.broadcasted_iota(jnp.int32, (TILE, TILE), 1)
    return jnp.where(keys <= queries, 0.0, FILL)


def masked_pair(pair_keys, pair_queries, length, keys_ref, queries_ref):
    slots = pair_keys.shape[0]
    lane = lax.broadcasted_iota(jnp.int32, (slots, 128), 1)
    position = lax.broadcasted_iota(jnp.int32, (slots, 128), 0)
    fill = jnp.where(position < length, 0.0, FILL)
    pair_keys = pair_keys.astype(F32)
    pair_queries = pair_queries.astype(F32)
    for half in (0, 1):
        spare = 64 * (1 - half)
        keys_ref[half] = jnp.where(lane == spare, fill, pair_keys).astype(BF)
        queries_ref[half] = jnp.where(
            lane // 64 == half, pair_queries, jnp.where(lane == spare, 1.0, 0.0)
        ).astype(BF)


def block_order(blocks):
    return [(block, 0) for block in range(blocks)] + [(block, 1) for block in reversed(range(blocks))]


def pair_lanes(pair, offset=0):
    return pl.ds(pl.multiple_of(offset + pair * 128, 128), 128)


def forward_pairs(length, qkv_ref, ctx_ref, ctxt_ref, lse_ref, scratch, results):
    ka_ref, qa_ref, vt_ref, score_ref, expo_ref = scratch
    width, slots = ctxt_ref.shape
    causal = causal_fill()

    @pl.loop(0, width // 128)
    def _(pair):
        lanes = pair_lanes(pair)
        masked_pair(
            qkv_ref[:, pair_lanes(pair, width)], qkv_ref[:, lanes], length, ka_ref, qa_ref
        )
        vt_ref[...] = qkv_ref[:, pair_lanes(pair, 2 * width)].T
        items = block_order(slots // TILE)
        state = {}

        def score(item):
            block, half = items[item]
            extent = (block + 1) * TILE
            columns = slice(block * TILE, extent)
            scores = dot_nt(ka_ref[half, :extent, :], qa_ref[half, columns, :])
            high = None
            for inner in range(block + 1):
                keys = slice(inner * TILE, (inner + 1) * TILE)
                part = scores[keys]
                if inner == block:
                    part = part + causal
                score_ref[item % 2, keys, :] = part
                most = jnp.max(part.reshape(TILE // 8, 8, TILE), 0)
                high = most if high is None else jnp.maximum(high, most)
            state[item] = jnp.max(high, 0, keepdims=True)

        def exponential(item):
            block, half = items[item]
            high = state[item]
            total = None
            for inner in range(block + 1):
                keys = slice(inner * TILE, (inner + 1) * TILE)
                expo = jnp.exp(score_ref[item % 2, keys, :] - high)
                part = jnp.sum(expo.reshape(TILE // 8, 8, TILE), 0)
                total = part if total is None else total + part
                expo_ref[item % 2, keys, :] = expo.astype(BF)
            state[item] = (high, jnp.sum(total, 0, keepdims=True))

        def mix(item):
            block, half = items[item]
            extent = (block + 1) * TILE
            columns = slice(block * TILE, extent)
            high, total = state[item]
            mixed = dot(vt_ref[64 * half : 64 * half + 64, :extent], expo_ref[item % 2, :extent, :])
            row = pl.multiple_of(pair * 128 + half * 64, 64)
            ctxt_ref[pl.ds(row, 64), columns] = mixed * (1.0 / total)
            lse_ref[pl.ds(pair * 2 + half, 1), columns] = high + jnp.log(total)

        count = len(items)
        score(0)
        for item in range(count + 1):
            if item + 1 < count:
                score(item + 1)
            if item >= 1:
                mix(item - 1)
            if item < count:
                exponential(item)
        ctx_ref[:, lanes] = ctxt_ref[lanes, :].T.astype(BF)
        start_all(results(pair))


def forward_own_kernel(
    length_ref, qkv_ref, lse_ref, ctx_out, ctxt_out, qkv_out, ctx_ref, ctxt_ref, *rest
):
    scratch, sems = rest[:5], rest[5]
    saved = pltpu.make_async_copy(qkv_ref, qkv_out, sems.at[2, 0])
    saved.start()

    def results(pair):
        lanes = pair_lanes(pair)
        return [
            pltpu.make_async_copy(ctx_ref.at[:, lanes], ctx_out.at[:, lanes], sems.at[0, pair]),
            pltpu.make_async_copy(ctxt_ref.at[lanes, :], ctxt_out.at[lanes, :], sems.at[1, pair]),
        ]

    forward_pairs(length_ref[0], qkv_ref, ctx_ref, ctxt_ref, lse_ref, scratch, results)
    for pair in range(ctx_ref.shape[1] // 128):
        wait_all(results(pair))
    saved.wait()


def forward_other_kernel(
    bits_ref, length_ref, other_vec_ref, vec_ref, a_hbm, x_hbm, ctx0_hbm, proj0_hbm, *rest
):
    pieces, proj_pieces, rest = rest[:4], rest[4:6], rest[6:]
    lse_ref, c_ref, ct_ref, middle_out, ctxt_out, qkv_out, *rest = rest
    both_ref, ctxt_ref, *rest = rest
    scratch, rest = rest[:5], rest[5:]
    qkv_ref, a_ref, w_ref, x_ref, proj_ref, middle_ref, sum_ref, *rest = rest
    a_sems, w_sems, qkv_sems, sems, late_sems, proj_sems, middle_sems = rest
    slots, width = ctx0_hbm.shape
    own = pl.ds(pl.multiple_of(bits_ref[3] * width, 128), width)
    other = pl.ds(pl.multiple_of((1 - bits_ref[3]) * width, 128), width)
    ctx_ref = both_ref.at[:, other]
    w_in = fetch_rows(pieces, bits_ref[1], w_ref, w_sems)
    start_all(w_in)
    a_in = tiles(a_hbm, a_ref, a_sems)
    start_all(a_in)
    late = [
        pltpu.make_async_copy(source, target, late_sems.at[index])
        for index, (source, target) in enumerate(
            ((x_hbm, x_ref), (ctx0_hbm, both_ref.at[:, own]), (proj0_hbm, proj_ref.at[own, :]))
        )
    ]
    halves_in = [piece.at[: width // 2, :] for piece in proj_pieces]
    late += fetch_rows(halves_in, bits_ref[0], proj_ref.at[other, :], proj_sems)
    start_all(late)
    bias, scale = qkv_bias(other_vec_ref[0:1, :], width)
    qkv_tiles = tiles(qkv_ref, qkv_out, qkv_sems)
    wait_all(w_in + a_in)

    @pl.loop(0, len(a_in))
    def _(index):
        rows = tile_of(index)
        product = dot(a_ref[rows, :], w_ref[...])
        qkv_ref[rows, :] = ((product + bias) * scale).astype(BF)

    start_all(qkv_tiles)

    def results(pair):
        lanes = pair_lanes(pair)
        return [
            pltpu.make_async_copy(ctxt_ref.at[lanes, :], ctxt_out.at[lanes, :], sems.at[pair])
        ]

    forward_pairs(length_ref[0], qkv_ref, ctx_ref, ctxt_ref, lse_ref, scratch, results)
    wait_all(late)
    count = slots // TILE

    def branch(index):
        return dot(both_ref[tile_of(index), :], proj_ref[...])

    def normalize(index):
        rows = tile_of(index)
        total = sum_ref[...] + vec_ref[BIAS_P : BIAS_P + 1, :]
        middle = x_ref[rows, :].astype(F32) + BRANCH * total
        middle_ref[rows, :] = middle
        normed, _ = norm_parts(middle)
        low = (normed * vec_ref[GAIN2 : GAIN2 + 1, :] + vec_ref[SHIFT2 : SHIFT2 + 1, :]).astype(BF)
        c_ref[rows, :] = low
        ct_ref[:, rows] = low.T

    sum_ref[...] = branch(0)

    @pl.loop(0, count - 1)
    def _(index):
        normalize(index)
        sum_ref[...] = branch(index + 1)
        tile_copy(middle_ref, middle_out, middle_sems, index).start()

    normalize(count - 1)
    middle_tiles = tiles(middle_ref, middle_out, middle_sems)
    middle_tiles[-1].start()
    for pair in range(width // 128):
        wait_all(results(pair))
    wait_all(qkv_tiles + middle_tiles)


def forward_scratch(slots, width):
    return [
        pltpu.VMEM((slots, width), BF),
        pltpu.VMEM((width, slots), F32),
        pltpu.VMEM((2, slots, 128), BF),
        pltpu.VMEM((2, slots, 128), BF),
        pltpu.VMEM((128, slots), BF),
        pltpu.VMEM((2, slots, TILE), F32),
        pltpu.VMEM((2, slots, TILE), BF),
    ]


def attention_forward_own(length, qkv):
    slots = qkv.shape[0]
    width = qkv.shape[1] // 3
    heads = width // 64
    return call(
        forward_own_kernel,
        "attention_forward_own",
        1,
        [(length, SMEM), (qkv, KEPT)],
        [
            ((heads, slots), F32, whole((heads, slots))),
            ((slots, width), BF, HBM),
            ((width, slots), F32, HBM),
            ((slots, 3 * width), BF, HBM),
        ],
        [*forward_scratch(slots, width), pltpu.SemaphoreType.DMA((3, width // 128))],
        6 * slots * slots * width,
        6,
    )


def attention_forward_other(bits, length, other_vec, vec, a_low, x, ctx, proj, pieces, proj_pieces):
    slots, model = x.shape
    width = ctx.shape[1]
    heads = width // 64
    tokens = slots // TILE
    dma = pltpu.SemaphoreType.DMA
    ins = [(bits, SMEM), (length, SMEM)]
    ins += [(value, whole(value.shape)) for value in (other_vec, vec)]
    ins += [(value, HBM) for value in (a_low, x, ctx, proj)]
    ins += [(value, LOOSE) for value in (*pieces, *proj_pieces)]
    return call(
        forward_other_kernel,
        "attention_forward_other",
        1,
        ins,
        [
            ((heads, slots), F32, whole((heads, slots))),
            ((slots, model), BF, KEPT),
            ((model, slots), BF, KEPT),
            ((slots, model), F32, HBM),
            ((width, slots), F32, HBM),
            ((slots, 3 * width), BF, HBM),
        ],
        [
            pltpu.VMEM((slots, 2 * width), BF),
            *forward_scratch(slots, width)[1:],
            pltpu.VMEM((slots, 3 * width), BF),
            pltpu.VMEM((slots, model), BF),
            pltpu.VMEM((model, 3 * width), BF),
            pltpu.VMEM((slots, model), BF),
            pltpu.VMEM((2 * width, model), BF),
            pltpu.VMEM((slots, model), F32),
            pltpu.VMEM((TILE, model), F32),
            dma((tokens,)),
            dma((12,)),
            dma((tokens,)),
            dma((width // 128,)),
            dma((3,)),
            dma((2,)),
            dma((tokens,)),
        ],
        6 * slots * slots * width + 10 * slots * model * width,
        20,
    )


def mlp_step(hidden, g_ref, ow):
    square = hidden * hidden
    tanh = jnp.tanh(hidden * (GELU + GELU * CUBIC * square))
    share = 0.5 + 0.5 * tanh
    value = hidden * share
    slope = share + value * (1.0 - share) * (2.0 * GELU + 6.0 * GELU * CUBIC * square)
    return value.astype(BF), (dot_nt(g_ref[...], ow) * slope).astype(BF)


def unit_bias(vec_ref, base, bias_ref):
    model = vec_ref.shape[1]
    for row in range(bias_ref.shape[1] // model):
        columns = slice(row * model, (row + 1) * model)
        bias_ref[:, columns] = vec_ref[base + row : base + row + 1, :]


def mlp_own_kernel(
    steps,
    block,
    bits_ref,
    c_ref,
    g_ref,
    ct_ref,
    gt_ref,
    vec_ref,
    fc_ref,
    ow_ref,
    gc_out,
    act_ref,
    fc_kept_ref,
    out_kept_ref,
    fc_sent_ref,
    out_sent_ref,
    db_ref,
    c_out,
    g_out,
    gc_ref,
    gc_low_ref,
    bias_ref,
    gh_ref,
    dw_ref,
    sems,
):
    saved = [
        pltpu.make_async_copy(c_ref, c_out, sems.at[1]),
        pltpu.make_async_copy(g_ref, g_out, sems.at[2]),
    ]
    step = pl.program_id(0)

    @pl.when(step == 0)
    def _():
        start_all(saved)
        unit_bias(vec_ref, BIAS_FC, bias_ref)
        clear(gc_ref)

    lanes = pl.ds(pl.multiple_of(step * HIDDEN, HIDDEN), HIDDEN)
    hidden = dot(c_ref[...], fc_ref[...]) + bias_ref[:, lanes]
    act, gh = mlp_step(hidden, g_ref, ow_ref[...])
    act_ref[...] = act
    gh_ref[...] = gh
    db_ref[...] = jnp.sum(gh.astype(F32), 0, keepdims=True)
    gc_ref[...] += dot_nt(gh, fc_ref[...])
    results = [pltpu.make_async_copy(gc_low_ref, gc_out, sems.at[0])]

    @pl.when(step == steps - 1)
    def _():
        gc_low_ref[...] = gc_ref[...].astype(BF)
        start_all(results)

    dw_ref[0] = dot(ct_ref[...], gh_ref[...]).astype(BF)
    halves(dw_ref.at[0], bits_ref[2], block, fc_kept_ref, fc_sent_ref.at[:, lanes])
    dw_ref[1] = dot(gt_ref[...], act_ref[...]).astype(BF)
    halves(dw_ref.at[1], bits_ref[2], block, out_kept_ref, out_sent_ref.at[:, lanes])

    @pl.when(step == steps - 1)
    def _():
        wait_all(results + saved)


def feed_forward_own(bits, block, c_low, grad_mlp, c_turned, grad_turned, vec, fc, ow):
    slots, model = c_low.shape
    units = fc.shape[1]
    steps = units // HIDDEN
    half = column_tile(model // 2, HIDDEN)
    return call(
        functools.partial(mlp_own_kernel, steps, block),
        "feed_forward_own",
        steps,
        [(bits, SMEM)]
        + [(value, KEPT) for value in (c_low, grad_mlp, c_turned, grad_turned)]
        + [
            (vec, whole(vec.shape)),
            (fc, column_tile(model, HIDDEN)),
            (ow, pl.BlockSpec((HIDDEN, model), lambda i: (i, 0))),
        ],
        [((slots, model), BF, HBM), ((slots, units), BF, column_tile(slots, HIDDEN))]
        + [((model // 2, units), BF, half)] * 2
        + [((model // 2, units), BF, KEPT)] * 2
        + [((1, units), F32, column_tile(1, HIDDEN))]
        + [((slots, model), BF, HBM)] * 2,
        [
            pltpu.VMEM((slots, model), F32),
            pltpu.VMEM((slots, model), BF),
            pltpu.VMEM((1, units), F32),
            pltpu.VMEM((slots, HIDDEN), BF),
            pltpu.VMEM((2, model, HIDDEN), BF),
            pltpu.SemaphoreType.DMA((3,)),
        ],
        10 * slots * model * units,
        19,
    )


def mlp_other_kernel(
    steps,
    bits_ref,
    length_ref,
    c_hbm,
    g_hbm,
    other_vec_ref,
    vec_ref,
    gc0_hbm,
    middle_hbm,
    cot_hbm,
    proj0_hbm,
    fc_kept_hbm,
    out_kept_hbm,
    *rest,
):
    fc_pieces, out_pieces, proj_pieces, rest = rest[:4], rest[4:6], rest[6:8], rest[8:]
    do0_ref, fc_kept_ref, out_kept_ref, sums_ref, act_ref, gmid_out, ga_out, do1_out, *rest = rest
    gc_ref, bias_ref, fc_ref, ow_ref, c_ref, g_ref, *rest = rest
    late_refs, (gmid_ref, ga_ref, low_ref, do1_ref, proj1_ref, *rest) = rest[:4], rest[4:]
    sems, late_sems, proj_sems, out_sems = rest
    step = pl.program_id(0)
    slots, model = c_ref.shape
    first = fetch_rows(fc_pieces, bits_ref[1], fc_ref, sems.at[0])
    first += [pltpu.make_async_copy(c_hbm, c_ref, sems.at[2, 0])]
    second = fetch_rows(out_pieces, bits_ref[0], ow_ref, sems.at[1])
    second += [pltpu.make_async_copy(g_hbm, g_ref, sems.at[2, 1])]
    late = [
        pltpu.make_async_copy(source, target, late_sems.at[index])
        for index, (source, target) in enumerate(
            zip(
                (gc0_hbm, middle_hbm, cot_hbm, proj0_hbm, fc_kept_hbm, out_kept_hbm),
                (*late_refs, fc_kept_ref, out_kept_ref),
            )
        )
    ]
    half = proj1_ref.shape[0] // 2
    halves_in = [piece.at[:half, :] for piece in proj_pieces]
    late += fetch_rows(halves_in, bits_ref[0], proj1_ref, proj_sems)

    @pl.when(step == 0)
    def _():
        start_all(first + second)
        unit_bias(other_vec_ref, 1, bias_ref)
        clear(gc_ref)
        wait_all(first + second)
        start_all(late)

    lanes = pl.ds(pl.multiple_of(step * HIDDEN, HIDDEN), HIDDEN)
    hidden = dot(c_ref[...], fc_ref[:, lanes]) + bias_ref[:, lanes]
    act, gh = mlp_step(hidden, g_ref, ow_ref[lanes, :])
    act_ref[...] = act
    gc_ref[...] += dot_nt(gh, fc_ref[:, lanes])

    @pl.when(step == steps - 1)
    def _():
        wait_all(late)
        gc0_ref, middle_ref, cot_ref, proj0_ref = late_refs
        pairs = ((gmid_ref, gmid_out), (ga_ref, ga_out), (do1_ref, do1_out))
        outs = [(*pair, out_sems.at[index]) for index, pair in enumerate(pairs)]
        count = slots // TILE
        sums_ref[...] = jnp.zeros(sums_ref.shape, F32)

        def elementwise(index):
            rows = tile_of(index)
            grad_c = gc_ref[rows, :].astype(BF).astype(F32) + gc0_ref[rows, :].astype(F32)
            normed, inverse = norm_parts(middle_ref[rows, :])
            top = grad_top_of(cot_ref[rows, :], length_ref[0], index * TILE)
            grad_middle = top + norm_back(grad_c, normed, inverse, vec_ref[GAIN2 : GAIN2 + 1, :])
            sums_ref[0:1, :] += jnp.sum(grad_c * normed, 0, keepdims=True)
            sums_ref[1:2, :] += jnp.sum(grad_c, 0, keepdims=True)
            sums_ref[2:3, :] += BRANCH * jnp.sum(grad_middle, 0, keepdims=True)
            gmid_ref[rows, :] = grad_middle
            low = (BRANCH * grad_middle).astype(BF)
            ga_ref[rows, :] = low
            low_ref[...] = low

        def project_back(index):
            rows = tile_of(index)
            do0_ref[rows, :] = dot_nt(low_ref[...], proj0_ref[...]).astype(BF)
            do1_ref[rows, :] = dot_nt(low_ref[...], proj1_ref[...]).astype(BF)

        elementwise(0)

        @pl.loop(0, count - 1)
        def _(index):
            project_back(index)
            elementwise(index + 1)
            for group in outs:
                tile_copy(*group, index).start()

        project_back(count - 1)
        for group in outs:
            tile_copy(*group, count - 1).start()
        for group in outs:
            wait_all(tiles(*group))


def feed_forward_other(
    bits, length, c_low, grad_mlp, other_vec, vec, grad_c, middle, cot, proj, kept, fc, ow, proj_pieces
):
    slots, model = c_low.shape
    width = proj.shape[0]
    units = fc[0].shape[1]
    steps = units // HIDDEN
    tokens = slots // TILE
    dma = pltpu.SemaphoreType.DMA
    return call(
        functools.partial(mlp_other_kernel, steps),
        "feed_forward_other",
        steps,
        [(bits, SMEM), (length, SMEM), (c_low, HBM), (grad_mlp, HBM)]
        + [(value, whole(value.shape)) for value in (other_vec, vec)]
        + [(value, HBM) for value in (grad_c, middle, cot, proj, *kept, *fc, *ow, *proj_pieces)],
        [
            ((slots, width), BF, KEPT),
            *[(value.shape, BF, KEPT) for value in kept],
            ((3, model), F32, whole((3, model))),
            ((slots, units), BF, column_tile(slots, HIDDEN)),
            ((slots, model), F32, HBM),
            ((slots, model), BF, HBM),
            ((slots, width), BF, HBM),
        ],
        [
            pltpu.VMEM((slots, model), F32),
            pltpu.VMEM((1, units), F32),
            pltpu.VMEM((model, units), BF),
            pltpu.VMEM((units, model), BF),
            pltpu.VMEM((slots, model), BF),
            pltpu.VMEM((slots, model), BF),
            pltpu.VMEM((slots, model), BF),
            pltpu.VMEM((slots, model), F32),
            pltpu.VMEM((slots, model), BF),
            pltpu.VMEM((width, model), BF),
            pltpu.VMEM((slots, model), F32),
            pltpu.VMEM((slots, model), BF),
            pltpu.VMEM((TILE, model), BF),
            pltpu.VMEM((slots, width), BF),
            pltpu.VMEM((width, model), BF),
            dma((3, 4)),
            dma((6,)),
            dma((2,)),
            dma((3, tokens)),
        ],
        6 * slots * model * units + 4 * slots * model * width,
        34,
    )


def output_kernel(vec_ref, act_ref, ow_ref, middle_ref, y_ref):
    mlp = dot(act_ref[tile_of(pl.program_id(0)), :], ow_ref[...]) + vec_ref[BIAS_O : BIAS_O + 1, :]
    y_ref[...] = (middle_ref[...] + BRANCH * mlp).astype(BF)


def block_result(vec, act, ow, middle):
    slots, model = middle.shape
    return call(
        output_kernel,
        "output",
        slots // TILE,
        [(vec, whole(vec.shape)), (act, KEPT), (ow, KEPT), (middle, row_tile(model))],
        [((slots, model), BF, row_tile(model))],
        [],
        2 * slots * model * act.shape[1],
        5,
    )[0]


def backward_pairs(length, qkv_ref, do_ref, ctxt_ref, lse_ref, d_ref, scratch, sources):
    (
        ka_ref,
        qa_ref,
        do_mask_ref,
        kt_ref,
        qt_ref,
        dot_ref,
        delta_ref,
        dqt_ref,
        dkt_ref,
        dvt_ref,
        score_ref,
        grad_ref,
        prob_ref,
        slope_ref,
    ) = scratch
    slots, width = do_ref.shape
    causal = causal_fill()
    blocks = slots // TILE

    @pl.loop(0, width // 128)
    def _(pair):
        lanes = pair_lanes(pair)
        wait_all(sources(pair))
        keys_low = qkv_ref[:, pair_lanes(pair, width)]
        queries = qkv_ref[:, lanes]
        masked_pair(keys_low, queries, length, ka_ref, qa_ref)
        grads = do_ref[:, lanes]
        lane = lax.broadcasted_iota(jnp.int32, (slots, 128), 1)
        for half in (0, 1):
            do_mask_ref[half] = jnp.where(lane // 64 == half, grads.astype(F32), 0.0).astype(BF)
        kt_ref[...] = keys_low.T
        qt_ref[...] = queries.T
        turned = grads.T
        dot_ref[...] = turned
        product = turned.astype(F32) * ctxt_ref[lanes, :]
        for half in (0, 1):
            delta_ref[half : half + 1, :] = jnp.sum(
                product[64 * half : 64 * half + 64], 0, keepdims=True
            )
        items = block_order(blocks)

        def score(item):
            block, half = items[item]
            extent = (block + 1) * TILE
            columns = slice(block * TILE, extent)
            score_ref[item % 2, :extent, :] = dot_nt(
                ka_ref[half, :extent, :], qa_ref[half, columns, :]
            )
            grad_ref[item % 2, :extent, :] = dot_nt(
                qkv_ref[:extent, pair_lanes(pair, 2 * width)], do_mask_ref[half, columns, :]
            )

        def softmax(item):
            block, half = items[item]
            columns = slice(block * TILE, (block + 1) * TILE)
            lse = lse_ref[pl.ds(pair * 2 + half, 1), columns]
            delta = delta_ref[half : half + 1, columns]
            for inner in range(block + 1):
                keys = slice(inner * TILE, (inner + 1) * TILE)
                scores = score_ref[item % 2, keys, :]
                if inner == block:
                    scores = scores + causal
                prob = jnp.exp(scores - lse)
                slope_ref[item % 2, keys, :] = (
                    prob * (grad_ref[item % 2, keys, :] - delta)
                ).astype(BF)
                prob_ref[item % 2, keys, :] = prob.astype(BF)

        def gradients(item):
            block, half = items[item]
            extent = (block + 1) * TILE
            columns = slice(block * TILE, extent)
            rows = slice(64 * half, 64 * half + 64)
            dv_part = dot_nt(dot_ref[rows, columns], prob_ref[item % 2, :extent, :])
            dk_part = dot_nt(qt_ref[rows, columns], slope_ref[item % 2, :extent, :])
            fresh = block * TILE if half == 0 else (0 if block == blocks - 1 else extent)
            if fresh < extent:
                dvt_ref[rows, fresh:extent] = dv_part[:, fresh:]
                dkt_ref[rows, fresh:extent] = dk_part[:, fresh:]
            if fresh:
                dvt_ref[rows, :fresh] += dv_part[:, :fresh]
                dkt_ref[rows, :fresh] += dk_part[:, :fresh]
            dqt_ref[rows, columns] = dot(kt_ref[rows, :extent], slope_ref[item % 2, :extent, :])

        count_items = len(items)
        score(0)
        for item in range(count_items + 1):
            if item + 1 < count_items:
                score(item + 1)
            if item >= 1:
                gradients(item - 1)
            if item < count_items:
                softmax(item)
        d_ref[:, lanes] = (dqt_ref[...] * 0.125).astype(BF).T
        d_ref[:, pair_lanes(pair, width)] = dkt_ref[...].astype(BF).T
        d_ref[:, pair_lanes(pair, 2 * width)] = dvt_ref[...].astype(BF).T


def pair_sources(pair, width, qkv, ctxt, do, sems):
    lanes = pair_lanes(pair)
    moves = []
    for matrix in range(3):
        columns = pair_lanes(pair, matrix * width)
        moves.append((qkv[0].at[:, columns], qkv[1].at[:, columns]))
    moves.append((ctxt[0].at[lanes, :], ctxt[1].at[lanes, :]))
    if do is not None:
        moves.append((do[0].at[:, lanes], do[1].at[:, lanes]))
    return [
        pltpu.make_async_copy(source, target, sems.at[index, pair])
        for index, (source, target) in enumerate(moves)
    ]


def backward_other_kernel(
    bits_ref, length_ref, lse_ref, qkv_hbm, ctxt_hbm, do_hbm, d0_hbm, w_hbm, ow_hbm, act0_hbm, act1_hbm, *rest
):
    pieces, out_pieces, rest = rest[:4], rest[4:6], rest[6:]
    both_ref, weight_ref, ow_ref, act_ref, qkv_ref, ctxt_ref, do_ref, *rest = rest
    scratch, (sems, late_sem, w_sems, ow_sems, act_sems) = rest[:14], rest[14:]
    width = do_ref.shape[1]
    sources = lambda pair: pair_sources(
        pair, width, (qkv_hbm, qkv_ref), (ctxt_hbm, ctxt_ref), (do_hbm, do_ref), sems
    )
    for pair in range(width // 128):
        start_all(sources(pair))
    own = pl.ds(pl.multiple_of(bits_ref[3] * 3 * width, 128), 3 * width)
    other = pl.ds(pl.multiple_of((1 - bits_ref[3]) * 3 * width, 128), 3 * width)
    late = [pltpu.make_async_copy(d0_hbm, both_ref.at[:, own], late_sem)]
    late += fetch_rows([w_hbm], 0, weight_ref.at[:, own], w_sems.at[0])
    late += fetch_rows(pieces, bits_ref[1], weight_ref.at[:, other], w_sems.at[1])
    units = ow_hbm.shape[0]
    rows = pl.ds(pl.multiple_of(bits_ref[3] * units, 128), units)
    late += fetch_rows([ow_hbm], 0, ow_ref.at[rows, :], ow_sems.at[0])
    late += [pltpu.make_async_copy(act0_hbm, act_ref.at[:, rows], act_sems.at[0])]
    rows = pl.ds(pl.multiple_of((1 - bits_ref[3]) * units, 128), units)
    late += fetch_rows(out_pieces, bits_ref[0], ow_ref.at[rows, :], ow_sems.at[1])
    late += [pltpu.make_async_copy(act1_hbm, act_ref.at[:, rows], act_sems.at[1])]
    start_all(late)
    d_ref = both_ref.at[:, other]
    backward_pairs(length_ref[0], qkv_ref, do_ref, ctxt_ref, lse_ref, d_ref, scratch, sources)
    wait_all(late)


def lane_sums(value):
    total = value[:, :128]
    for start in range(128, value.shape[1], 128):
        total = total + value[:, start : start + 128]
    return jnp.sum(total.T, 0, keepdims=True)


def backward_own_kernel(
    block,
    bits_ref,
    length_ref,
    lse_ref,
    vec_ref,
    ob_ref,
    sums_ref,
    db_ref,
    do_ref,
    qkv_hbm,
    ctxt_hbm,
    at_hbm,
    gat_hbm,
    w_hbm,
    lead_ref,
    vectors_ref,
    kept_ref,
    sent_ref,
    d_out,
    qkv_ref,
    ctxt_ref,
    *rest,
):
    scratch, rest = rest[:14], rest[14:]
    d_ref, at_ref, gat_ref, w_ref, dw_ref, total_ref, sems, w_sems, late_sems, out_sem = rest
    width = do_ref.shape[1]
    model = at_ref.shape[0]
    sources = lambda pair: pair_sources(
        pair, width, (qkv_hbm, qkv_ref), (ctxt_hbm, ctxt_ref), None, sems
    )
    for pair in range(width // 128):
        start_all(sources(pair))
    late = fetch_rows([w_hbm], 0, w_ref, w_sems)
    late += [
        pltpu.make_async_copy(at_hbm, at_ref, late_sems.at[0]),
        pltpu.make_async_copy(gat_hbm, gat_ref, late_sems.at[1]),
    ]
    start_all(late)
    backward_pairs(length_ref[0], qkv_ref, do_ref, ctxt_ref, lse_ref, d_ref, scratch, sources)
    saved = pltpu.make_async_copy(d_ref, d_out, out_sem)
    saved.start()
    lead_ref[...] = jnp.zeros(lead_ref.shape, F32)
    wait_all(late)
    low = ctxt_ref[...].astype(BF)
    dw_ref[:, 3 * width :] = dot(low, gat_ref[...]).T.astype(BF)
    total_ref[...] = jnp.zeros(total_ref.shape, F32)

    @pl.loop(0, d_ref.shape[0] // TILE)
    def _(index):
        total_ref[...] += jnp.sum(d_ref[tile_of(index), :].astype(F32), 0, keepdims=True)

    sums = total_ref[...]

    @pl.loop(0, model // TILE)
    def _(index):
        rows = tile_of(index)
        part = dot(at_ref[rows, :], d_ref[...])
        dw_ref[rows, : 3 * width] = part.astype(BF)
        weight = w_ref[rows, :].astype(F32)
        lead_ref[0:1, rows] = lane_sums(part * weight)
        lead_ref[1:2, rows] = lane_sums(weight * sums)

    halves(dw_ref, bits_ref[2], block, kept_ref, sent_ref)
    scaled, shift = lead_ref[0:1, :], lead_ref[1:2, :]
    gain1, shift1 = vec_ref[GAIN1 : GAIN1 + 1, :], vec_ref[SHIFT1 : SHIFT1 + 1, :]
    vectors_ref[...] = jnp.zeros(vectors_ref.shape, F32)
    lead_ref[0:1, :] = (scaled - shift1 * shift) / gain1
    vectors_ref[2:3, :] = ob_ref[...]
    vectors_ref[3:6, :] = sums_ref[...]
    for index in range(2):
        vectors_ref[6 + index : 7 + index, :] = db_ref[:, index * model : (index + 1) * model]
    vectors_ref[8:9, :width] = sums[:, :width]
    vectors_ref[8:9, width:] = sums[:, 2 * width :]
    saved.wait()


def backward_scratch(slots):
    return [
        pltpu.VMEM((2, slots, 128), BF),
        pltpu.VMEM((2, slots, 128), BF),
        pltpu.VMEM((2, slots, 128), BF),
        pltpu.VMEM((128, slots), BF),
        pltpu.VMEM((128, slots), BF),
        pltpu.VMEM((128, slots), BF),
        pltpu.VMEM((2, slots), F32),
        pltpu.VMEM((128, slots), F32),
        pltpu.VMEM((128, slots), F32),
        pltpu.VMEM((128, slots), F32),
        pltpu.VMEM((2, slots, TILE), F32),
        pltpu.VMEM((2, slots, TILE), F32),
        pltpu.VMEM((2, slots, TILE), BF),
        pltpu.VMEM((2, slots, TILE), BF),
    ]


def attention_backward_other(
    bits, length, lse, qkv, ctxt, do, d0, weight, ow, act0, act1, pieces, out_pieces
):
    slots, width = do.shape
    model = weight.shape[1]
    dma = pltpu.SemaphoreType.DMA
    ins = [(bits, SMEM), (length, SMEM), (lse, whole(lse.shape))]
    ins += [(value, HBM) for value in (qkv, ctxt, do, d0, weight, ow, act0, act1)]
    ins += [(value, HBM) for value in (*pieces, *out_pieces)]
    return call(
        backward_other_kernel,
        "attention_backward_other",
        1,
        ins,
        [
            ((slots, 6 * width), BF, KEPT),
            ((model, 6 * width), BF, KEPT),
            ((2 * ow.shape[0], model), BF, KEPT),
            ((slots, 2 * ow.shape[0]), BF, KEPT),
        ],
        [
            pltpu.VMEM((slots, 3 * width), BF),
            pltpu.VMEM((width, slots), F32),
            pltpu.VMEM((slots, width), BF),
            *backward_scratch(slots),
            dma((5, width // 128)),
            dma,
            dma((2, 12)),
            dma((2, 4)),
            dma((2,)),
        ],
        9 * slots * slots * width,
        12,
    )


def attention_backward_own(bits, length, block, lse, vec, sums, do, qkv, ctxt, at, gat, weight):
    slots, width = do.shape
    model = at.shape[0]
    dma = pltpu.SemaphoreType.DMA
    ins = [(bits, SMEM), (length, SMEM)]
    ins += [(value, whole(value.shape)) for value in (lse, vec, *sums)]
    ins += [(do, KEPT)] + [(value, HBM) for value in (qkv, ctxt, at, gat, weight)]
    outs = [((rows, model), F32, KEPT) for rows in (8, 16)] + [((model // 2, 4 * width), BF, KEPT)] * 2
    outs += [((slots, 3 * width), BF, HBM)]
    return call(
        functools.partial(backward_own_kernel, block),
        "attention_backward_own",
        1,
        ins,
        outs,
        [
            pltpu.VMEM((slots, 3 * width), BF),
            pltpu.VMEM((width, slots), F32),
            *backward_scratch(slots),
            pltpu.VMEM((slots, 3 * width), BF),
            pltpu.VMEM((model, slots), BF),
            pltpu.VMEM((slots, model), BF),
            pltpu.VMEM((model, 3 * width), BF),
            pltpu.VMEM((model, 4 * width), BF),
            pltpu.VMEM((1, 3 * width), F32),
            dma((4, width // 128)),
            dma((3,)),
            dma((2,)),
            dma,
        ],
        9 * slots * slots * width + 8 * slots * model * width,
        21,
    )


def final_kernel(vec_ref, d_ref, w_ref, x_hbm, gmid_hbm, gin_out, *rest):
    x_ref, gmid_ref, gin_ref, product_ref, x_sems, gmid_sems, gin_sems = rest
    x_in = tiles(x_hbm, x_ref, x_sems)
    gmid_in = tiles(gmid_hbm, gmid_ref, gmid_sems)
    gin_tiles = tiles(gin_ref, gin_out, gin_sems)
    start_all(x_in + gmid_in)
    count = len(x_in)

    def product(index):
        return dot_nt(d_ref[tile_of(index), :], w_ref[...])

    def norm(index):
        rows = tile_of(index)
        normed, inverse = norm_parts(x_ref[rows, :].astype(F32))
        back = norm_back(product_ref[...], normed, inverse, vec_ref[GAIN1 : GAIN1 + 1, :])
        gin_ref[rows, :] = gmid_ref[rows, :] + back

    product_ref[...] = product(0)
    wait_all(x_in + gmid_in)

    @pl.loop(0, count - 1)
    def _(index):
        norm(index)
        product_ref[...] = product(index + 1)
        tile_copy(gin_ref, gin_out, gin_sems, index).start()

    norm(count - 1)
    gin_tiles[-1].start()
    wait_all(gin_tiles)


def gradient_of_input(vec, both, weight, x, gmid):
    slots, model = x.shape
    tokens = slots // TILE
    dma = pltpu.SemaphoreType.DMA
    return call(
        final_kernel,
        "final",
        1,
        [(vec, whole(vec.shape)), (both, KEPT), (weight, KEPT), (x, HBM), (gmid, HBM)],
        [((slots, model), F32, HBM)],
        [
            pltpu.VMEM((slots, model), BF),
            pltpu.VMEM((slots, model), F32),
            pltpu.VMEM((slots, model), F32),
            pltpu.VMEM((TILE, model), F32),
            dma((tokens,)),
            dma((tokens,)),
            dma((tokens,)),
        ],
        2 * slots * model * both.shape[1],
        13,
    )[0]


def stage_kernel(blocks, bits_ref, fc_kept, out_kept, fc_got, out_got, *rest):
    kept_refs, sent_refs, (got_ref, total_ref, sems) = rest[:2], rest[2:4], rest[4:]
    copies = [
        pltpu.make_async_copy(got, got_ref.at[index], sems.at[index])
        for index, got in enumerate((fc_got, out_got))
    ]
    start_all(copies)
    for index, kept in enumerate((fc_kept, out_kept)):
        copies[index].wait()

        @pl.loop(0, kept.shape[0] // 48)
        def _(part):
            rows = pl.ds(pl.multiple_of(part * 48, 16), 48)
            total = kept[rows, :].astype(F32) + got_ref[index, rows, :].astype(F32)
            total_ref[index, rows, :] = total.astype(BF)

        halves(
            total_ref.at[index], bits_ref[4 + index], blocks[index], kept_refs[index], sent_refs[index]
        )


def second_stage(bits, blocks, kept, got):
    rows, columns = kept[0].shape
    shape = (rows // 2, columns)
    saved, sent = (shape, BF, whole(shape)), (shape, BF, KEPT)
    return call(
        functools.partial(stage_kernel, blocks),
        "second_stage",
        1,
        [(bits, SMEM)] + [(value, KEPT) for value in kept] + [(value, HBM) for value in got],
        [saved] * 2 + [sent] * 2,
        [
            pltpu.VMEM((2, rows, columns), BF),
            pltpu.VMEM((2, rows, columns), BF),
            pltpu.SemaphoreType.DMA((2,)),
        ],
        4 * rows * columns,
        12,
    )


def across(value):
    return lax.ppermute(value, "tensor", [(0, 1), (1, 0)])


def swap(value, bit):
    count = lax.axis_size("dp")
    return lax.ppermute(value, "dp", [(i, i ^ bit) for i in range(count)])


def tie(*values):
    return lax.optimization_barrier(values)


def pick(value, index, axis):
    return lax.dynamic_index_in_dim(value, index, axis, keepdims=False)


def split_rows(value, count):
    shape = value.shape
    return value.reshape(*shape[:-2], count, shape[-2] // count, shape[-1])


class Reduction:
    def __init__(self, kept, first_bit, order):
        self.order = order
        self.bits = [bit for bit in reversed(range(len(order) + 1)) if bit != first_bit]
        rows = kept.shape[0] >> len(self.bits)
        self.kept = kept.reshape(*[2] * len(self.bits), rows, kept.shape[1])

    def advance(self, got):
        got = got.reshape(self.kept.shape)
        self.bit = self.order.pop(0)
        axis = self.bits.index(self.bit)
        self.bits.remove(self.bit)
        side = (lax.axis_index("dp") >> self.bit) & 1

        def part(index):
            total = pick(self.kept, index, axis).astype(F32) + pick(got, index, axis).astype(F32)
            return total.astype(BF)

        sent = part(1 - side)
        self.kept = part(side)
        return sent.reshape(-1, sent.shape[-1])

    def block(self):
        lower = [bit for bit in self.bits if bit < self.order[0]]
        return self.kept.shape[-2] << len(lower)

    def advanced(self, kept):
        self.bit = self.order.pop(0)
        self.bits.remove(self.bit)
        self.kept = kept.reshape(*[2] * len(self.bits), *self.kept.shape[-2:])

    def finish(self, got):
        return self.kept.astype(F32) + got.reshape(self.kept.shape).astype(F32)


def local(
    block_input,
    first_gain,
    first_shift,
    qkv_weight,
    qv_bias,
    proj_weight,
    proj_bias,
    second_gain,
    second_shift,
    fc_weight,
    fc_bias,
    out_weight,
    out_bias,
    cotangent,
    lengths,
):
    slots, model = block_input.shape
    width = qkv_weight.shape[2]
    units = fc_weight.shape[1]
    shards = lax.axis_size("dp")
    levels = shards.bit_length() - 1
    share = model // shards
    first_bit = next(bit for bit in range(levels) if (share << bit) % 16 == 0)
    block = share << first_bit
    later = list(range(first_bit + 1, levels)) + list(range(first_bit))
    order_a = list(later)
    order_b = [later[1], later[0]] + later[2:]
    place = lax.axis_index("dp")
    quarter = jnp.bitwise_and(place, 3)
    one_bit = jnp.bitwise_and(place, 1)
    bits = jnp.stack(
        [
            one_bit,
            quarter,
            (place >> first_bit) & 1,
            lax.axis_index("tensor"),
            (place >> order_a[0]) & 1,
            (place >> order_b[0]) & 1,
        ]
    ).astype(jnp.int32)
    length = lengths.astype(jnp.int32)

    qkv_mine = across(pick(split_rows(qkv_weight, 4), quarter, 1))
    vectors = (first_gain, first_shift, proj_bias, second_gain, second_shift, out_bias)
    (
        vec,
        qkv0,
        grad_mlp,
        grad_mlp_turned,
        grad_out_bias,
        a_low,
        a_turned,
        proj_send,
        fc_send,
        out_send,
    ) = project(
        bits,
        length,
        block_input,
        cotangent,
        (*vectors, qv_bias, fc_bias),
        qkv_weight,
        proj_weight,
        fc_weight,
        out_weight,
    )

    fc_mine = across(fc_send)
    proj_got = across(proj_send)
    qkv_mine, qkv0 = tie(qkv_mine, qkv0)
    qkv_side = swap(qkv_mine, 2)
    qkv_core = swap(qkv_mine, 1)
    lse0, ctx0, ctxt0, qkv0 = attention_forward_own(length, qkv0)

    qkv_side, qkv_core, proj_got, ctx0, out_send = tie(
        qkv_side, qkv_core, proj_got, ctx0, out_send
    )
    half_rows = width // 2
    parts = proj_got[half_rows : half_rows + 24].astype(F32).reshape(3, 8, model)
    other_vec = (parts[0] + parts[1]) + parts[2]
    proj_other = [proj_got, swap(proj_got, 1)]
    qkv_other = [qkv_mine, qkv_core, qkv_side, swap(qkv_side, 1)]
    out_mine = across(out_send)
    lse1, c_low, c_turned, middle, ctxt1, qkv1 = attention_forward_other(
        bits,
        length,
        other_vec,
        vec,
        a_low,
        block_input,
        ctx0,
        proj_weight,
        qkv_other,
        proj_other,
    )

    c_low, fc_mine = tie(c_low, fc_mine)
    fc_side = swap(fc_mine, 2)
    fc_core = swap(fc_mine, 1)
    gc0, act0, fc_kept, out_kept, fc_sent, out_sent, grad_fc_bias, c_low, grad_mlp = feed_forward_own(
        bits, block, c_low, grad_mlp, c_turned, grad_mlp_turned, vec, fc_weight, out_weight
    )

    fc_sent, out_sent, fc_side, fc_core, out_mine = tie(
        fc_sent, out_sent, fc_side, fc_core, out_mine
    )
    fc_other = [fc_mine, fc_core, fc_side, swap(fc_side, 1)]
    out_other = [out_mine, swap(out_mine, 1)]
    fc_sent, out_sent, fc_other[3], out_other[1] = tie(
        fc_sent, out_sent, fc_other[3], out_other[1]
    )
    fc_got = swap(fc_sent, 1 << first_bit)
    out_got = swap(out_sent, 1 << first_bit)
    do0, fc_kept, out_kept, sums2, act1, grad_middle, grad_attn, do1 = feed_forward_other(
        bits,
        length,
        c_low,
        grad_mlp,
        other_vec,
        vec,
        gc0,
        middle,
        cotangent,
        proj_weight,
        (fc_kept, out_kept),
        fc_other,
        out_other,
        proj_other,
    )

    fc_sum = Reduction(fc_kept, first_bit, list(order_a))
    out_sum = Reduction(out_kept, first_bit, list(order_b))
    do0, fc_got, out_got = tie(do0, fc_got, out_got)
    fc_kept, out_kept, fc_sent, out_sent = second_stage(
        bits, (fc_sum.block(), out_sum.block()), (fc_kept, out_kept), (fc_got, out_got)
    )
    fc_sum.advanced(fc_kept)
    out_sum.advanced(out_kept)
    do0, fc_sent, out_sent = tie(do0, fc_sent, out_sent)
    fc_got = swap(fc_sent, 1 << fc_sum.bit)
    out_got = swap(out_sent, 1 << out_sum.bit)
    lead, vectors, kept, sent, d0 = attention_backward_own(
        bits,
        length,
        block,
        lse0,
        vec,
        (grad_out_bias, sums2, grad_fc_bias),
        do0,
        qkv0,
        ctxt0,
        a_turned,
        grad_attn,
        qkv_weight,
    )

    sent, lead, fc_got, out_got = tie(sent, lead, fc_got, out_got)
    attn_got = swap(sent, 1 << first_bit)
    lead_got = across(lead)
    fc_sent = fc_sum.advance(fc_got)
    out_sent = out_sum.advance(out_got)
    fc_got = swap(fc_sent, 1 << fc_sum.bit)
    out_got = swap(out_sent, 1 << out_sum.bit)

    def rounded(vectors):
        return lax.reduce_precision(vectors, 8, 7)

    def join(vectors, got):
        return rounded(vectors) + got.astype(F32)

    vectors = jnp.concatenate([(lead + lead_got)[:2], vectors[2:]], 0)
    lines = vectors.shape[0]
    vectors = join(vectors, swap(vectors.astype(BF), 1 << first_bit))
    first_sum = Reduction(kept[:, :model], first_bit, list(order_a))
    second_sum = Reduction(kept[:, model:], first_bit, list(order_b))
    first_sent = jnp.concatenate(
        [first_sum.advance(attn_got[:, :model]), vectors.astype(BF)], 0
    )
    second_sent = second_sum.advance(attn_got[:, model:])
    first_sent, second_sent, qkv1 = tie(first_sent, second_sent, qkv1)
    first_got = swap(first_sent, 1 << first_sum.bit)
    second_got = swap(second_sent, 1 << second_sum.bit)
    both, weights, ow, act = attention_backward_other(
        bits,
        length,
        lse1,
        qkv1,
        ctxt1,
        do1,
        d0,
        qkv_weight,
        out_weight,
        act0,
        act1,
        qkv_other,
        out_other,
    )

    both, fc_got, out_got, first_got, second_got = tie(both, fc_got, out_got, first_got, second_got)
    vectors = join(vectors, first_got[-lines:])
    first_sent = jnp.concatenate(
        [first_sum.advance(first_got[:-lines]), vectors.astype(BF)], 0
    )
    second_sent = second_sum.advance(second_got)
    rest_sent = jnp.concatenate([fc_sum.advance(fc_got), out_sum.advance(out_got)], 0)
    both, first_sent, second_sent, rest_sent = tie(both, first_sent, second_sent, rest_sent)
    first_got = swap(first_sent, 1 << first_sum.bit)
    second_got = swap(second_sent, 1 << second_sum.bit)
    rest_got = swap(rest_sent, 1 << fc_sum.bit)
    grad_input = gradient_of_input(vec, both, weights, block_input, grad_middle)

    grad_input, first_got, second_got, act = tie(grad_input, first_got, second_got, act)
    for level in range(3, levels):
        vectors = join(vectors, first_got[-lines:])
        sent = [first_sum.advance(first_got[:-lines]), second_sum.advance(second_got)]
        rows = sent[0].shape[0]
        sent = jnp.concatenate([*sent, vectors.astype(BF)], 0)
        sent, act = tie(sent, act)
        got = swap(sent, 1 << first_sum.bit)
        first_got = jnp.concatenate([got[:rows], got[2 * rows :]], 0)
        second_got = got[rows : 2 * rows]
        if fc_sum.order:
            rows = rest_got.shape[0] // 2
            rest_sent = [fc_sum.advance(rest_got[:rows]), out_sum.advance(rest_got[rows:])]
            rest_got = swap(jnp.concatenate(rest_sent, 0), 1 << fc_sum.bit)
    block_output = block_result(vec, act, ow, middle)
    vectors = join(vectors, first_got[-lines:])
    first = first_sum.finish(first_got[:-lines])
    second = second_sum.finish(second_got)
    rows = rest_got.shape[0] // 2
    grad_fc_weight = fc_sum.finish(rest_got[:rows])
    grad_out_weight = out_sum.finish(rest_got[rows:]).T
    grad_qkv_weight = jnp.stack([first[:, :width], first[:, width:], second[:, :width]])
    grad_proj_weight = second[:, width:].T
    return (
        block_output,
        grad_input,
        vectors[0],
        vectors[1],
        grad_qkv_weight,
        vectors[8].reshape(2, width),
        grad_proj_weight,
        vectors[5],
        vectors[3],
        vectors[4],
        grad_fc_weight,
        vectors[6:8].reshape(units),
        grad_out_weight,
        vectors[2],
    )


def solution(mesh):
    placed = (
        P("dp", None),
        P(),
        P(),
        P(None, None, "tensor"),
        P(None, "tensor"),
        P("tensor", None),
        P(),
        P(),
        P(),
        P(None, "tensor"),
        P("tensor"),
        P("tensor", None),
        P(),
        P("dp", None),
        P("dp"),
    )
    return jax.shard_map(
        local,
        mesh=mesh,
        in_specs=placed,
        out_specs=(
            P("dp", None),
            P("dp", None),
            P(),
            P(),
            P(None, "dp", "tensor"),
            P(None, "tensor"),
            P("tensor", "dp"),
            P(),
            P(),
            P(),
            P("dp", "tensor"),
            P("tensor"),
            P("tensor", "dp"),
            P(),
        ),
        check_vma=False,
    )
```
